32 devices in a mesh: seq: 4 (over x, core), shard: 8 (over z, y).
Axes of the slice: x: 2, y: 2, z: 4, core: 2. Of those that a mesh axis runs over, the one named last changes fastest.
Arguments:
- tokens: bfloat16 [16, 1024, 768], P('shard', 'seq'), may hold values from -6 to 6
- teacher: bfloat16 [16, 1024, 768], P('shard', 'seq'), may hold values from -9 to 9
- cotangent: bfloat16 [16, 1024, 768], P('shard', 'seq'), may hold values from -6 to 6
- lengths: int32 [16], P('shard'), may hold values from 256 to 1024, as said below
- w_qkv: bfloat16 [768, 2304], P('shard'), may hold values from -0.21875 to 0.21875
- w_out: bfloat16 [768, 768], P('shard'), may hold values from -0.875 to 0.875
- w_up: bfloat16 [768, 3072], P('shard'), may hold values from -0.21875 to 0.21875
- w_down: bfloat16 [3072, 768], P('shard'), may hold values from -0.109375 to 0.109375
- norm_gain: bfloat16 [2, 768], P(None, 'shard'), may hold values from 0.5 to 1.5
- norm_bias: bfloat16 [2, 768], P(None, 'shard'), may hold values from -1.1953125 to 1.1953125
- proj_bias: bfloat16 [4, 768], P(None, 'shard'), may hold values from -1.1953125 to 1.1953125
- up_bias: bfloat16 [3072], P('shard'), may hold values from -1.1953125 to 1.1953125
Outputs:
- output: bfloat16 [16, 1024, 768], P('shard', 'seq')
- distill_loss: float32 [], replicated
- g_tokens: float32 [16, 1024, 768], P('shard', 'seq')
- g_w_qkv: float32 [768, 2304], P('shard')
- g_w_out: float32 [768, 768], P('shard')
- g_w_up: float32 [768, 3072], P('shard')
- g_w_down: float32 [3072, 768], P('shard')
- g_norm_gain: float32 [2, 768], P(None, 'shard')
- g_norm_bias: float32 [2, 768], P(None, 'shard')
- g_proj_bias: float32 [4, 768], P(None, 'shard')
- g_up_bias: float32 [3072], P('shard')
The draws below stay inside these ranges and needn't reach their ends.
Inputs may be any that keep to these rules, and one draw needn't show every extreme that they name: The valid tokens of sequence s are its first lengths[s] slots; in every draw one sequence is full and one has 256 valid tokens.
All inputs are finite; a program needn't handle non-finite values.
Results may differ from the reference program's by a relative error of at most 0.013.
Values may be sent and summed in bfloat16 or wider, within the bound.
No kernel may reach another device: no remote copies, remote signals or barrier semaphores. Data moves between devices by JAX's collectives and lax.ppermute only.
A program may use at most 192 MiB of HBM per device.

```python
import jax
import jax.numpy as jnp
from jax import lax

D = 768
HEADS = 12
HD = 64
FF = 3072
LEN = 1024
MIN_LEN = 256
SEQUENCES = 16


def draw_lengths(key, part):
    key_jitter, key_full, key_short = jax.random.split(key, 3)
    seq_index = jnp.arange(SEQUENCES, dtype=jnp.int32)
    spread = LEN - MIN_LEN
    rising = spread * seq_index // (SEQUENCES - 1)
    jitter = jax.random.randint(key_jitter, (SEQUENCES,), 0, spread + 1)
    values = MIN_LEN + (jitter + rising) // 2
    full_at = jax.random.randint(key_full, (), 0, SEQUENCES)
    short_at = (full_at + 1 + jax.random.randint(key_short, (), 0, SEQUENCES - 1)) % SEQUENCES
    values = values.at[full_at].set(LEN)
    values = values.at[short_at].set(MIN_LEN)
    return values.astype(jnp.int32)


def steps_of(key, extent, cuts, least, largest):
    level = 1.0
    for position, blocks in cuts:
        draws = jax.random.uniform(jax.random.fold_in(jax.random.fold_in(key, 6), position), (blocks,), jnp.float32, least / len(cuts), largest / len(cuts))
        level = level * jnp.repeat(jnp.exp(draws), extent[position] // blocks).reshape((-1,) + (1,) * (len(extent) - 1 - position))
    return level


def normal_values(key, shape, width, reach, pieces=(), kind=jnp.bfloat16):
    array = width * jax.random.normal(key, shape, jnp.float32)
    if pieces:
        array = array * steps_of(key, shape, pieces, -0.22, 0.18)
    return jnp.clip(array, -reach, reach).astype(kind)


def setup_inputs(seed: int = 0) -> dict:
    key_of = jax.random.split(jax.random.key(seed), 13)
    tokens = normal_values(key_of[0], (SEQUENCES, LEN, D), 1.0, 6.0, ((0, 8), (1, 4)))
    teacher = normal_values(key_of[1], (SEQUENCES, LEN, D), 1.5, 9.0, ((0, 8), (1, 4)))
    cotangent = normal_values(key_of[2], (SEQUENCES, LEN, D), 1.0, 6.0, ((0, 8), (1, 4)))
    lengths = draw_lengths(jax.random.fold_in(key_of[12], 71), 0)
    w_qkv = normal_values(key_of[4], (D, 3 * D), D ** -0.5, 0.21875, ((0, 8),))
    w_out = normal_values(key_of[5], (D, D), (D // 16) ** -0.5, 0.875, ((0, 8),))
    w_up = normal_values(key_of[6], (D, FF), D ** -0.5, 0.21875, ((0, 8),))
    w_down = normal_values(key_of[7], (FF, D), FF ** -0.5, 0.109375, ((0, 8),))
    norm_gain = jnp.clip(1.0 + 0.1 * jax.random.normal(key_of[8], (2, D), jnp.float32), 0.5, 1.5).astype(jnp.bfloat16)
    norm_bias = normal_values(key_of[9], (2, D), 0.2, 1.1953125, ((1, 8),))
    proj_bias = normal_values(key_of[10], (4, D), 0.2, 1.1953125, ((1, 8),))
    up_bias = normal_values(key_of[11], (FF,), 0.2, 1.1953125, ((0, 8),))
    return dict(tokens=tokens, teacher=teacher, cotangent=cotangent, lengths=lengths, w_qkv=w_qkv, w_out=w_out, w_up=w_up, w_down=w_down, norm_gain=norm_gain, norm_bias=norm_bias, proj_bias=proj_bias, up_bias=up_bias)


EPSILON = 1e-06
NEG_FILL = -1e+30
HIGH = lax.Precision.HIGHEST

@jax.custom_vjp
def low(v):
    return lax.optimization_barrier(v.astype(jnp.bfloat16)).astype(jnp.float32)

@jax.custom_vjp
def low_back(v):
    return v

def low_keep(v):
    return (low(v), None)

def low_pass(kept, grad):
    return (grad,)

def back_keep(v):
    return (v, None)

def back_low(kept, grad):
    return (low(grad),)
low.defvjp(low_keep, low_pass)
low_back.defvjp(back_keep, back_low)

def norm_apply(rows_in, gain_row, shift_row):
    centre = lax.optimization_barrier(jnp.mean(rows_in, axis=-1, keepdims=True))
    centred = rows_in - centre
    second = lax.optimization_barrier(jnp.mean(centred * centred, axis=-1, keepdims=True))
    return centred * lax.rsqrt(second + EPSILON) * gain_row + shift_row

def block(inputs, targets, cotan, valid_len, params):
    w_qkv, w_out, w_up, w_down, norm_gain, norm_bias, proj_bias, up_bias = params
    group = inputs.shape[0]
    live = jnp.arange(LEN, dtype=jnp.int32)[None, :] < valid_len[:, None]
    row_mask = live[:, :, None].astype(inputs.dtype)
    normed_in = low(norm_apply(inputs, norm_gain[0], norm_bias[0]))
    qkv_bias = jnp.concatenate([proj_bias[0], jnp.zeros_like(proj_bias[0]), proj_bias[1]])
    joined = jnp.einsum('gld,de->gle', normed_in, w_qkv, precision=HIGH) + qkv_bias
    joined = low_back(low(joined)).reshape(group, LEN, 3, HEADS, HD)
    queries = joined[:, :, 0]
    keys_in = joined[:, :, 1]
    values_in = joined[:, :, 2]
    scores = jnp.einsum('gqhd,gkhd->ghqk', queries, keys_in, precision=HIGH) * HD ** (-0.5)
    scores = low_back(jnp.where(live[:, None, None, :], scores, NEG_FILL))
    attn_f = jax.nn.softmax(scores, axis=-1)
    mixed = jnp.einsum('ghqk,gkhd->gqhd', low(attn_f), values_in, precision=HIGH).reshape(group, LEN, D)
    mixed = low_back(low(mixed))
    branch = low_back(jnp.einsum('gld,de->gle', mixed, w_out, precision=HIGH) + proj_bias[2])
    resid_mid = inputs + branch
    normed_mid = low(norm_apply(resid_mid, norm_gain[1], norm_bias[1]))
    preact = low_back(jnp.einsum('gld,df->glf', normed_mid, w_up, precision=HIGH) + up_bias)
    activ = low(jax.nn.gelu(preact, approximate=False))
    ffn_out = low_back(jnp.einsum('glf,fd->gld', activ, w_down, precision=HIGH) + proj_bias[3])
    result = resid_mid + ffn_out
    error = result - targets
    return (result, jnp.sum(row_mask * cotan * result), jnp.sum(row_mask * error * error))

def reference(tokens, teacher, cotangent, lengths, w_qkv, w_out, w_up, w_down, norm_gain, norm_bias, proj_bias, up_bias):
    count = jnp.sum(lengths).astype(jnp.float32)
    group = 2 if SEQUENCES % 2 == 0 else 1
    rounds = SEQUENCES // group
    inputs = tokens.astype(jnp.float32).reshape(rounds, group, LEN, D)
    targets = teacher.astype(jnp.float32).reshape(rounds, group, LEN, D)
    cotans = cotangent.astype(jnp.float32).reshape(rounds, group, LEN, D)
    valid = lengths.reshape(rounds, group)
    params = tuple((item.astype(jnp.float32) for item in (w_qkv, w_out, w_up, w_down, norm_gain, norm_bias, proj_bias, up_bias)))

    def objective(inputs_all, params_all):

        def one_round(carry, item):
            part_in, part_target, part_cotan, part_len = item
            result, dot_term, square_term = block(part_in, part_target, part_cotan, part_len, params_all)
            return ((carry[0] + dot_term, carry[1] + square_term), result)
        zero = jnp.zeros((), inputs_all.dtype)
        (dot_total, sse_total), results = lax.scan(jax.checkpoint(one_round), (zero, zero), (inputs_all, targets, cotans, valid))
        sse_scaled = sse_total / (count * D)
        return (dot_total + sse_scaled, (results, sse_scaled))
    total, pullback, extras = jax.vjp(objective, inputs, params, has_aux=True)
    g_inputs, g_params = pullback(jnp.ones_like(total))
    results, distill_loss = extras
    output = results.reshape(SEQUENCES, LEN, D).astype(jnp.bfloat16)
    g_tokens = g_inputs.reshape(SEQUENCES, LEN, D)
    return (output, distill_loss, g_tokens, g_params[0], g_params[1], g_params[2], g_params[3], g_params[4], g_params[5], g_params[6], g_params[7])
```

```python
import functools

import jax
import jax.numpy as jnp
from jax import lax
from jax.experimental import pallas as pl
from jax.experimental.pallas import tpu as pltpu
from jax.sharding import Mesh
from jax.sharding import PartitionSpec as P

HD = 64
EPSILON = 1e-06
NEG_FILL = -1e30
LOG2E = 1.4426950408889634
ALL = ("x", "core", "z", "y")
BF = jnp.bfloat16
F32 = jnp.float32
CHUNK = 256


def dot_f32(a, b, dims):
    return lax.dot_general(a, b, (dims, ((), ())), preferred_element_type=F32)


def attn_fwd_kernel(q_ref, k0_ref, v0_ref, k1_ref, v1_ref, bias_ref, out_ref, lse_ref):
    rows = q_ref.shape[0]
    keys = jnp.concatenate([k0_ref[...], k1_ref[...]], axis=0)
    values_t = jnp.concatenate([v0_ref[...], v1_ref[...]], axis=0).T
    lane = lax.broadcasted_iota(jnp.int32, (CHUNK, 2 * HD), 1)
    bias = jnp.concatenate([bias_ref[...]] * (CHUNK // 128), axis=1)
    lse_ref[...] = jnp.zeros_like(lse_ref)
    for start in range(0, rows, CHUNK):
        q_both = q_ref[start : start + CHUNK, :]
        parts = []
        for head in range(2):
            keep = (lane < HD) if head == 0 else (lane >= HD)
            q_one = jnp.where(keep, q_both, jnp.zeros_like(q_both))
            logits = dot_f32(keys, q_one, ((1,), (1,))) * (HD**-0.5 * LOG2E) + bias
            top = jnp.max(logits, axis=0, keepdims=True)
            expo = jnp.exp2(logits - top)
            total = jnp.sum(expo, axis=0, keepdims=True)
            mixed_t = dot_f32(
                values_t[head * HD : (head + 1) * HD], expo.astype(BF), ((1,), (0,))
            )
            parts.append(mixed_t / total)
            lse_ref[0, head : head + 1, start : start + CHUNK] = top + jnp.log2(total)
        out_ref[start : start + CHUNK, :] = jnp.concatenate(parts, axis=0).T.astype(BF)


def attn_bwd_kernel(
    q_ref, k0_ref, v0_ref, k1_ref, v1_ref, bias_ref, lse_ref, mix_ref, dmix_ref,
    dq_ref, dkv0_ref, dkv1_ref, dk_acc, dv_acc,
):
    rows = q_ref.shape[0]
    factor = HD**-0.5
    keys = jnp.concatenate([k0_ref[...], k1_ref[...]], axis=0)
    values = jnp.concatenate([v0_ref[...], v1_ref[...]], axis=0)
    keys_t = keys.T
    lane = lax.broadcasted_iota(jnp.int32, (CHUNK, 2 * HD), 1)
    bias = jnp.concatenate([bias_ref[...]] * (CHUNK // 128), axis=1)
    for start in range(0, rows, CHUNK):
        q_both = q_ref[start : start + CHUNK, :]
        d_both = dmix_ref[start : start + CHUNK, :]
        prod_t = (
            d_both.astype(F32) * mix_ref[start : start + CHUNK, :].astype(F32)
        ).T
        parts = []
        for head in range(2):
            keep = (lane < HD) if head == 0 else (lane >= HD)
            q_one = jnp.where(keep, q_both, jnp.zeros_like(q_both))
            d_one = jnp.where(keep, d_both, jnp.zeros_like(d_both))
            delta = jnp.sum(prod_t[head * HD : (head + 1) * HD], axis=0, keepdims=True)
            logits = dot_f32(keys, q_one, ((1,), (1,))) * (factor * LOG2E) + bias
            probs = jnp.exp2(logits - lse_ref[0, head : head + 1, start : start + CHUNK])
            d_probs = dot_f32(values, d_one, ((1,), (1,)))
            d_scores = (probs * (d_probs - delta)).astype(BF)
            dv_new = dot_f32(probs.astype(BF), d_one, ((1,), (0,)))
            dk_new = dot_f32(d_scores, q_one, ((1,), (0,)))
            if start == 0 and head == 0:
                dv_acc[...] = dv_new
                dk_acc[...] = dk_new
            else:
                dv_acc[...] += dv_new
                dk_acc[...] += dk_new
            parts.append(
                dot_f32(keys_t[head * HD : (head + 1) * HD], d_scores, ((1,), (0,)))
            )
        dq_ref[start : start + CHUNK, :] = (
            (jnp.concatenate(parts, axis=0) * factor).T.astype(BF)
        )
    dkv0_ref[0] = (dk_acc[:rows] * factor).astype(BF)
    dkv1_ref[0] = (dk_acc[rows:] * factor).astype(BF)
    dkv0_ref[1] = dv_acc[:rows].astype(BF)
    dkv1_ref[1] = dv_acc[rows:].astype(BF)


def attention_forward(qkv, kv_other, bias_cols):
    rows, width = qkv.shape[0], qkv.shape[1] // 3
    pairs = width // (2 * HD)
    col = lambda base: pl.BlockSpec((rows, 2 * HD), lambda i, base=base: (0, base + i))
    return pl.pallas_call(
        attn_fwd_kernel,
        grid=(pairs,),
        in_specs=[
            col(0), col(pairs), col(2 * pairs), col(0), col(pairs),
            pl.BlockSpec(bias_cols.shape, lambda i: (0, 0)),
        ],
        out_specs=[col(0), pl.BlockSpec((1, 8, rows), lambda i: (i, 0, 0))],
        out_shape=[
            jax.ShapeDtypeStruct((rows, width), BF),
            jax.ShapeDtypeStruct((pairs, 8, rows), F32),
        ],
        cost_estimate=pl.CostEstimate(
            flops=rows * rows * width * 8, bytes_accessed=rows * width * 12,
            transcendentals=rows * rows * 2 * pairs * 2,
        ),
        name="attn_fwd",
    )(qkv, qkv, qkv, kv_other, kv_other, bias_cols)


def attention_backward(qkv, kv_other, bias_cols, lse, mixed, d_mixed):
    rows, width = qkv.shape[0], qkv.shape[1] // 3
    pairs = width // (2 * HD)
    col = lambda base: pl.BlockSpec((rows, 2 * HD), lambda i, base=base: (0, base + i))
    both = pl.BlockSpec((2, rows, 2 * HD), lambda i: (0, 0, i))
    return pl.pallas_call(
        attn_bwd_kernel,
        grid=(pairs,),
        in_specs=[
            col(0), col(pairs), col(2 * pairs), col(0), col(pairs),
            pl.BlockSpec(bias_cols.shape, lambda i: (0, 0)),
            pl.BlockSpec((1, 8, rows), lambda i: (i, 0, 0)), col(0), col(0),
        ],
        out_specs=[col(0), both, both],
        out_shape=[
            jax.ShapeDtypeStruct((rows, width), BF),
            jax.ShapeDtypeStruct((2, rows, width), BF),
            jax.ShapeDtypeStruct((2, rows, width), BF),
        ],
        scratch_shapes=[
            pltpu.VMEM((2 * rows, 2 * HD), F32), pltpu.VMEM((2 * rows, 2 * HD), F32)
        ],
        cost_estimate=pl.CostEstimate(
            flops=rows * rows * width * 20, bytes_accessed=rows * width * 30,
            transcendentals=rows * rows * 2 * pairs * 2,
        ),
        name="attn_bwd",
    )(qkv, qkv, qkv, kv_other, kv_other, bias_cols, lse, mixed, d_mixed)


def swap(value, axis):
    return lax.ppermute(value, axis, [(0, 1), (1, 0)])


def stage_swap(value, first):
    sizes = [lax.axis_size(a) for a in ALL]
    pairs = []
    for x in range(sizes[0]):
        for core in range(sizes[1]):
            for z in range(sizes[2]):
                for y in range(sizes[3]):
                    over_y = (core == 0) == first
                    tx, ty = (x, 1 - y) if over_y else (1 - x, y)
                    flat = lambda a, b: ((a * sizes[1] + core) * sizes[2] + z) * sizes[3] + b
                    pairs.append((flat(x, y), flat(tx, ty)))
    return lax.ppermute(value, ALL, pairs)


def gather_pieces(piece):
    depth = lax.axis_size("z")
    spread = jnp.broadcast_to(piece[None], (depth,) + piece.shape)
    own = lax.all_to_all(spread, "z", 0, 0, tiled=True)
    near = jnp.stack([own, stage_swap(own, True)])
    far = stage_swap(near, False)
    return near, far, swap(near, "core"), swap(far, "core")


def place_kernel(rows, splits, slot_ref, *refs):
    sources, outs, sem = refs[:4], refs[4:-1], refs[-1]
    copies = []
    for who in range(2):
        for outer in range(2):
            for inner in range(2):
                slot = slot_ref[who * 4 + outer * 2 + inner]
                offset = 0
                for out, cols in zip(outs, splits, strict=True):
                    column = pl.multiple_of(slot_ref[8 + who] * cols, 128)
                    copies.append(
                        pltpu.make_async_copy(
                            sources[who * 2 + outer].at[
                                inner, :, pl.ds(0, rows), pl.ds(offset, cols)
                            ],
                            out.at[:, slot, :, pl.ds(column, cols)],
                            sem.at[len(copies)],
                        )
                    )
                    offset += cols
    for copy in copies:
        copy.start()
    for copy in copies:
        copy.wait()


def place_pieces(pieces, slots, rows, splits):
    depth = pieces[0].shape[1]
    outs = pl.pallas_call(
        functools.partial(place_kernel, rows, splits),
        grid_spec=pltpu.PrefetchScalarGridSpec(
            num_scalar_prefetch=1,
            grid=(1,),
            in_specs=[pl.BlockSpec(memory_space=pl.ANY)] * 4,
            out_specs=[
                pl.BlockSpec((depth, 4, rows, 2 * cols), lambda i, s: (0, 0, 0, 0))
                for cols in splits
            ],
            scratch_shapes=[pltpu.SemaphoreType.DMA((8 * len(splits),))],
        ),
        out_shape=[
            jax.ShapeDtypeStruct((depth, 4, rows, 2 * cols), BF) for cols in splits
        ],
        name="place",
    )(slots, *pieces)
    return [out.reshape(depth * 4 * rows, -1) for out in outs]


def halves(value, bit, axis):
    take = lambda b: lax.dynamic_index_in_dim(value, b, axis, keepdims=False)
    return take(bit), take(1 - bit)


def reduce_pieces(blocks, order):
    for axis in order:
        dim = 2 if axis == "x" else 1
        if axis == "y" and order[0] == "y":
            dim = 1
        elif axis == "x" and order[0] == "y":
            dim = 1
        keep, send = halves(blocks, lax.axis_index(axis), dim)
        blocks = keep.astype(F32) + swap(send.astype(BF), axis).astype(F32)
    parts = lax.all_to_all(blocks.astype(BF), "z", 0, 0, tiled=True)
    return jnp.sum(parts.astype(F32), axis=0)


def ordered(mine, other, bit, axis):
    return jnp.where(
        bit == 0,
        jnp.concatenate([mine, other], axis),
        jnp.concatenate([other, mine], axis),
    )


def norm_stats(rows_in):
    centre = jnp.mean(rows_in, axis=-1, keepdims=True)
    centred = rows_in - centre
    second = jnp.mean(centred * centred, axis=-1, keepdims=True)
    return centre, lax.rsqrt(second + EPSILON)


def norm_back(grad, xhat, rstd, gain):
    scaled = grad * gain
    mean_a = jnp.mean(scaled, axis=-1, keepdims=True)
    mean_b = jnp.mean(scaled * xhat, axis=-1, keepdims=True)
    return (
        rstd * (scaled - mean_a - xhat * mean_b),
        jnp.sum(grad * xhat, axis=0),
        jnp.sum(grad, axis=0),
    )


def shards(
    tokens, teacher, cotangent, lengths, w_qkv, w_out, w_up, w_down,
    norm_gain, norm_bias, proj_bias, up_bias,
):
    groups, local_len, width = tokens.shape
    chip = lax.axis_index("x")
    core = lax.axis_index("core")
    row_y = lax.axis_index("y")
    depth = lax.axis_size("z")
    owners = depth * 2
    ff = w_down.shape[0] * owners
    fast = (width // owners) % 32 == 0
    heads_pair = width // (2 * HD)

    def regroup(blocks):
        mine, send = halves(blocks, chip, 0)
        return jnp.concatenate([mine, swap(send, "x")], axis=0)

    def half_cols(value, which, axis=-1):
        size = value.shape[axis] // 2
        return lax.dynamic_slice_in_dim(value, which * size, size, axis)

    small = jnp.concatenate(
        [norm_gain.reshape(-1), norm_bias.reshape(-1), proj_bias.reshape(-1), up_bias]
    )
    len_parts = jnp.concatenate([lengths // 32, lengths % 32]).astype(BF)
    tok_bf = regroup(tokens)
    if fast:
        quarter = lambda w: half_cols(half_cols(w, chip, 0), core, 1)
        first_w = quarter(w_qkv)
        cols = first_w.shape[1]
        extra = jnp.zeros((8, cols), BF)
        extra = extra.at[0, : small.size].set(small)
        extra = extra.at[1, : len_parts.size].set(len_parts)
        pieces_a = gather_pieces(jnp.concatenate([first_w, extra], axis=0))
        pieces_b = gather_pieces(jnp.concatenate([quarter(w_out), quarter(w_up)], axis=1))
        pieces_c = gather_pieces(quarter(w_down))
        slots = []
        for who in range(2):
            zero = (core if who == 0 else 1 - core) == 0
            for outer in range(2):
                for inner in range(2):
                    slots.append(
                        jnp.where(
                            zero,
                            (row_y ^ inner) * 2 + (chip ^ outer),
                            (row_y ^ outer) * 2 + (chip ^ inner),
                        )
                    )
        slots = jnp.stack(slots + [core, 1 - core]).astype(jnp.int32)
        rows_a = first_w.shape[0]
        (wq_all,) = place_pieces(pieces_a, slots, rows_a, (cols,))
        wo_all, wup_all = place_pieces(
            pieces_b, slots, rows_a, (w_out.shape[1] // 2, w_up.shape[1] // 2)
        )
        (wdn_all,) = place_pieces(
            pieces_c, slots, w_down.shape[0] // 2, (w_down.shape[1] // 2,)
        )
        near, far = pieces_a[0], pieces_a[1]
        tail = lambda v: v[:, rows_a : rows_a + 2]
        other_y = jnp.where(core == 0, tail(near[1]), tail(far[0]))
        both = ordered(tail(near[0])[:, None], other_y[:, None], row_y, 1)
        both = both.reshape(owners, 2, cols)
        small_all = both[:, 0, : small.size]
        lens_all = both[:, 1, : len_parts.size]
    else:
        full = lambda w: lax.all_gather(w, ("z", "y"), axis=0, tiled=True)
        wq_all, wo_all, wup_all, wdn_all = map(full, (w_qkv, w_out, w_up, w_down))
        small_all = lax.all_gather(small, ("z", "y"), axis=0)
        lens_all = lax.all_gather(len_parts, ("z", "y"), axis=0)
    small_all = small_all.astype(F32)
    span = width // owners

    def vectors(start, count):
        part = small_all[:, start * span : (start + count) * span]
        return part.reshape(owners, count, span).transpose(1, 0, 2).reshape(count, width)

    gains, shifts, biases = vectors(0, 2), vectors(2, 2), vectors(4, 4)
    up_shift = small_all[:, 8 * span :].reshape(ff)
    lens_f = lens_all.astype(F32)
    count = jnp.sum(lens_f[:, :groups] * 32.0 + lens_f[:, groups:])

    length = lax.dynamic_index_in_dim(lengths, chip, 0, keepdims=False)
    steps = jnp.arange(local_len, dtype=jnp.int32)
    block_at = lambda x_at, c_at: (x_at * 2 + c_at) * local_len + steps
    mine_at = jnp.concatenate([block_at(chip, core), block_at(1 - chip, core)])
    other_at = jnp.concatenate([block_at(chip, 1 - core), block_at(1 - chip, 1 - core)])
    live = (mine_at < length).astype(F32)[:, None]
    key_at = jnp.concatenate([mine_at, other_at])
    bias_cols = jnp.broadcast_to(
        jnp.where(key_at < length, 0.0, NEG_FILL)[:, None], (key_at.shape[0], 128)
    ).astype(F32)

    inputs = tok_bf.astype(F32)
    centre_in, rstd_in = norm_stats(inputs)
    xhat_in = (inputs - centre_in) * rstd_in
    normed_in = (xhat_in * gains[0] + shifts[0]).astype(BF)
    qkv_bias = jnp.concatenate([biases[0], jnp.zeros((width,), F32), biases[1]])
    qkv = (dot_f32(normed_in, wq_all, ((1,), (0,))) + qkv_bias).astype(BF)
    kv_other = swap(qkv[:, width:], "core")
    mixed, lse = attention_forward(qkv, kv_other, bias_cols)
    resid_mid = inputs + dot_f32(mixed, wo_all, ((1,), (0,))) + biases[2]
    centre_mid, rstd_mid = norm_stats(resid_mid)
    xhat_mid = (resid_mid - centre_mid) * rstd_mid
    normed_mid = (xhat_mid * gains[1] + shifts[1]).astype(BF)
    preact = dot_f32(normed_mid, wup_all, ((1,), (0,))) + up_shift
    bell = 0.5 * (1.0 + lax.erf(preact * 0.7071067811865476))
    activ = (preact * bell).astype(BF)
    slope = (
        bell + preact * jnp.exp(-0.5 * preact * preact) * 0.3989422804014327
    ).astype(BF)
    result = resid_mid + dot_f32(activ, wdn_all, ((1,), (0,))) + biases[3]
    error = result - regroup(teacher).astype(F32)
    sse = jnp.sum(live * error * error)

    d_result = live * (regroup(cotangent).astype(F32) + 2.0 / (count * width) * error)
    d_branch = d_result.astype(BF)

    def both_rows(value):
        return jnp.concatenate([value, swap(value, "core")], axis=0)

    def both_halves(value):
        return jnp.concatenate(
            [half_cols(value, core), swap(half_cols(value, 1 - core), "core")], axis=0
        )

    def weight_grad(left, right):
        grad = dot_f32(both_rows(left), both_halves(right), ((0,), (0,)))
        return grad.reshape(depth, 2, 2, -1, grad.shape[1])

    g_wdn = weight_grad(activ, d_branch)
    d_activ = dot_f32(d_branch, wdn_all, ((1,), (1,)))
    d_pre_f = d_activ * slope.astype(F32)
    d_preact = d_pre_f.astype(BF)
    g_wup = weight_grad(normed_mid, d_preact)
    d_normed_mid = dot_f32(d_preact, wup_all, ((1,), (1,)))
    d_mid_part, d_gain_mid, d_shift_mid = norm_back(
        d_normed_mid, xhat_mid, rstd_mid, gains[1]
    )
    d_resid_mid = d_result + d_mid_part
    d_attn = d_resid_mid.astype(BF)
    g_wo = weight_grad(mixed, d_attn)
    d_mixed = dot_f32(d_attn, wo_all, ((1,), (1,))).astype(BF)
    dq, dkv_mine, dkv_other = attention_backward(
        qkv, kv_other, bias_cols, lse, mixed, d_mixed
    )
    dkv = (dkv_mine.astype(F32) + swap(dkv_other, "core").astype(F32)).astype(BF)
    d_qkv = jnp.concatenate([dq, dkv[0], dkv[1]], axis=1)
    g_wq = weight_grad(normed_in, d_qkv)
    d_normed_in = dot_f32(d_qkv, wq_all, ((1,), (1,)))
    d_in_part, d_gain_in, d_shift_in = norm_back(d_normed_in, xhat_in, rstd_in, gains[0])
    g_tok = d_resid_mid + d_in_part

    column_sum = lambda v: jnp.sum(v.astype(F32), axis=0)
    rows8 = jnp.stack(
        [
            d_gain_in, d_gain_mid, d_shift_in, d_shift_mid,
            column_sum(dq), column_sum(dkv[1]), column_sum(d_attn), column_sum(d_branch),
        ]
    )
    g_small = jnp.concatenate(
        [
            rows8.reshape(8, owners, span).transpose(1, 0, 2).reshape(owners, -1),
            column_sum(d_preact).reshape(owners, -1),
        ],
        axis=1,
    )
    sse_hi = sse.astype(BF).astype(F32)
    sse_row = jnp.stack([sse_hi, sse - sse_hi])

    if fast:
        cols = g_wq.shape[-1]
        rest = jnp.zeros((owners, 8, cols), F32)
        rest = rest.at[:, 0, : g_small.shape[1]].set(g_small)
        rest = rest.at[:, 1, :2].set(sse_row)
        rest = jnp.broadcast_to(
            rest.reshape(depth, 2, 1, 8, cols), (depth, 2, 2, 8, cols)
        )
        parts = [
            reduce_pieces(g_wdn, "xy"),
            reduce_pieces(jnp.concatenate([g_wup, g_wo], axis=-1), "yx"),
            reduce_pieces(jnp.concatenate([g_wq, rest], axis=3), "xy"),
        ]
        small_sum = parts[2][rows_a:]
        parts[2] = parts[2][:rows_a]
        split = g_wup.shape[-1]
        parts = [parts[2], parts[1][:, split:], parts[1][:, :split], parts[0]]

        def assemble(part):
            part = part.astype(BF)
            part = ordered(part, swap(part, "x"), chip, 0)
            return ordered(part, swap(part, "core"), core, 1).astype(F32)

        g_weights = [assemble(part) for part in parts]
        small_sum = small_sum + swap(small_sum, "core")
        small_mine = small_sum[0, : g_small.shape[1]]
        sse_all = small_sum[1, 0] + small_sum[1, 1]
    else:

        def generic(grad):
            grad = grad.reshape(-1, grad.shape[-1])
            part = lax.psum_scatter(
                grad, ("z", "y"), scatter_dimension=0, tiled=True
            ).astype(BF)
            part = lax.psum(part, "x")
            return ordered(part, swap(part, "core"), core, 1).astype(F32)

        g_weights = [generic(g) for g in (g_wq, g_wo, g_wup, g_wdn)]
        small_mine = lax.psum(
            lax.psum_scatter(g_small, ("z", "y"), scatter_dimension=0), ("x", "core")
        )
        sse_all = lax.psum(sse, ALL)
    distill_loss = sse_all / (count * width)

    def ungroup(value):
        mine = value[:local_len]
        other = swap(value[local_len:].astype(BF), "x").astype(value.dtype)
        return ordered(mine[None], other[None], chip, 0)

    vec = lambda start, n: small_mine[start * span : (start + n) * span].reshape(n, span)
    return (
        ungroup(result.astype(BF)),
        distill_loss,
        ungroup(g_tok),
        *g_weights,
        vec(0, 2),
        vec(2, 2),
        vec(4, 4),
        small_mine[8 * span :],
    )


def solution(mesh):
    seq, owners = mesh.shape["seq"], mesh.shape["shard"]
    fine = Mesh(mesh.devices.reshape(seq // 2, 2, owners // 2, 2), ALL)
    rows = ("z", "y")
    act = P(rows, ("x", "core"), None)
    mat, vec, col = P(rows, None), P(rows), P(None, rows)
    return jax.shard_map(
        shards,
        mesh=fine,
        in_specs=(act, act, act, vec, mat, mat, mat, mat, col, col, col, vec),
        out_specs=(act, P(), act, mat, mat, mat, mat, col, col, col, vec),
        check_vma=False,
    )
```

```python
import functools

import jax
import jax.numpy as jnp
from jax import lax
from jax.experimental import pallas as pl
from jax.experimental.pallas import tpu as pltpu
from jax.sharding import Mesh
from jax.sharding import PartitionSpec as P

HD = 64
EPSILON = 1e-06
NEG_FILL = -1e30
SCALE2 = HD**-0.5 * 1.4426950408889634
ALL = ("x", "core", "z", "y")
BF = jnp.bfloat16
F32 = jnp.float32


def dot_f32(a, b, dims):
    return lax.dot_general(a, b, (dims, ((), ())), preferred_element_type=F32)


def after(value, *done):
    return lax.optimization_barrier((value, *done))[0]


def folded_max(x):
    size = x.shape[0]
    while size > 8:
        size //= 2
        x = jnp.maximum(x[:size], x[size:])
    return jnp.max(x, axis=0, keepdims=True)


def side_rows(first, second):
    n = first.shape[1]

    def split(v):
        a = v.astype(BF).astype(F32)
        b = (v - a).astype(BF).astype(F32)
        return [a, b, (v - a - b).astype(BF).astype(F32)]

    zero = jnp.zeros((HD - 3, n), F32)
    return jnp.concatenate(split(second) + [zero] + split(first) + [zero], axis=0).T.astype(BF)


def by_lane(low, first, second):
    return jnp.where(low, first, second)


def attn_fwd_kernel(q_ref, k_ref, v_ref, side_ref, out_ref, aux_ref):
    rows = q_ref.shape[0]
    lane = lax.broadcasted_iota(jnp.int32, (rows, 2 * HD), 1)
    low = lane < HD
    q, k, side = q_ref[...], k_ref[...], side_ref[...]
    vt = v_ref[...].T
    ones = jnp.ones((16, rows), BF)
    mask_lane = jnp.where((lane == 3) | (lane == HD + 3), jnp.ones_like(q), jnp.zeros_like(q))
    parts, norms = [], []
    for head in range(2):
        sel = (lambda a, b: by_lane(low, a, b)) if head == 0 else (lambda a, b: by_lane(low, b, a))
        scores = dot_f32(sel(k, side), sel(q, mask_lane), ((1,), (1,)))
        top = folded_max(scores)
        expo = jnp.exp2((scores - top) * SCALE2).astype(BF)
        left = jnp.concatenate([vt[head * HD : (head + 1) * HD], ones], axis=0)
        mixed_t = dot_f32(left, expo, ((1,), (0,)))
        total = mixed_t[HD : HD + 1]
        parts.append(mixed_t[:HD] / total)
        norms.append(-(top + jnp.log2(total) * (1.0 / SCALE2)))
    out_ref[...] = jnp.concatenate(parts, axis=0).T.astype(BF)
    aux_ref[...] = side_rows(norms[0], norms[1]) + mask_lane


def attn_bwd_kernel(q_ref, k_ref, v_ref, side_ref, aux_ref, mix_ref, dmix_ref, dqkv_ref, sum_ref):
    rows = q_ref.shape[0]
    factor = HD**-0.5
    low = lax.broadcasted_iota(jnp.int32, (rows, 2 * HD), 1) < HD
    q, k, v, side = q_ref[...], k_ref[...], v_ref[...], side_ref[...]
    d, aux = dmix_ref[...], aux_ref[...]
    kt = k.T
    prod = (d.astype(F32) * mix_ref[...].astype(F32)).T
    deltas = side_rows(
        -jnp.sum(prod[:HD], axis=0, keepdims=True), -jnp.sum(prod[HD:], axis=0, keepdims=True)
    )
    zero = jnp.zeros_like(q)
    parts, dv, dk = [], None, None
    for head in range(2):
        sel = (lambda a, b: by_lane(low, a, b)) if head == 0 else (lambda a, b: by_lane(low, b, a))
        probs = jnp.exp2(dot_f32(sel(k, side), sel(q, aux), ((1,), (1,))) * SCALE2)
        d_scores = (probs * dot_f32(sel(v, side), sel(d, deltas), ((1,), (1,)))).astype(BF)
        dv_one = dot_f32(probs.astype(BF), sel(d, zero), ((1,), (0,)))
        dk_one = dot_f32(d_scores, sel(q, zero), ((1,), (0,)))
        dv = dv_one if head == 0 else dv + dv_one
        dk = dk_one if head == 0 else dk + dk_one
        parts.append(dot_f32(kt[head * HD : (head + 1) * HD], d_scores, ((1,), (0,))))
    dq = (jnp.concatenate(parts, axis=0) * factor).T
    for at, grad in enumerate((dq, dk * factor, dv)):
        grad = grad.astype(BF)
        dqkv_ref[:, at * 2 * HD : (at + 1) * 2 * HD] = grad
        sums = jnp.sum(grad.astype(F32), axis=0, keepdims=True)
        sum_ref[:, at * 2 * HD : (at + 1) * 2 * HD] = jnp.broadcast_to(sums, (8, 2 * HD))


def attention_forward(qkv, side, pair):
    rows = qkv.shape[0]
    col = lambda base: pl.BlockSpec((rows, 2 * HD), lambda i: (0, base))
    piece = jax.ShapeDtypeStruct((rows, 2 * HD), BF)
    return pl.pallas_call(
        attn_fwd_kernel,
        grid=(1,),
        in_specs=[col(3 * pair), col(3 * pair + 1), col(3 * pair + 2), col(0)],
        out_specs=[col(0), col(0)],
        out_shape=[piece, piece],
        cost_estimate=pl.CostEstimate(
            flops=rows * rows * HD * 32, bytes_accessed=rows * HD * 20,
            transcendentals=rows * rows * 2,
        ),
        name="attn_fwd",
    )(qkv, qkv, qkv, side)


def attention_backward(qkv, side, aux, mixed, d_mixed, pair):
    rows = qkv.shape[0]
    col = lambda base: pl.BlockSpec((rows, 2 * HD), lambda i: (0, base))
    return pl.pallas_call(
        attn_bwd_kernel,
        grid=(1,),
        in_specs=[col(3 * pair), col(3 * pair + 1), col(3 * pair + 2), col(0), col(0), col(0), col(pair)],
        out_specs=[
            pl.BlockSpec((rows, 6 * HD), lambda i: (0, 0)), pl.BlockSpec((8, 6 * HD), lambda i: (0, 0))
        ],
        out_shape=[
            jax.ShapeDtypeStruct((rows, 6 * HD), BF), jax.ShapeDtypeStruct((8, 6 * HD), F32)
        ],
        cost_estimate=pl.CostEstimate(
            flops=rows * rows * HD * 80, bytes_accessed=rows * HD * 30,
            transcendentals=rows * rows * 2,
        ),
        name="attn_bwd",
    )(qkv, qkv, qkv, side, aux, mixed, d_mixed)


def swap(value, axis):
    return lax.ppermute(value, axis, [(0, 1), (1, 0)])


def rot(value, shift):
    depth = lax.axis_size("z")
    return lax.ppermute(value, "z", [(i, (i + shift) % depth) for i in range(depth)])


def cross_swap(value, first_axis):
    sizes = [lax.axis_size(a) for a in ALL]
    pairs = []
    for x in range(sizes[0]):
        for core in range(sizes[1]):
            for z in range(sizes[2]):
                for y in range(sizes[3]):
                    over_y = (core == 0) == (first_axis == "y")
                    tx, ty = (x, 1 - y) if over_y else (1 - x, y)
                    flat = lambda a, b: ((a * sizes[1] + core) * sizes[2] + z) * sizes[3] + b
                    pairs.append((flat(x, y), flat(tx, ty)))
    return lax.ppermute(value, ALL, pairs)


def spread_z(piece):
    return [rot(piece, shift) for shift in range(1, lax.axis_size("z"))]


def spread_xy(own):
    first = cross_swap(own, "y")
    second = cross_swap(own, "x")
    return first, second, cross_swap(first, "x")


def place_kernel(moves, n_sources, slot_ref, *refs):
    sources, outs, sem = refs[:n_sources], refs[n_sources:-1], refs[-1]
    copies = []
    for source, step, slot_at, start, rows, offset, cols, out, column_at in moves:
        origin = sources[source]
        origin = origin if step is None else origin.at[step]
        z_at = slot_ref[(source if step is None else step) % 4]
        column = 0 if column_at is None else pl.multiple_of(slot_ref[column_at] * cols, 128)
        copies.append(
            pltpu.make_async_copy(
                origin.at[pl.ds(start, rows), pl.ds(offset, cols)],
                outs[out].at[z_at, slot_ref[slot_at], :, pl.ds(column, cols)],
                sem.at[len(copies)],
            )
        )
    for copy in copies:
        copy.start()
    for copy in copies:
        copy.wait()


def place(slots, sources, moves, shapes):
    return pl.pallas_call(
        functools.partial(place_kernel, moves, len(sources)),
        grid_spec=pltpu.PrefetchScalarGridSpec(
            num_scalar_prefetch=1,
            grid=(1,),
            in_specs=[pl.BlockSpec(memory_space=pl.ANY)] * len(sources),
            out_specs=[pl.BlockSpec(shape, lambda i, s: (0, 0, 0, 0)) for shape in shapes],
            scratch_shapes=[pltpu.SemaphoreType.DMA((len(moves),))],
        ),
        out_shape=[jax.ShapeDtypeStruct(shape, BF) for shape in shapes],
        name="place",
    )(slots, *sources)


def take(value, index, axis):
    return lax.dynamic_index_in_dim(value, index, axis, keepdims=False)


def join(parts):
    return parts[0] if len(parts) == 1 else jnp.concatenate(parts, axis=-1)


def reduce_y(grads, row_y):
    return swap(join([take(g, 1 - row_y, 1) for g in grads]), "y")


def reduce_z(grads, got, row_y, z):
    depth = lax.axis_size("z")

    def block(shift):
        at = (z + shift) % depth
        here = join([take(take(g, row_y, 1), at, 0) for g in grads])
        return here.astype(F32) + take(got, at, 0).astype(F32)

    return block(0), [rot(block(s).astype(BF), s) for s in range(1, depth)]


def reduce_x(own, parts):
    for part in parts:
        own = own + part.astype(F32)
    own = own.astype(BF)
    return own, swap(own, "x")


def reduce_core(own, got):
    both = (own.astype(F32) + got.astype(F32)).astype(BF)
    return both, swap(both, "core")


def ordered(mine, other, bit, axis):
    return jnp.where(
        bit == 0,
        jnp.concatenate([mine, other], axis),
        jnp.concatenate([other, mine], axis),
    )


def norm_stats(rows_in):
    centre = jnp.mean(rows_in, axis=-1, keepdims=True)
    centred = rows_in - centre
    second = jnp.mean(centred * centred, axis=-1, keepdims=True)
    return centre, lax.rsqrt(second + EPSILON)


def norm_back(grad, xhat, rstd, gain):
    scaled = grad * gain
    mean_a = jnp.mean(scaled, axis=-1, keepdims=True)
    mean_b = jnp.mean(scaled * xhat, axis=-1, keepdims=True)
    return (
        rstd * (scaled - mean_a - xhat * mean_b),
        jnp.sum(grad * xhat, axis=0, keepdims=True),
        jnp.sum(grad, axis=0, keepdims=True),
    )


def shards(
    tokens, teacher, cotangent, lengths, w_qkv, w_out, w_up, w_down,
    norm_gain, norm_bias, proj_bias, up_bias,
):
    groups, local_len, width = tokens.shape
    chip = lax.axis_index("x")
    core = lax.axis_index("core")
    row_y = lax.axis_index("y")
    row_z = lax.axis_index("z")
    depth = lax.axis_size("z")
    owners = depth * 2
    ff = w_down.shape[0] * owners
    span = width // owners
    fast = span % 32 == 0
    half = width // 2
    rows = 2 * groups * local_len
    mine = rows // 2
    pairs = half // (2 * HD)
    per_owner = ff // owners // 2

    def regroup(blocks):
        own = take(blocks, chip, 0)
        got = swap(take(blocks, 1 - chip, 0), "x")
        return jnp.concatenate([own, got], axis=0)

    def chip_rows(part):
        return ordered(part, swap(part, "core"), core, 0)

    def own_rows(value):
        return lax.dynamic_slice_in_dim(value, core * mine, mine, 0)

    def pair_major(v):
        part = take(v.reshape(-1, 3, 2, pairs, 2 * HD), core, 2)
        return part.transpose(0, 2, 1, 3).reshape(-1, 3 * half)

    wq_core = pair_major(w_qkv)
    wup_core = take(w_up.reshape(-1, owners, 2, per_owner), core, 2).reshape(-1, ff // 2)
    wo_core = lax.dynamic_slice_in_dim(w_out, core * half, half, 1)
    wdn_core = take(w_down.reshape(2, per_owner, width), core, 0)

    small = jnp.concatenate(
        [norm_gain.reshape(-1), norm_bias.reshape(-1), proj_bias.reshape(-1), up_bias]
    )
    len_parts = jnp.concatenate([lengths // 32, lengths % 32]).astype(BF)
    if fast:
        x_half = lambda w: take(w.reshape(2, -1, w.shape[1]), chip, 0)
        packed = jnp.zeros((8, 3 * half), BF)
        packed = packed.at[0, : small.size].set(small)
        packed = packed.at[1, : len_parts.size].set(len_parts)
        piece_a = jnp.concatenate([x_half(wq_core), packed], axis=0)
        rots_a = spread_z(piece_a)
        tok_part = regroup(tokens)
        piece_b = jnp.concatenate([x_half(wo_core), x_half(wup_core)], axis=1)
        rots_b = spread_z(after(piece_b, *rots_a))
        own_a = jnp.stack([piece_a] + rots_a)
        rest_a = spread_xy(own_a)
        tok_all = chip_rows(after(tok_part, own_a))
        rots_c = spread_z(after(wdn_core, *rots_b))
        own_b = after(jnp.stack([piece_b] + rots_b), rest_a[2])
        rest_b = spread_xy(own_b)

        slot_of = lambda y, x: y * 2 + x
        slot_first = jnp.where(core == 0, slot_of(1 - row_y, chip), slot_of(row_y, 1 - chip))
        slot_second = jnp.where(core == 0, slot_of(row_y, 1 - chip), slot_of(1 - row_y, chip))
        slots = jnp.stack(
            [(row_z - s) % depth for s in range(depth)]
            + [slot_of(row_y, chip), slot_first, slot_second, slot_of(1 - row_y, 1 - chip)]
            + [core, 1 - core, row_y, 1 - row_y]
        ).astype(jnp.int32)
        rows_a = span // 2
        steps = range(depth)
        wq_all, small_all = place(
            slots, [own_a, *rest_a],
            [(i, s, 4 + i, 0, rows_a, 0, 3 * half, 0, None) for i in range(4) for s in steps]
            + [(i, s, 4 + i, rows_a, 8, 0, 3 * half, 1, None) for i in range(4) for s in steps],
            [(depth, 4, rows_a, 3 * half), (depth, 4, 8, 3 * half)],
        )
        wq_all = wq_all.reshape(width, -1)
        small_all = small_all[:, ::2].reshape(owners, 8, -1)
        lens_all = small_all[:, 1, : len_parts.size]
        small_all = small_all[:, 0, : small.size]
    else:
        tok_all = chip_rows(regroup(tokens))
        full = lambda w: lax.all_gather(w, ("z", "y"), axis=0, tiled=True)
        wq_all, wup_all, wdn_all, wo_all = map(full, (wq_core, wup_core, wdn_core, w_out))
        small_all = lax.all_gather(small, ("z", "y"), axis=0)
        lens_all = lax.all_gather(len_parts, ("z", "y"), axis=0)
    small_all = small_all.astype(F32)

    def vectors(start, count):
        part = small_all[:, start * span : (start + count) * span]
        return part.reshape(owners, count, span).transpose(1, 0, 2).reshape(count, width)

    gains, shifts, biases = vectors(0, 2), vectors(2, 2), vectors(4, 4)
    up_shift = take(small_all[:, 8 * span :].reshape(owners, 2, per_owner), core, 1).reshape(-1)
    qkv_bias = pair_major(
        jnp.concatenate([biases[0], jnp.zeros((width,), F32), biases[1]])[None]
    )
    lens_f = lens_all.astype(F32)
    count = jnp.sum(lens_f[:, :groups] * 32.0 + lens_f[:, groups:])

    length = take(lengths, chip, 0)
    steps_at = jnp.arange(local_len, dtype=jnp.int32)
    row_at = jnp.concatenate(
        [(x_at * 2 + c_at) * local_len + steps_at for c_at in range(2) for x_at in (chip, 1 - chip)]
    )
    live = (row_at < length).astype(F32)[:, None]
    lane = jnp.arange(2 * HD, dtype=jnp.int32)[None, :] % HD
    mask = jnp.where(row_at < length, 0.0, NEG_FILL)[:, None]
    side = jnp.where(lane < 3, 1.0, jnp.where(lane == 3, mask, 0.0)).astype(BF)

    inputs = tok_all.astype(F32)
    centre_in, rstd_in = norm_stats(inputs)
    normed_in = ((inputs - centre_in) * rstd_in * gains[0] + shifts[0]).astype(BF)
    qkv = (dot_f32(normed_in, wq_all, ((1,), (0,))) + qkv_bias).astype(BF)
    fwd = []
    mixed_away = []
    part_tea, part_cot = regroup(teacher), regroup(cotangent)
    for pair in range(pairs):
        if fast and pair == 0:
            qkv = after(qkv, rest_b[0])
            swap_o = [swap(v[..., :half], "core") for v in (own_b, *rest_b)]
            own_c = [wdn_core] + rots_c
        if fast and pair == 1:
            qkv = after(qkv, *rots_c)
            away_c = [swap(after(v, rest_b[2]), "y") for v in own_c]
            part_tea = regroup(after(teacher, rest_b[1]))
        if fast and pair == 2:
            part_cot = regroup(after(cotangent, rest_b[1]))
        fwd.append(attention_forward(qkv, side, pair))
        mixed_away.append(swap(fwd[pair][0], "core"))
    if fast:
        moves = []
        for i in range(4):
            for s in steps:
                moves.append((i, s, 4 + i, 0, rows_a, half, ff // 2, 1, None))
                moves.append((i, s, 4 + i, 0, rows_a, 0, half, 0, 8))
                moves.append((4 + i, s, 4 + (0, 2, 1, 3)[i], 0, rows_a, 0, half, 0, 9))
        wo_all, wup_all = place(
            slots, [own_b, *rest_b, *swap_o], moves,
            [(depth, 4, rows_a, width), (depth, 4, rows_a, ff // 2)],
        )
        wo_all, wup_all = wo_all.reshape(width, -1), wup_all.reshape(width, -1)
    mixed_parts = [part for part, _ in fwd]
    mixed = ordered(
        jnp.concatenate(mixed_parts, axis=1), jnp.concatenate(mixed_away, axis=1), core, 1
    )
    resid_mid = inputs + dot_f32(mixed, wo_all, ((1,), (0,))) + biases[2]
    centre_mid, rstd_mid = norm_stats(resid_mid)
    xhat_mid = (resid_mid - centre_mid) * rstd_mid
    normed_mid = (xhat_mid * gains[1] + shifts[1]).astype(BF)
    preact = dot_f32(normed_mid, wup_all, ((1,), (0,))) + up_shift
    bell = 0.5 * (1.0 + lax.erf(preact * 0.7071067811865476))
    activ = (preact * bell).astype(BF)
    slope = (
        bell + preact * jnp.exp(-0.5 * preact * preact) * 0.3989422804014327
    ).astype(BF)
    if fast:
        (wdn_all,) = place(
            slots, own_c + away_c,
            [(4 * i + s, None, 10 + i, 0, per_owner, 0, width, 0, None) for i in range(2) for s in steps],
            [(depth, 2, per_owner, width)],
        )
        wdn_all = wdn_all.reshape(-1, width)
    down = dot_f32(activ, wdn_all, ((1,), (0,))).astype(BF)
    tea_all, cot_all = chip_rows(part_tea), chip_rows(part_cot)
    result = resid_mid + (down.astype(F32) + swap(down, "core").astype(F32)) + biases[3]
    error = result - tea_all.astype(F32)
    sse = 0.5 * jnp.sum(live * error * error)

    d_result = live * (cot_all.astype(F32) + 2.0 / (count * width) * error)
    d_branch = d_result.astype(BF)

    def leave(value):
        return swap(value[local_len:].astype(BF), "x")

    def ungroup(value, there):
        return ordered(value[None, :local_len], there.astype(value.dtype)[None], chip, 0)

    def weight_grad(left, right):
        grad = dot_f32(left, right, ((0,), (0,))).astype(BF if fast else F32)
        return grad.reshape(depth, 2, -1, grad.shape[1])

    column_sum = lambda v: jnp.sum(v.astype(F32), axis=0, keepdims=True)
    output_own = own_rows(result).astype(BF)
    output_there = leave(output_own)
    g_wdn = weight_grad(activ, d_branch)
    if fast:
        y_c = reduce_y([g_wdn], row_y)
    d_activ = dot_f32(d_branch, wdn_all, ((1,), (1,)))
    d_preact = (d_activ * slope.astype(F32)).astype(BF)
    d_norm_part = dot_f32(d_preact, wup_all, ((1,), (1,))).astype(BF)
    d_norm_away = swap(d_norm_part, "core")
    g_wup = weight_grad(normed_mid, d_preact)
    if fast:
        y_b = reduce_y([after(g_wup, y_c)], row_y)
    d_normed_mid = d_norm_part.astype(F32) + d_norm_away.astype(F32)
    d_mid_part, d_gain_mid, d_shift_mid = norm_back(
        d_normed_mid, xhat_mid, rstd_mid, gains[1]
    )
    d_resid_mid = d_result + d_mid_part
    d_attn = d_resid_mid.astype(BF)
    wo_rows = lax.dynamic_slice_in_dim(wo_all, core * half, half, 0)
    d_mixed = dot_f32(d_attn, wo_rows, ((1,), (1,))).astype(BF)
    g_wo = weight_grad(mixed, lax.dynamic_slice_in_dim(d_attn, core * half, half, 1))
    d_pairs, sums, g_pairs = [], [], []
    if fast:
        z_c = reduce_z([g_wdn], y_c, row_y, row_z)
        d_mixed = after(d_mixed, z_c[0], output_there)
    for pair in range(pairs):
        if fast and pair == 1:
            d_mixed = after(d_mixed, y_b)
            z_b = reduce_z([g_wup], y_b, row_y, row_z)
        if fast and pair == pairs - 1:
            x_c = reduce_x(*z_c)
            early = [g_wo] + g_pairs
            y_o = reduce_y(early, row_y)
            d_mixed = after(d_mixed, x_c[0])
        d_pair, sum_pair = attention_backward(
            qkv, side, fwd[pair][1], mixed_parts[pair], d_mixed, pair
        )
        d_pairs.append(d_pair)
        sums.append(sum_pair[:1])
        g_pairs.append(weight_grad(normed_in, d_pair))
    if fast:
        late = g_pairs[pairs - 1 :]
        y_a = reduce_y(late, row_y)
    pair_cols = 6 * HD
    d_in = 0.0
    for pair in range(pairs):
        columns = wq_all[:, pair * pair_cols : (pair + 1) * pair_cols]
        d_in = d_in + dot_f32(d_pairs[pair], columns, ((1,), (1,)))
    d_in_half = d_in.astype(BF)
    d_in_away = swap(lax.dynamic_slice_in_dim(d_in_half, (1 - core) * mine, mine, 0), "core")
    d_normed_in = own_rows(d_in_half).astype(F32) + d_in_away.astype(F32)
    xhat_own = (own_rows(inputs) - own_rows(centre_in)) * own_rows(rstd_in)
    d_in_part, d_gain_in, d_shift_in = norm_back(
        d_normed_in, xhat_own, own_rows(rstd_in), gains[0]
    )
    g_tok = own_rows(d_resid_mid) + d_in_part
    g_tok_there = leave(g_tok)

    at_half = lambda v: lax.dynamic_update_slice_in_dim(
        jnp.zeros((1, width), F32), v, core * half, 1
    )
    up_both = lax.dynamic_update_slice_in_dim(
        jnp.zeros((owners, 2, per_owner), F32), column_sum(d_preact).reshape(owners, 1, per_owner), core, 1
    )
    by_part = jnp.concatenate(sums, axis=0).reshape(pairs, 3, 2 * HD)
    q_sums, v_sums = by_part[:, 0].reshape(1, half), by_part[:, 2].reshape(1, half)
    small_rows = [
        up_both.reshape(-1, width),
        0.5 * d_gain_mid, 0.5 * d_shift_mid, 0.5 * column_sum(d_attn), 0.5 * column_sum(d_branch),
        jnp.full((1, width), sse), at_half(q_sums), at_half(v_sums), d_gain_in, d_shift_in,
    ]
    total = jnp.concatenate(small_rows, axis=0)
    if fast:
        for axis in ("core", "x", "y"):
            total = total + swap(total, axis)
        spread = jnp.stack([total] + spread_z(total))
        total = 0.0
        for at in range(depth):
            total = total + take(spread, (row_z - at) % depth, 0)
    else:
        total = lax.psum(total, ALL)
    owner = row_z * 2 + row_y
    n_up = ff // width
    up_mine = take(total[:n_up].reshape(owners, -1), owner, 0)
    vec_mine = lax.dynamic_slice_in_dim(total[n_up:], owner * span, span, 1)
    distill_loss = total[n_up + 4, 0] / (count * width)
    vec = lambda *at: jnp.concatenate([vec_mine[i : i + 1] for i in at], axis=0)

    if fast:
        x_b = reduce_x(*z_b)
        part_c = reduce_core(*x_c)
        z_o = reduce_z(early, y_o, row_y, row_z)
        part_b = reduce_core(*x_b)
        x_o = reduce_x(*z_o)
        z_a = reduce_z(late, y_a, row_y, row_z)
        part_o = reduce_core(*x_o)
        x_a = reduce_x(*z_a)
        part_a = reduce_core(*x_a)
        cut = lambda part, at: [v[:, at * half : (at + 1) * half] for v in part]
        part_w = cut(part_o, 0)
        parts_q = [cut(part_o, 1 + at) for at in range(pairs - 1)] + [list(part_a)]
        parts_u, parts_d = part_b, part_c
    else:

        def generic(grad):
            grad = grad.reshape(-1, grad.shape[-1])
            part = lax.psum_scatter(
                grad, ("z", "y"), scatter_dimension=0, tiled=True
            ).astype(BF)
            part = lax.psum(part, "x")
            return part, swap(part, "core")

        part_w, parts_u, parts_d = generic(g_wo), generic(g_wup), generic(g_wdn)
        parts_q = [generic(g) for g in g_pairs]

    sorted_q = [ordered(own[None], got[None], core, 0) for own, got in parts_q]
    g_qkv = jnp.concatenate(
        [
            part[c, :, at * 2 * HD : (at + 1) * 2 * HD]
            for at in range(3) for c in range(2) for part in sorted_q
        ],
        axis=1,
    ).astype(F32)
    g_out = ordered(*part_w, core, 1).astype(F32)
    cols_u = lambda v: v.reshape(span, owners, 1, per_owner)
    g_up = ordered(*map(cols_u, parts_u), core, 2).reshape(span, -1).astype(F32)
    g_down = ordered(*parts_d, core, 0).astype(F32)

    return (
        ungroup(output_own, output_there),
        distill_loss,
        ungroup(g_tok, g_tok_there),
        g_qkv,
        g_out,
        g_up,
        g_down,
        vec(7, 0),
        vec(8, 1),
        vec(5, 6, 2, 3),
        up_mine,
    )


def solution(mesh):
    seq, owners = mesh.shape["seq"], mesh.shape["shard"]
    fine = Mesh(mesh.devices.reshape(seq // 2, 2, owners // 2, 2), ALL)
    rows = ("z", "y")
    act = P(rows, ("x", "core"), None)
    mat, vec, col = P(rows, None), P(rows), P(None, rows)
    return jax.shard_map(
        shards,
        mesh=fine,
        in_specs=(act, act, act, vec, mat, mat, mat, mat, col, col, col, vec),
        out_specs=(act, P(), act, mat, mat, mat, mat, col, col, col, vec),
        check_vma=False,
    )
```

```python
import functools

import jax
import jax.numpy as jnp
from jax import lax
from jax.experimental import pallas as pl
from jax.experimental.pallas import tpu as pltpu
from jax.sharding import Mesh
from jax.sharding import PartitionSpec as P

HD = 64
EPSILON = 1e-06
NEG_FILL = -1e30
SCALE2 = HD**-0.5 * 1.4426950408889634
ALL = ("x", "core", "z", "y")
BF = jnp.bfloat16
F32 = jnp.float32
BRIEF = pl.CostEstimate(flops=10**8, bytes_accessed=10**5, transcendentals=0)


def dot_f32(a, b, dims):
    return lax.dot_general(a, b, (dims, ((), ())), preferred_element_type=F32)


def after(value, *done):
    return lax.optimization_barrier((value, *done))[0]


def folded_max(x):
    size = x.shape[0]
    while size > 8:
        size //= 2
        x = jnp.maximum(x[:size], x[size:])
    return jnp.max(x, axis=0, keepdims=True)


def side_rows(first, second):
    n = first.shape[1]

    def split(v):
        a = v.astype(BF).astype(F32)
        b = (v - a).astype(BF).astype(F32)
        return [a, b, (v - a - b).astype(BF).astype(F32)]

    zero = jnp.zeros((HD - 3, n), F32)
    return jnp.concatenate(split(second) + [zero] + split(first) + [zero], axis=0).T.astype(BF)


def by_lane(low, first, second):
    return jnp.where(low, first, second)


def attn_fwd_kernel(q_ref, k_ref, v_ref, side_ref, out_ref, aux_ref):
    rows = q_ref.shape[0]
    lane = lax.broadcasted_iota(jnp.int32, (rows, 2 * HD), 1)
    low = lane < HD
    q, k, side = q_ref[...], k_ref[...], side_ref[...]
    vt = v_ref[...].T
    ones = jnp.ones((16, rows), BF)
    mask_lane = jnp.where((lane == 3) | (lane == HD + 3), jnp.ones_like(q), jnp.zeros_like(q))
    parts, norms = [], []
    for head in range(2):
        sel = (lambda a, b: by_lane(low, a, b)) if head == 0 else (lambda a, b: by_lane(low, b, a))
        scores = dot_f32(sel(k, side), sel(q, mask_lane), ((1,), (1,)))
        top = folded_max(scores)
        expo = jnp.exp2((scores - top) * SCALE2).astype(BF)
        left = jnp.concatenate([vt[head * HD : (head + 1) * HD], ones], axis=0)
        mixed_t = dot_f32(left, expo, ((1,), (0,)))
        total = mixed_t[HD : HD + 1]
        parts.append(mixed_t[:HD] / total)
        norms.append(-(top + jnp.log2(total) * (1.0 / SCALE2)))
    out_ref[...] = jnp.concatenate(parts, axis=0).T.astype(BF)
    aux_ref[...] = side_rows(norms[0], norms[1]) + mask_lane


def attn_bwd_kernel(q_ref, k_ref, v_ref, side_ref, aux_ref, mix_ref, dmix_ref, dqkv_ref, sum_ref):
    rows = q_ref.shape[0]
    factor = HD**-0.5
    low = lax.broadcasted_iota(jnp.int32, (rows, 2 * HD), 1) < HD
    q, k, v, side = q_ref[...], k_ref[...], v_ref[...], side_ref[...]
    d, aux = dmix_ref[...], aux_ref[...]
    kt = k.T
    prod = (d.astype(F32) * mix_ref[...].astype(F32)).T
    deltas = side_rows(
        -jnp.sum(prod[:HD], axis=0, keepdims=True), -jnp.sum(prod[HD:], axis=0, keepdims=True)
    )
    zero = jnp.zeros_like(q)
    parts, dv, dk = [], None, None
    for head in range(2):
        sel = (lambda a, b: by_lane(low, a, b)) if head == 0 else (lambda a, b: by_lane(low, b, a))
        probs = jnp.exp2(dot_f32(sel(k, side), sel(q, aux), ((1,), (1,))) * SCALE2)
        d_scores = (probs * dot_f32(sel(v, side), sel(d, deltas), ((1,), (1,)))).astype(BF)
        dv_one = dot_f32(probs.astype(BF), sel(d, zero), ((1,), (0,)))
        dk_one = dot_f32(d_scores, sel(q, zero), ((1,), (0,)))
        dv = dv_one if head == 0 else dv + dv_one
        dk = dk_one if head == 0 else dk + dk_one
        parts.append(dot_f32(kt[head * HD : (head + 1) * HD], d_scores, ((1,), (0,))))
    dq = (jnp.concatenate(parts, axis=0) * factor).T
    for at, grad in enumerate((dq, dk * factor, dv)):
        grad = grad.astype(BF)
        dqkv_ref[:, at * 2 * HD : (at + 1) * 2 * HD] = grad
        sums = jnp.sum(grad.astype(F32), axis=0, keepdims=True)
        sum_ref[:, at * 2 * HD : (at + 1) * 2 * HD] = jnp.broadcast_to(sums, (8, 2 * HD))


def attention_forward(qkv, side, pair):
    rows = qkv.shape[0]
    col = lambda base: pl.BlockSpec((rows, 2 * HD), lambda i: (0, base))
    piece = jax.ShapeDtypeStruct((rows, 2 * HD), BF)
    return pl.pallas_call(
        attn_fwd_kernel,
        grid=(1,),
        in_specs=[col(3 * pair), col(3 * pair + 1), col(3 * pair + 2), col(0)],
        out_specs=[col(0), col(0)],
        out_shape=[piece, piece],
        cost_estimate=BRIEF,
        name="attn_fwd",
    )(qkv, qkv, qkv, side)


def attention_backward(qkv, side, aux, mixed, d_mixed, pair):
    rows = qkv.shape[0]
    col = lambda base: pl.BlockSpec((rows, 2 * HD), lambda i: (0, base))
    return pl.pallas_call(
        attn_bwd_kernel,
        grid=(1,),
        in_specs=[col(3 * pair), col(3 * pair + 1), col(3 * pair + 2), col(0), col(0), col(0), col(pair)],
        out_specs=[
            pl.BlockSpec((rows, 6 * HD), lambda i: (0, 0)), pl.BlockSpec((8, 6 * HD), lambda i: (0, 0))
        ],
        out_shape=[
            jax.ShapeDtypeStruct((rows, 6 * HD), BF), jax.ShapeDtypeStruct((8, 6 * HD), F32)
        ],
        cost_estimate=BRIEF,
        name="attn_bwd",
    )(qkv, qkv, qkv, side, aux, mixed, d_mixed)


def swap(value, axis):
    return lax.ppermute(value, axis, [(0, 1), (1, 0)])


def trade_z(blocks):
    return lax.all_to_all(blocks, "z", 0, 0, tiled=True)


def cross_swap(value, first_axis):
    sizes = [lax.axis_size(a) for a in ALL]
    pairs = []
    for x in range(sizes[0]):
        for core in range(sizes[1]):
            for z in range(sizes[2]):
                for y in range(sizes[3]):
                    over_y = (core == 0) == (first_axis == "y")
                    tx, ty = (x, 1 - y) if over_y else (1 - x, y)
                    flat = lambda a, b: ((a * sizes[1] + core) * sizes[2] + z) * sizes[3] + b
                    pairs.append((flat(x, y), flat(tx, ty)))
    return lax.ppermute(value, ALL, pairs)


def spread_z(piece):
    return trade_z(jnp.broadcast_to(piece[None], (lax.axis_size("z"),) + piece.shape))


def place_kernel(moves, n_sources, slot_ref, *refs):
    sources, outs, sem = refs[:n_sources], refs[n_sources:-1], refs[-1]
    copies = []
    for source, step, slot_at, start, rows, offset, cols, out in moves:
        copies.append(
            pltpu.make_async_copy(
                sources[source].at[step, pl.ds(start, rows), pl.ds(offset, cols)],
                outs[out].at[step, slot_ref[slot_at]],
                sem.at[len(copies)],
            )
        )
    for copy in copies:
        copy.start()
    for copy in copies:
        copy.wait()


def place(slots, sources, moves, shapes):
    return pl.pallas_call(
        functools.partial(place_kernel, moves, len(sources)),
        grid_spec=pltpu.PrefetchScalarGridSpec(
            num_scalar_prefetch=1,
            grid=(1,),
            in_specs=[pl.BlockSpec(memory_space=pl.ANY)] * len(sources),
            out_specs=[pl.BlockSpec(shape, lambda i, s: (0, 0, 0, 0)) for shape in shapes],
            scratch_shapes=[pltpu.SemaphoreType.DMA((len(moves),))],
        ),
        out_shape=[jax.ShapeDtypeStruct(shape, BF) for shape in shapes],
        name="place",
    )(slots, *sources)


def take(value, index, axis):
    return lax.dynamic_index_in_dim(value, index, axis, keepdims=False)


def join(parts):
    return parts[0] if len(parts) == 1 else jnp.concatenate(parts, axis=-1)


def blocks_z(grads, got, row_y):
    here = join([take(g, row_y, 1) for g in grads])
    return (here.astype(F32) + got.astype(F32)).astype(BF)


def away_y(grads, row_y):
    return join([take(g, 1 - row_y, 1) for g in grads])


def summed(parts):
    return jnp.sum(parts.astype(F32), axis=0).astype(BF)


def column_half(value, which):
    size = value.shape[-1] // 2
    return lax.dynamic_slice_in_dim(value, which * size, size, value.ndim - 1)


def reduce_core(own, got):
    both = (own.astype(F32) + got.astype(F32)).astype(BF)
    return both, swap(both, "core")


def ordered(mine, other, bit, axis):
    return jnp.where(
        bit == 0,
        jnp.concatenate([mine, other], axis),
        jnp.concatenate([other, mine], axis),
    )


def norm_stats(rows_in):
    centre = jnp.mean(rows_in, axis=-1, keepdims=True)
    centred = rows_in - centre
    second = jnp.mean(centred * centred, axis=-1, keepdims=True)
    return centre, lax.rsqrt(second + EPSILON)


def norm_back(grad, xhat, rstd, gain):
    scaled = grad * gain
    mean_a = jnp.mean(scaled, axis=-1, keepdims=True)
    mean_b = jnp.mean(scaled * xhat, axis=-1, keepdims=True)
    return (
        rstd * (scaled - mean_a - xhat * mean_b),
        jnp.sum(grad * xhat, axis=0, keepdims=True),
        jnp.sum(grad, axis=0, keepdims=True),
    )


def shards(
    tokens, teacher, cotangent, lengths, w_qkv, w_out, w_up, w_down,
    norm_gain, norm_bias, proj_bias, up_bias,
):
    groups, local_len, width = tokens.shape
    chip = lax.axis_index("x")
    core = lax.axis_index("core")
    row_y = lax.axis_index("y")
    row_z = lax.axis_index("z")
    depth = lax.axis_size("z")
    owners = depth * 2
    ff = w_down.shape[0] * owners
    span = width // owners
    fast = span % 32 == 0
    half = width // 2
    rows = 2 * groups * local_len
    mine = rows // 2
    pairs = half // (2 * HD)
    per_owner = ff // owners // 2

    def regroup(blocks):
        own = take(blocks, chip, 0)
        got = swap(take(blocks, 1 - chip, 0), "x")
        return jnp.concatenate([own, got], axis=0)

    def chip_rows(part):
        return ordered(part, swap(part, "core"), core, 0)

    def own_rows(value):
        return lax.dynamic_slice_in_dim(value, core * mine, mine, 0)

    def pair_major(v):
        part = take(v.reshape(-1, 3, 2, pairs, 2 * HD), core, 2)
        return part.transpose(0, 2, 1, 3).reshape(-1, 3 * half)

    wq_core = pair_major(w_qkv)
    wup_core = take(w_up.reshape(-1, owners, 2, per_owner), core, 2).reshape(-1, ff // 2)
    wdn_core = take(w_down.reshape(2, per_owner, width), core, 0)

    small = jnp.concatenate(
        [norm_gain.reshape(-1), norm_bias.reshape(-1), proj_bias.reshape(-1), up_bias]
    )
    len_parts = jnp.concatenate([lengths // 32, lengths % 32]).astype(BF)
    if fast:
        x_half = lambda w: take(w.reshape(2, -1, w.shape[1]), chip, 0)
        packed = jnp.zeros((8, 3 * half), BF)
        packed = packed.at[0, : small.size].set(small)
        packed = packed.at[1, : len_parts.size].set(len_parts)
        piece_a = jnp.concatenate([x_half(wq_core), packed], axis=0)
        own_a = spread_z(piece_a)
        tok_part = regroup(tokens)
        piece_b = jnp.concatenate([x_half(w_out), x_half(wup_core)], axis=1)
        rest_a = [cross_swap(own_a, "y"), cross_swap(own_a, "x")]
        rest_a.append(cross_swap(rest_a[0], "x"))
        own_b = spread_z(after(piece_b, rest_a[0]))
        tok_all = chip_rows(after(tok_part, own_a))
        rest_b = [cross_swap(after(own_b, rest_a[2]), axis) for axis in "yx"]

        slot_of = lambda y, x: y * 2 + x
        slot_first = jnp.where(core == 0, slot_of(1 - row_y, chip), slot_of(row_y, 1 - chip))
        slot_second = jnp.where(core == 0, slot_of(row_y, 1 - chip), slot_of(1 - row_y, chip))
        slots = jnp.stack(
            [slot_of(row_y, chip), slot_first, slot_second, slot_of(1 - row_y, 1 - chip)]
            + [row_y, 1 - row_y]
        ).astype(jnp.int32)
        rows_a = span // 2
        steps = range(depth)
        wq_all, small_all = place(
            slots, [own_a, *rest_a],
            [(i, s, i, 0, rows_a, 0, 3 * half, 0) for i in range(4) for s in steps]
            + [(i, s, i, rows_a, 8, 0, 3 * half, 1) for i in range(4) for s in steps],
            [(depth, 4, rows_a, 3 * half), (depth, 4, 8, 3 * half)],
        )
        own_c = spread_z(after(wdn_core, wq_all))
        wq_all = wq_all.reshape(width, -1)
        small_all = small_all[:, ::2].reshape(owners, 8, -1)
        lens_all = small_all[:, 1, : len_parts.size]
        small_all = small_all[:, 0, : small.size]
    else:
        tok_all = chip_rows(regroup(tokens))
        full = lambda w: lax.all_gather(w, ("z", "y"), axis=0, tiled=True)
        wq_all, wup_all, wdn_all, wo_all = map(full, (wq_core, wup_core, wdn_core, w_out))
        small_all = lax.all_gather(small, ("z", "y"), axis=0)
        lens_all = lax.all_gather(len_parts, ("z", "y"), axis=0)
    small_all = small_all.astype(F32)

    def vectors(start, count):
        part = small_all[:, start * span : (start + count) * span]
        return part.reshape(owners, count, span).transpose(1, 0, 2).reshape(count, width)

    gains, shifts, biases = vectors(0, 2), vectors(2, 2), vectors(4, 4)
    up_shift = take(small_all[:, 8 * span :].reshape(owners, 2, per_owner), core, 1).reshape(-1)
    qkv_bias = pair_major(
        jnp.concatenate([biases[0], jnp.zeros((width,), F32), biases[1]])[None]
    )
    lens_f = lens_all.astype(F32)
    count = jnp.sum(lens_f[:, :groups] * 32.0 + lens_f[:, groups:])

    length = take(lengths, chip, 0)
    steps_at = jnp.arange(local_len, dtype=jnp.int32)
    row_at = jnp.concatenate(
        [(x_at * 2 + c_at) * local_len + steps_at for c_at in range(2) for x_at in (chip, 1 - chip)]
    )
    live = (row_at < length).astype(F32)[:, None]
    lane = jnp.arange(2 * HD, dtype=jnp.int32)[None, :] % HD
    mask = jnp.where(row_at < length, 0.0, NEG_FILL)[:, None]
    side = jnp.where(lane < 3, 1.0, jnp.where(lane == 3, mask, 0.0)).astype(BF)

    inputs = tok_all.astype(F32)
    centre_in, rstd_in = norm_stats(inputs)
    normed_in = ((inputs - centre_in) * rstd_in * gains[0] + shifts[0]).astype(BF)
    qkv = (dot_f32(normed_in, wq_all, ((1,), (0,))) + qkv_bias).astype(BF)
    fwd = []
    mixed_away = []
    targets = [teacher, cotangent]
    for pair in range(pairs):
        if fast and pair == 1:
            qkv = after(qkv, rest_b[0], rest_b[1])
        if fast and pair == 2:
            qkv = after(qkv, own_c)
        fwd.append(attention_forward(qkv, side, pair))
        mixed_away.append(swap(fwd[pair][0], "core"))
        if fast and pair == 0:
            rest_b.append(cross_swap(after(rest_b[0], fwd[0][0]), "x"))
        if fast and pair == 1:
            biases, up_shift = (after(v, fwd[1][0]) for v in (biases, up_shift))
            targets = [after(v, fwd[1][0]) for v in targets]
    if fast:
        away_c = swap(own_c, "y")
        moves = []
        for i in range(4):
            for s in steps:
                moves.append((i, s, i, 0, rows_a, width, ff // 2, 1))
                moves.append((i, s, i, 0, rows_a, 0, width, 0))
        wo_all, wup_all = place(
            slots, [own_b, *rest_b], moves,
            [(depth, 4, rows_a, width), (depth, 4, rows_a, ff // 2)],
        )
        wo_all, wup_all = wo_all.reshape(width, -1), wup_all.reshape(width, -1)
    mixed_parts = [part for part, _ in fwd]
    tied = [after(part, wo_all) for part in mixed_parts]
    mixed = ordered(
        jnp.concatenate(tied, axis=1), jnp.concatenate(mixed_away, axis=1), core, 1
    )
    resid_mid = inputs + dot_f32(mixed, wo_all, ((1,), (0,))) + biases[2]
    centre_mid, rstd_mid = norm_stats(resid_mid)
    xhat_mid = (resid_mid - centre_mid) * rstd_mid
    normed_mid = (xhat_mid * gains[1] + shifts[1]).astype(BF)
    preact = dot_f32(normed_mid, wup_all, ((1,), (0,))) + up_shift
    bell = 0.5 * (1.0 + lax.erf(preact * 0.7071067811865476))
    activ = (preact * bell).astype(BF)
    slope = (
        bell + preact * jnp.exp(-0.5 * preact * preact) * 0.3989422804014327
    ).astype(BF)
    if fast:
        (wdn_all,) = place(
            slots, [after(own_c, activ), away_c],
            [(i, s, 4 + i, 0, per_owner, 0, width, 0) for i in range(2) for s in steps],
            [(depth, 2, per_owner, width)],
        )
        wdn_all = wdn_all.reshape(-1, width)
    down = dot_f32(activ, wdn_all, ((1,), (0,))).astype(BF)
    both_at = lambda at: jnp.stack([take(v, at, 0) for v in targets])
    here, there = both_at(chip), swap(both_at(1 - chip), "x")
    here = jnp.concatenate([here, there], axis=1)
    here = ordered(here, swap(here, "core"), core, 1)
    tea_all, cot_all = here[0], here[1]
    result = resid_mid + (down.astype(F32) + swap(down, "core").astype(F32)) + biases[3]
    error = result - tea_all.astype(F32)
    sse = 0.5 * jnp.sum(live * error * error)

    d_result = live * (cot_all.astype(F32) + 2.0 / (count * width) * error)
    d_branch = d_result.astype(BF)

    def leave(value):
        return swap(value[local_len:].astype(BF), "x")

    def ungroup(value, there):
        return ordered(value[None, :local_len], there.astype(value.dtype)[None], chip, 0)

    def weight_grad(left, right):
        grad = dot_f32(left, right, ((0,), (0,))).astype(BF if fast else F32)
        return grad.reshape(depth, 2, -1, grad.shape[1])

    column_sum = lambda v: jnp.sum(v.astype(F32), axis=0, keepdims=True)
    output_own = own_rows(result).astype(BF)
    output_there = leave(output_own)
    g_wdn = weight_grad(activ, d_branch)
    if fast:
        send_c = column_half(g_wdn, 1 - chip)
        first_c = swap(send_c, "x")
        d_branch_b = after(d_branch, send_c)
    else:
        d_branch_b = d_branch
    d_activ = dot_f32(d_branch_b, wdn_all, ((1,), (1,)))
    d_preact = (d_activ * slope.astype(F32)).astype(BF)
    d_norm_part = dot_f32(d_preact, wup_all, ((1,), (1,))).astype(BF)
    d_norm_away = swap(d_norm_part, "core")
    g_wup = weight_grad(normed_mid, d_preact)
    if fast:
        y_b = swap(away_y([g_wup], row_y), "y")
    d_normed_mid = d_norm_part.astype(F32) + d_norm_away.astype(F32)
    d_mid_part, d_gain_mid, d_shift_mid = norm_back(
        d_normed_mid, xhat_mid, rstd_mid, gains[1]
    )
    d_resid_mid = d_result + d_mid_part
    d_attn = d_resid_mid.astype(BF)
    wo_rows = lax.dynamic_slice_in_dim(wo_all, core * half, half, 0)
    d_mixed = dot_f32(d_attn, wo_rows, ((1,), (1,))).astype(BF)
    g_wo = weight_grad(mixed, lax.dynamic_slice_in_dim(d_attn, core * half, half, 1))
    d_pairs, sums, g_pairs = [], [], []
    if fast:
        first_c = after(first_c, d_attn)
        blocks_c = (column_half(g_wdn, chip).astype(F32) + first_c.astype(F32)).astype(BF)
        d_mixed = after(d_mixed, blocks_c)
        second_c = swap(take(blocks_c, 1 - row_y, 1), "y")
    for pair in range(pairs):
        if fast and pair == 1:
            second_c = after(second_c, d_pairs[0])
            y_b = after(y_b, d_pairs[0])
            blocks_c = (take(blocks_c, row_y, 1).astype(F32) + second_c.astype(F32)).astype(BF)
            blocks_b = blocks_z([g_wup], y_b, row_y)
            parts_c = trade_z(blocks_c)
            d_mixed = after(d_mixed, blocks_c, blocks_b)
            parts_b = trade_z(after(blocks_b, parts_c))
        if fast and pair == pairs - 1:
            early = [g_wo] + g_pairs
            send_o = away_y(early, row_y)
            y_o = swap(send_o, "y")
            d_mixed = after(d_mixed, send_o, parts_c)
        d_pair, sum_pair = attention_backward(
            qkv, side, fwd[pair][1], mixed_parts[pair], d_mixed, pair
        )
        d_pairs.append(d_pair)
        sums.append(sum_pair[:1])
        g_pairs.append(weight_grad(normed_in, d_pair))
    if fast:
        late = g_pairs[pairs - 1 :]
        y_a = swap(away_y(late, row_y), "y")
        sum_c = summed(after(parts_c, d_pairs[-1]))
        sum_c = ordered(sum_c, swap(sum_c, "x"), chip, 1)
    d_qkv = jnp.concatenate(d_pairs, axis=1)
    d_in_half = dot_f32(d_qkv, wq_all, ((1,), (1,))).astype(BF)
    if fast:
        parts_b = after(parts_b, d_in_half)
        blocks_o = blocks_z(early, after(y_o, d_in_half), row_y)
        parts_o = trade_z(after(blocks_o, parts_b))
    d_in_away = swap(lax.dynamic_slice_in_dim(d_in_half, (1 - core) * mine, mine, 0), "core")
    d_normed_in = own_rows(d_in_half).astype(F32) + d_in_away.astype(F32)
    xhat_own = (own_rows(inputs) - own_rows(centre_in)) * own_rows(rstd_in)
    d_in_part, d_gain_in, d_shift_in = norm_back(
        d_normed_in, xhat_own, own_rows(rstd_in), gains[0]
    )
    g_tok = own_rows(d_resid_mid) + d_in_part
    g_tok_there = leave(g_tok)

    at_half = lambda v: lax.dynamic_update_slice_in_dim(
        jnp.zeros((1, width), F32), v, core * half, 1
    )
    up_sums = after(column_sum(d_preact), d_in_half).reshape(owners, 1, per_owner)
    up_both = lax.dynamic_update_slice_in_dim(
        jnp.zeros((owners, 2, per_owner), F32), up_sums, core, 1
    )
    sums = [after(v, d_in_half) for v in sums]
    by_part = jnp.concatenate(sums, axis=0).reshape(pairs, 3, 2 * HD)
    q_sums, v_sums = by_part[:, 0].reshape(1, half), by_part[:, 2].reshape(1, half)
    small_rows = [
        up_both.reshape(-1, width),
        *(0.5 * after(v, d_in_half) for v in (d_gain_mid, d_shift_mid, column_sum(d_attn), column_sum(d_branch))),
        jnp.full((1, width), sse), at_half(q_sums), at_half(v_sums), d_gain_in, d_shift_in,
    ]
    total = jnp.concatenate(small_rows, axis=0)
    if fast:
        for axis in ("core", "x", "y"):
            total = total + swap(total, axis)
        high = total.astype(BF)
        low = (total - high.astype(F32)).astype(BF)
        extra = jnp.concatenate([v[:, at : at + half] for v in (high, low) for at in (0, half)])
        blocks_a = blocks_z(late, y_a, row_y)
        extra = jnp.broadcast_to(extra[None], (depth,) + extra.shape)
        blocks_a = after(jnp.concatenate([blocks_a, extra], axis=1), parts_o)
        parts_a = trade_z(blocks_a)
        n_rows = total.shape[0]
        extra = jnp.sum(parts_a[:, span:].astype(F32), axis=0).reshape(2, 2, n_rows, half)
        total = jnp.concatenate([extra[0, 0] + extra[1, 0], extra[0, 1] + extra[1, 1]], axis=1)
    else:
        total = lax.psum(total, ALL)
    owner = row_z * 2 + row_y
    n_up = ff // width
    up_mine = take(total[:n_up].reshape(owners, -1), owner, 0)
    vec_mine = lax.dynamic_slice_in_dim(total[n_up:], owner * span, span, 1)
    distill_loss = total[n_up + 4, 0] / (count * width)
    vec = lambda *at: jnp.concatenate([vec_mine[i : i + 1] for i in at], axis=0)

    if fast:
        part_c = (sum_c, swap(sum_c, "core"))
        sum_b = summed(parts_b)
        part_b = reduce_core(sum_b, swap(sum_b, "x"))
        sum_o = summed(parts_o)
        part_o = reduce_core(sum_o, swap(sum_o, "x"))
        sum_a = summed(parts_a[:, :span])
        part_a = reduce_core(sum_a, swap(sum_a, "x"))
        cut = lambda part, at: [v[:, at * half : (at + 1) * half] for v in part]
        part_w = cut(part_o, 0)
        parts_q = [cut(part_o, 1 + at) for at in range(pairs - 1)] + [list(part_a)]
        parts_u, parts_d = part_b, part_c
    else:

        def generic(grad):
            grad = grad.reshape(-1, grad.shape[-1])
            part = lax.psum_scatter(
                grad, ("z", "y"), scatter_dimension=0, tiled=True
            ).astype(BF)
            part = lax.psum(part, "x")
            return part, swap(part, "core")

        part_w, parts_u, parts_d = generic(g_wo), generic(g_wup), generic(g_wdn)
        parts_q = [generic(g) for g in g_pairs]

    sorted_q = [ordered(own[None], got[None], core, 0) for own, got in parts_q]
    g_qkv = jnp.concatenate(
        [
            part[c, :, at * 2 * HD : (at + 1) * 2 * HD]
            for at in range(3) for c in range(2) for part in sorted_q
        ],
        axis=1,
    ).astype(F32)
    g_out = ordered(*part_w, core, 1).astype(F32)
    cols_u = lambda v: v.reshape(span, owners, 1, per_owner)
    g_up = ordered(*map(cols_u, parts_u), core, 2).reshape(span, -1).astype(F32)
    g_down = ordered(*parts_d, core, 0).astype(F32)

    return (
        ungroup(output_own, after(output_there, g_tok)),
        distill_loss,
        ungroup(g_tok, g_tok_there),
        g_qkv,
        g_out,
        g_up,
        g_down,
        vec(7, 0),
        vec(8, 1),
        vec(5, 6, 2, 3),
        up_mine,
    )


def solution(mesh):
    seq, owners = mesh.shape["seq"], mesh.shape["shard"]
    fine = Mesh(mesh.devices.reshape(seq // 2, 2, owners // 2, 2), ALL)
    rows = ("z", "y")
    act = P(rows, ("x", "core"), None)
    mat, vec, col = P(rows, None), P(rows), P(None, rows)
    return jax.shard_map(
        shards,
        mesh=fine,
        in_specs=(act, act, act, vec, mat, mat, mat, mat, col, col, col, vec),
        out_specs=(act, P(), act, mat, mat, mat, mat, col, col, col, vec),
        check_vma=False,
    )
```

```python
import functools

import jax
import jax.numpy as jnp
from jax import lax
from jax.experimental import pallas as pl
from jax.experimental.pallas import tpu as pltpu
from jax.sharding import Mesh
from jax.sharding import PartitionSpec as P

HD = 64
EPSILON = 1e-06
NEG_FILL = -1e30
SCALE2 = HD**-0.5 * 1.4426950408889634
ALL = ("x", "core", "z", "y")
BF = jnp.bfloat16
F32 = jnp.float32
BRIEF = pl.CostEstimate(flops=10**8, bytes_accessed=10**5, transcendentals=0)


def dot_f32(a, b, dims):
    return lax.dot_general(a, b, (dims, ((), ())), preferred_element_type=F32)


def after(value, *done):
    return lax.optimization_barrier((value, *done))[0]


def folded_max(x):
    size = x.shape[0]
    while size > 8:
        size //= 2
        x = jnp.maximum(x[:size], x[size:])
    return jnp.max(x, axis=0, keepdims=True)


def side_rows(first, second):
    n = first.shape[1]

    def split(v):
        a = v.astype(BF).astype(F32)
        b = (v - a).astype(BF).astype(F32)
        return [a, b, (v - a - b).astype(BF).astype(F32)]

    zero = jnp.zeros((HD - 3, n), F32)
    return jnp.concatenate(split(second) + [zero] + split(first) + [zero], axis=0).T.astype(BF)


def by_lane(low, first, second):
    return jnp.where(low, first, second)


def attn_fwd_kernel(q_ref, k_ref, v_ref, side_ref, out_ref, aux_ref):
    rows = q_ref.shape[0]
    lane = lax.broadcasted_iota(jnp.int32, (rows, 2 * HD), 1)
    low = lane < HD
    q, k, side = q_ref[...], k_ref[...], side_ref[...]
    vt = v_ref[...].T
    ones = jnp.ones((16, rows), BF)
    mask_lane = jnp.where((lane == 3) | (lane == HD + 3), jnp.ones_like(q), jnp.zeros_like(q))
    parts, norms = [], []
    for head in range(2):
        sel = (lambda a, b: by_lane(low, a, b)) if head == 0 else (lambda a, b: by_lane(low, b, a))
        scores = dot_f32(sel(k, side), sel(q, mask_lane), ((1,), (1,)))
        top = folded_max(scores)
        expo = jnp.exp2((scores - top) * SCALE2).astype(BF)
        left = jnp.concatenate([vt[head * HD : (head + 1) * HD], ones], axis=0)
        mixed_t = dot_f32(left, expo, ((1,), (0,)))
        total = mixed_t[HD : HD + 1]
        parts.append(mixed_t[:HD] / total)
        norms.append(-(top + jnp.log2(total) * (1.0 / SCALE2)))
    out_ref[...] = jnp.concatenate(parts, axis=0).T.astype(BF)
    aux_ref[...] = side_rows(norms[0], norms[1]) + mask_lane


def attn_bwd_kernel(q_ref, k_ref, v_ref, side_ref, aux_ref, mix_ref, dmix_ref, dqkv_ref, sum_ref):
    rows = q_ref.shape[0]
    factor = HD**-0.5
    low = lax.broadcasted_iota(jnp.int32, (rows, 2 * HD), 1) < HD
    q, k, v, side = q_ref[...], k_ref[...], v_ref[...], side_ref[...]
    d, aux = dmix_ref[...], aux_ref[...]
    kt = k.T
    prod = (d.astype(F32) * mix_ref[...].astype(F32)).T
    deltas = side_rows(
        -jnp.sum(prod[:HD], axis=0, keepdims=True), -jnp.sum(prod[HD:], axis=0, keepdims=True)
    )
    zero = jnp.zeros_like(q)
    parts, dv, dk = [], None, None
    for head in range(2):
        sel = (lambda a, b: by_lane(low, a, b)) if head == 0 else (lambda a, b: by_lane(low, b, a))
        probs = jnp.exp2(dot_f32(sel(k, side), sel(q, aux), ((1,), (1,))) * SCALE2)
        d_scores = (probs * dot_f32(sel(v, side), sel(d, deltas), ((1,), (1,)))).astype(BF)
        dv_one = dot_f32(probs.astype(BF), sel(d, zero), ((1,), (0,)))
        dk_one = dot_f32(d_scores, sel(q, zero), ((1,), (0,)))
        dv = dv_one if head == 0 else dv + dv_one
        dk = dk_one if head == 0 else dk + dk_one
        parts.append(dot_f32(kt[head * HD : (head + 1) * HD], d_scores, ((1,), (0,))))
    dq = (jnp.concatenate(parts, axis=0) * factor).T
    for at, grad in enumerate((dq, dk * factor, dv)):
        grad = grad.astype(BF)
        dqkv_ref[:, at * 2 * HD : (at + 1) * 2 * HD] = grad
        sums = jnp.sum(grad.astype(F32), axis=0, keepdims=True)
        sum_ref[:, at * 2 * HD : (at + 1) * 2 * HD] = jnp.broadcast_to(sums, (8, 2 * HD))


def attention_forward(qkv, side, pair):
    rows = qkv.shape[0]
    col = lambda base: pl.BlockSpec((rows, 2 * HD), lambda i: (0, base))
    piece = jax.ShapeDtypeStruct((rows, 2 * HD), BF)
    return pl.pallas_call(
        attn_fwd_kernel,
        grid=(1,),
        in_specs=[col(3 * pair), col(3 * pair + 1), col(3 * pair + 2), col(0)],
        out_specs=[col(0), col(0)],
        out_shape=[piece, piece],
        cost_estimate=BRIEF,
        name="attn_fwd",
    )(qkv, qkv, qkv, side)


def attention_backward(qkv, side, aux, mixed, d_mixed, pair):
    rows = qkv.shape[0]
    col = lambda base: pl.BlockSpec((rows, 2 * HD), lambda i: (0, base))
    return pl.pallas_call(
        attn_bwd_kernel,
        grid=(1,),
        in_specs=[col(3 * pair), col(3 * pair + 1), col(3 * pair + 2), col(0), col(0), col(0), col(pair)],
        out_specs=[
            pl.BlockSpec((rows, 6 * HD), lambda i: (0, 0)), pl.BlockSpec((8, 6 * HD), lambda i: (0, 0))
        ],
        out_shape=[
            jax.ShapeDtypeStruct((rows, 6 * HD), BF), jax.ShapeDtypeStruct((8, 6 * HD), F32)
        ],
        cost_estimate=BRIEF,
        name="attn_bwd",
    )(qkv, qkv, qkv, side, aux, mixed, d_mixed)


def swap(value, axis):
    return lax.ppermute(value, axis, [(0, 1), (1, 0)])


def trade_z(blocks):
    return lax.all_to_all(blocks, "z", 0, 0, tiled=True)


def cross_swap(value, first_axis):
    sizes = [lax.axis_size(a) for a in ALL]
    pairs = []
    for x in range(sizes[0]):
        for core in range(sizes[1]):
            for z in range(sizes[2]):
                for y in range(sizes[3]):
                    over_y = (core == 0) == (first_axis == "y")
                    tx, ty = (x, 1 - y) if over_y else (1 - x, y)
                    flat = lambda a, b: ((a * sizes[1] + core) * sizes[2] + z) * sizes[3] + b
                    pairs.append((flat(x, y), flat(tx, ty)))
    return lax.ppermute(value, ALL, pairs)


def spread_z(piece):
    return trade_z(jnp.broadcast_to(piece[None], (lax.axis_size("z"),) + piece.shape))


def place_kernel(moves, n_sources, slot_ref, *refs):
    sources, outs, sem = refs[:n_sources], refs[n_sources:-1], refs[-1]
    copies = []
    for source, step, slot_at, start, rows, offset, cols, out in moves:
        copies.append(
            pltpu.make_async_copy(
                sources[source].at[step, pl.ds(start, rows), pl.ds(offset, cols)],
                outs[out].at[step, slot_ref[slot_at]],
                sem.at[len(copies)],
            )
        )
    for copy in copies:
        copy.start()
    for copy in copies:
        copy.wait()


def place(slots, sources, moves, shapes):
    return pl.pallas_call(
        functools.partial(place_kernel, moves, len(sources)),
        grid_spec=pltpu.PrefetchScalarGridSpec(
            num_scalar_prefetch=1,
            grid=(1,),
            in_specs=[pl.BlockSpec(memory_space=pl.ANY)] * len(sources),
            out_specs=[pl.BlockSpec(shape, lambda i, s: (0, 0, 0, 0)) for shape in shapes],
            scratch_shapes=[pltpu.SemaphoreType.DMA((len(moves),))],
        ),
        out_shape=[jax.ShapeDtypeStruct(shape, BF) for shape in shapes],
        name="place",
    )(slots, *sources)


def take(value, index, axis):
    return lax.dynamic_index_in_dim(value, index, axis, keepdims=False)


def join(parts):
    return parts[0] if len(parts) == 1 else jnp.concatenate(parts, axis=-1)


def blocks_z(grads, got, row_y):
    here = join([take(g, row_y, 1) for g in grads])
    return (here.astype(F32) + got.astype(F32)).astype(BF)


def away_y(grads, row_y):
    return join([take(g, 1 - row_y, 1) for g in grads])


def summed(parts):
    return jnp.sum(parts.astype(F32), axis=0).astype(BF)


def pick(grads, slot):
    halves = [g.reshape(g.shape[0], 4, -1, g.shape[-1]) for g in grads]
    return join([take(g, slot, 1) for g in halves])


def slots_of(chip, core, row_y):
    keep = jnp.where(core == 0, chip, 2 * row_y)
    send = jnp.where(core == 0, 1 - chip, 2 * (1 - row_y))
    return keep, send, jnp.where(core == 0, 2, 1), jnp.where(core == 0, row_y, chip)


def first_send(grads, slots):
    return jnp.stack([pick(grads, slots[1] + i * slots[2]) for i in range(2)], axis=1)


def after_first(grads, got, slots, bit):
    return pick(grads, slots[0] + bit * slots[2]).astype(F32) + take(got, bit, 1).astype(F32)


def second_send(grads, got, slots):
    return after_first(grads, got, slots, 1 - slots[3]).astype(BF)


def after_second(grads, got, got_second, slots):
    return (after_first(grads, got, slots, slots[3]) + got_second.astype(F32)).astype(BF)


def reduce_core(own, got):
    both = (own.astype(F32) + got.astype(F32)).astype(BF)
    return both, swap(both, "core")


def ordered(mine, other, bit, axis):
    return jnp.where(
        bit == 0,
        jnp.concatenate([mine, other], axis),
        jnp.concatenate([other, mine], axis),
    )

def weave_kernel(width, core_ref, own_ref, got_ref, out_ref):
    first = core_ref[0] == 0
    own, got = own_ref[...].astype(F32), got_ref[...].astype(F32)
    halves = (jnp.where(first, own, got), jnp.where(first, got, own))
    owners = out_ref.shape[1] // (2 * width)
    for at in range(owners):
        part = [v[:, at * width : (at + 1) * width] for v in halves]
        out_ref[:, 2 * at * width : 2 * (at + 1) * width] = jnp.concatenate(part, axis=1)


def norm_stats(rows_in):
    centre = jnp.mean(rows_in, axis=-1, keepdims=True)
    centred = rows_in - centre
    second = jnp.mean(centred * centred, axis=-1, keepdims=True)
    return centre, lax.rsqrt(second + EPSILON)


def norm_back(grad, xhat, rstd, gain):
    scaled = grad * gain
    mean_a = jnp.mean(scaled, axis=-1, keepdims=True)
    mean_b = jnp.mean(scaled * xhat, axis=-1, keepdims=True)
    return (
        rstd * (scaled - mean_a - xhat * mean_b),
        jnp.sum(grad * xhat, axis=0, keepdims=True),
        jnp.sum(grad, axis=0, keepdims=True),
    )


def shards(
    tokens, teacher, cotangent, lengths, w_qkv, w_out, w_up, w_down,
    norm_gain, norm_bias, proj_bias, up_bias,
):
    groups, local_len, width = tokens.shape
    chip = lax.axis_index("x")
    core = lax.axis_index("core")
    row_y = lax.axis_index("y")
    row_z = lax.axis_index("z")
    depth = lax.axis_size("z")
    owners = depth * 2
    ff = w_down.shape[0] * owners
    span = width // owners
    fast = span % 32 == 0
    half = width // 2
    rows = 2 * groups * local_len
    mine = rows // 2
    pairs = half // (2 * HD)
    per_owner = ff // owners // 2

    def regroup(blocks):
        own = take(blocks, chip, 0)
        got = swap(take(blocks, 1 - chip, 0), "x")
        return jnp.concatenate([own, got], axis=0)

    def chip_rows(part):
        return ordered(part, swap(part, "core"), core, 0)

    def own_rows(value):
        return lax.dynamic_slice_in_dim(value, core * mine, mine, 0)

    def pair_major(v):
        part = take(v.reshape(-1, 3, 2, pairs, 2 * HD), core, 2)
        return part.transpose(0, 2, 1, 3).reshape(-1, 3 * half)

    wq_core = pair_major(w_qkv)
    wup_core = take(w_up.reshape(-1, owners, 2, per_owner), core, 2).reshape(-1, ff // 2)
    wdn_core = take(w_down.reshape(2, per_owner, width), core, 0)

    small = jnp.concatenate(
        [norm_gain.reshape(-1), norm_bias.reshape(-1), proj_bias.reshape(-1), up_bias]
    )
    len_parts = jnp.concatenate([lengths // 32, lengths % 32]).astype(BF)
    if fast:
        x_half = lambda w: take(w.reshape(2, -1, w.shape[1]), chip, 0)
        packed = jnp.zeros((8, 3 * half), BF)
        packed = packed.at[0, : small.size].set(small)
        packed = packed.at[1, : len_parts.size].set(len_parts)
        piece_a = jnp.concatenate([x_half(wq_core), packed], axis=0)
        own_a = spread_z(piece_a)
        tok_part = regroup(tokens)
        piece_b = jnp.concatenate([x_half(w_out), x_half(wup_core)], axis=1)
        rest_a = [cross_swap(own_a, "y"), cross_swap(own_a, "x")]
        rest_a.append(cross_swap(rest_a[0], "x"))
        own_b = spread_z(after(piece_b, own_a))
        tok_all = chip_rows(after(tok_part, own_a))
        rest_b = [cross_swap(after(own_b, rest_a[2]), axis) for axis in "yx"]

        slot_of = lambda y, x: y * 2 + x
        slot_first = jnp.where(core == 0, slot_of(1 - row_y, chip), slot_of(row_y, 1 - chip))
        slot_second = jnp.where(core == 0, slot_of(row_y, 1 - chip), slot_of(1 - row_y, chip))
        slots = jnp.stack(
            [slot_of(row_y, chip), slot_first, slot_second, slot_of(1 - row_y, 1 - chip)]
            + [row_y, 1 - row_y]
        ).astype(jnp.int32)
        rows_a = span // 2
        steps = range(depth)
        wq_all, small_all = place(
            slots, [own_a, *rest_a],
            [(i, s, i, 0, rows_a, 0, 3 * half, 0) for i in range(4) for s in steps]
            + [(i, s, i, rows_a, 8, 0, 3 * half, 1) for i in range(4) for s in steps],
            [(depth, 4, rows_a, 3 * half), (depth, 4, 8, 3 * half)],
        )
        wq_all = wq_all.reshape(width, -1)
        small_all = small_all[:, ::2].reshape(owners, 8, -1)
        lens_all = small_all[:, 1, : len_parts.size]
        small_all = small_all[:, 0, : small.size]
    else:
        tok_all = chip_rows(regroup(tokens))
        full = lambda w: lax.all_gather(w, ("z", "y"), axis=0, tiled=True)
        wq_all, wup_all, wdn_all, wo_all = map(full, (wq_core, wup_core, wdn_core, w_out))
        small_all = lax.all_gather(small, ("z", "y"), axis=0)
        lens_all = lax.all_gather(len_parts, ("z", "y"), axis=0)
    small_all = small_all.astype(F32)

    def vectors(start, count):
        part = small_all[:, start * span : (start + count) * span]
        return part.reshape(owners, count, span).transpose(1, 0, 2).reshape(count, width)

    gains, shifts, biases = vectors(0, 2), vectors(2, 2), vectors(4, 4)
    up_shift = take(small_all[:, 8 * span :].reshape(owners, 2, per_owner), core, 1).reshape(-1)
    qkv_bias = pair_major(
        jnp.concatenate([biases[0], jnp.zeros((width,), F32), biases[1]])[None]
    )
    lens_f = lens_all.astype(F32)
    count = jnp.sum(lens_f[:, :groups] * 32.0 + lens_f[:, groups:])

    length = take(lengths, chip, 0)
    steps_at = jnp.arange(local_len, dtype=jnp.int32)
    row_at = jnp.concatenate(
        [(x_at * 2 + c_at) * local_len + steps_at for c_at in range(2) for x_at in (chip, 1 - chip)]
    )
    live = (row_at < length).astype(F32)[:, None]
    lane = jnp.arange(2 * HD, dtype=jnp.int32)[None, :] % HD
    mask = jnp.where(row_at < length, 0.0, NEG_FILL)[:, None]
    side = jnp.where(lane < 3, 1.0, jnp.where(lane == 3, mask, 0.0)).astype(BF)

    inputs = tok_all.astype(F32)
    centre_in, rstd_in = norm_stats(inputs)
    normed_in = ((inputs - centre_in) * rstd_in * gains[0] + shifts[0]).astype(BF)
    if fast:
        own_c = spread_z(after(wdn_core, normed_in))
    qkv = (dot_f32(normed_in, wq_all, ((1,), (0,))) + qkv_bias).astype(BF)
    fwd = []
    mixed_away = []
    targets = [teacher, cotangent]
    for pair in range(pairs):
        if fast and pair == 1:
            qkv = after(qkv, rest_b[0], rest_b[1], fwd[0][0])
        if fast and pair == 2:
            qkv = after(qkv, own_c, fwd[1][0], rest_b[2])
        fwd.append(attention_forward(qkv, side, pair))
        mixed_away.append(swap(fwd[pair][0], "core"))
        if fast and pair == 0:
            rest_b.append(cross_swap(after(rest_b[0], fwd[0][0]), "x"))
        if fast and pair == 1:
            biases, up_shift = (after(v, fwd[1][0]) for v in (biases, up_shift))
    if fast:
        away_c = swap(own_c, "y")
        targets = [after(v, rest_b[2]) for v in targets]
        moves = []
        for i in range(4):
            for s in steps:
                moves.append((i, s, i, 0, rows_a, width, ff // 2, 1))
                moves.append((i, s, i, 0, rows_a, 0, width, 0))
        wo_all, wup_all = place(
            slots, [own_b, *rest_b], moves,
            [(depth, 4, rows_a, width), (depth, 4, rows_a, ff // 2)],
        )
        wo_all, wup_all = wo_all.reshape(width, -1), wup_all.reshape(width, -1)
    mixed_parts = [part for part, _ in fwd]
    tied = [after(part, wo_all) for part in mixed_parts]
    mixed = ordered(
        jnp.concatenate(tied, axis=1), jnp.concatenate(mixed_away, axis=1), core, 1
    )
    resid_mid = inputs + dot_f32(mixed, wo_all, ((1,), (0,))) + biases[2]
    centre_mid, rstd_mid = norm_stats(resid_mid)
    xhat_mid = (resid_mid - centre_mid) * rstd_mid
    normed_mid = (xhat_mid * gains[1] + shifts[1]).astype(BF)
    preact = dot_f32(normed_mid, wup_all, ((1,), (0,))) + up_shift
    bell = 0.5 * (1.0 + lax.erf(preact * 0.7071067811865476))
    activ = (preact * bell).astype(BF)
    slope = (
        bell + preact * jnp.exp(-0.5 * preact * preact) * 0.3989422804014327
    ).astype(BF)
    if fast:
        (wdn_all,) = place(
            slots, [after(own_c, activ), away_c],
            [(i, s, 4 + i, 0, per_owner, 0, width, 0) for i in range(2) for s in steps],
            [(depth, 2, per_owner, width)],
        )
        wdn_all = wdn_all.reshape(-1, width)
    down = dot_f32(activ, wdn_all, ((1,), (0,))).astype(BF)
    both_at = lambda at: jnp.stack([take(v, at, 0) for v in targets])
    here, there = both_at(chip), after(swap(both_at(1 - chip), "x"), down)
    here = jnp.concatenate([here, there], axis=1)
    here = ordered(here, swap(here, "core"), core, 1)
    tea_all, cot_all = here[0], here[1]
    result = resid_mid + (down.astype(F32) + swap(down, "core").astype(F32)) + biases[3]
    error = result - tea_all.astype(F32)
    sse = 0.5 * jnp.sum(live * error * error)

    d_result = live * (cot_all.astype(F32) + 2.0 / (count * width) * error)
    d_branch = d_result.astype(BF)

    def leave(value):
        return swap(value[local_len:].astype(BF), "x")

    def ungroup(value, there):
        return ordered(value[None, :local_len], there.astype(value.dtype)[None], chip, 0)

    def weight_grad(left, right):
        grad = dot_f32(left, right, ((0,), (0,))).astype(BF if fast else F32)
        return grad.reshape(depth, 2, -1, grad.shape[1])

    column_sum = lambda v: jnp.sum(v.astype(F32), axis=0, keepdims=True)
    output_own = own_rows(result).astype(BF)
    g_wdn = weight_grad(activ, d_branch)
    if fast:
        at = slots_of(chip, core, row_y)
        send_c = first_send([g_wdn], at)
        first_c = cross_swap(send_c, "x")
        d_branch_b = after(d_branch, send_c)
    else:
        d_branch_b = d_branch
    d_activ = dot_f32(d_branch_b, wdn_all, ((1,), (1,)))
    d_preact = (d_activ * slope.astype(F32)).astype(BF)
    d_norm_part = dot_f32(d_preact, wup_all, ((1,), (1,))).astype(BF)
    d_norm_away = swap(d_norm_part, "core")
    g_wup = weight_grad(normed_mid, d_preact)
    if fast:
        first_b = cross_swap(first_send([g_wup], at), "x")
    if fast:
        send_c = second_send([g_wdn], first_c, at)
        second_c = cross_swap(send_c, "y")
        d_norm_away = after(d_norm_away, send_c)
    d_normed_mid = d_norm_part.astype(F32) + d_norm_away.astype(F32)
    d_mid_part, d_gain_mid, d_shift_mid = norm_back(
        d_normed_mid, xhat_mid, rstd_mid, gains[1]
    )
    d_resid_mid = d_result + d_mid_part
    d_attn = d_resid_mid.astype(BF)
    wo_rows = lax.dynamic_slice_in_dim(wo_all, core * half, half, 0)
    d_mixed = dot_f32(d_attn, wo_rows, ((1,), (1,))).astype(BF)
    g_wo = weight_grad(mixed, lax.dynamic_slice_in_dim(d_attn, core * half, half, 1))
    d_pairs, sums, g_pairs = [], [], []
    if fast:
        blocks_c = after_second([g_wdn], first_c, after(second_c, d_attn), at)
        parts_c = trade_z(blocks_c)
        d_mixed = after(d_mixed, blocks_c)
    for pair in range(pairs):
        if fast and pair == 1:
            send_b = second_send([g_wup], after(first_b, d_pairs[0]), at)
            second_b = cross_swap(send_b, "y")
            d_mixed = after(d_mixed, send_b, d_pairs[0])
            output_own = after(output_own, d_pairs[0])
        if fast and pair == pairs - 1:
            early = [g_wo] + g_pairs
            send_o = first_send(early, at)
            first_o = cross_swap(send_o, "x")
            blocks_b = after_second([g_wup], first_b, after(second_b, d_pairs[1]), at)
            parts_b = trade_z(after(blocks_b, parts_c))
            d_mixed = after(d_mixed, send_o, parts_c, blocks_b, d_pairs[1])
        d_pair, sum_pair = attention_backward(
            qkv, side, fwd[pair][1], mixed_parts[pair], d_mixed, pair
        )
        d_pairs.append(d_pair)
        sums.append(sum_pair[:1])
        g_pairs.append(weight_grad(normed_in, d_pair))
    output_there = leave(output_own)
    if fast:
        late = g_pairs[pairs - 1 :]
        y_a = swap(away_y(late, row_y), "y")
        send_o = second_send(early, after(first_o, d_pairs[-1]), at)
        second_o = cross_swap(send_o, "y")
    d_qkv = jnp.concatenate(d_pairs, axis=1)
    if fast:
        d_qkv = after(d_qkv, parts_b, send_o)
    d_in_half = dot_f32(d_qkv, wq_all, ((1,), (1,))).astype(BF)
    if fast:
        blocks_o = after_second(early, first_o, after(second_o, d_in_half), at)
        parts_o = trade_z(after(blocks_o, parts_b))
    d_in_away = swap(lax.dynamic_slice_in_dim(d_in_half, (1 - core) * mine, mine, 0), "core")
    if fast:
        d_in_away = after(d_in_away, blocks_o)
    if fast:
        parts_b, parts_c = after(parts_b, d_in_half), after(parts_c, d_pairs[-1])
    d_normed_in = own_rows(d_in_half).astype(F32) + d_in_away.astype(F32)
    xhat_own = (own_rows(inputs) - own_rows(centre_in)) * own_rows(rstd_in)
    d_in_part, d_gain_in, d_shift_in = norm_back(
        d_normed_in, xhat_own, own_rows(rstd_in), gains[0]
    )
    g_tok = own_rows(d_resid_mid) + d_in_part
    at_half = lambda v: lax.dynamic_update_slice_in_dim(
        jnp.zeros((1, width), F32), v, core * half, 1
    )
    up_sums = after(column_sum(d_preact), d_in_half).reshape(owners, 1, per_owner)
    up_both = lax.dynamic_update_slice_in_dim(
        jnp.zeros((owners, 2, per_owner), F32), up_sums, core, 1
    )
    sums = [after(v, d_in_half) for v in sums]
    by_part = jnp.concatenate(sums, axis=0).reshape(pairs, 3, 2 * HD)
    q_sums, v_sums = by_part[:, 0].reshape(1, half), by_part[:, 2].reshape(1, half)
    small_rows = [
        up_both.reshape(-1, width),
        *(after(v, d_in_half) for v in (d_gain_mid, d_shift_mid, column_sum(d_attn), column_sum(d_branch))),
        jnp.full((1, width), sse), at_half(q_sums), at_half(v_sums), d_gain_in, d_shift_in,
    ]
    total = jnp.concatenate(small_rows, axis=0)
    if fast:
        parts_o = after(parts_o, total)
    if fast:
        for axis in ("core", "x", "y"):
            total = total + swap(after(total, parts_o) if axis == "y" else total, axis)
        parts_o, g_tok = after(parts_o, total), after(g_tok, total)
        high = total.astype(BF)
        low = (total - high.astype(F32)).astype(BF)
        extra = jnp.concatenate([v[:, at : at + half] for v in (high, low) for at in (0, half)])
        blocks_a = blocks_z(late, y_a, row_y)
        extra = jnp.broadcast_to(extra[None], (depth,) + extra.shape)
        blocks_a = after(jnp.concatenate([blocks_a, extra], axis=1), parts_o)
        parts_a = trade_z(blocks_a)
        n_rows = total.shape[0]
        extra = jnp.sum(parts_a[:, span:].astype(F32), axis=0).reshape(2, 2, n_rows, half)
        total = jnp.concatenate([extra[0, 0] + extra[1, 0], extra[0, 1] + extra[1, 1]], axis=1)
    else:
        total = lax.psum(total, ALL)
    g_tok_there = leave(g_tok)
    owner = row_z * 2 + row_y
    n_up = ff // width
    up_mine = take(total[:n_up].reshape(owners, -1), owner, 0)
    vec_mine = lax.dynamic_slice_in_dim(total[n_up:], owner * span, span, 1)
    both_cores = jnp.arange(vec_mine.shape[0])[:, None] < 4
    vec_mine = jnp.where(both_cores, 0.5 * vec_mine, vec_mine)
    distill_loss = total[n_up + 4, 0] / (count * width)
    vec = lambda *at: jnp.concatenate([vec_mine[i : i + 1] for i in at], axis=0)

    if fast:

        def gathered(parts):
            part = summed(parts)
            part = ordered(part, swap(part, "x"), chip, 0)
            return part, swap(part, "core")

        part_c, part_b, part_o = gathered(parts_c), gathered(parts_b), gathered(parts_o)
        sum_a = summed(parts_a[:, :span])
        part_a = reduce_core(sum_a, swap(sum_a, "x"))
        cut = lambda part, at: [v[:, at * half : (at + 1) * half] for v in part]
        part_w = cut(part_o, 0)
        parts_q = [cut(part_o, 1 + at) for at in range(pairs - 1)] + [list(part_a)]
        parts_u, parts_d = part_b, part_c
    else:

        def generic(grad):
            grad = grad.reshape(-1, grad.shape[-1])
            part = lax.psum_scatter(
                grad, ("z", "y"), scatter_dimension=0, tiled=True
            ).astype(BF)
            part = lax.psum(part, "x")
            return part, swap(part, "core")

        part_w, parts_u, parts_d = generic(g_wo), generic(g_wup), generic(g_wdn)
        parts_q = [generic(g) for g in g_pairs]

    sorted_q = [ordered(own[None], got[None], core, 0) for own, got in parts_q]
    g_qkv = jnp.concatenate(
        [
            part[c, :, at * 2 * HD : (at + 1) * 2 * HD]
            for at in range(3) for c in range(2) for part in sorted_q
        ],
        axis=1,
    ).astype(F32)
    g_out = ordered(*part_w, core, 1).astype(F32)
    if fast:
        whole = lambda n: pl.BlockSpec((span, n), lambda i, c: (0, 0))
        g_up = pl.pallas_call(
            functools.partial(weave_kernel, per_owner),
            grid_spec=pltpu.PrefetchScalarGridSpec(
                num_scalar_prefetch=1,
                grid=(1,),
                in_specs=[whole(ff // 2), whole(ff // 2)],
                out_specs=whole(ff),
            ),
            out_shape=jax.ShapeDtypeStruct((span, ff), F32),
            name="weave",
        )(core[None].astype(jnp.int32), *parts_u)
    else:
        cols_u = lambda v: v.reshape(span, owners, 1, per_owner)
        g_up = ordered(*map(cols_u, parts_u), core, 2).reshape(span, -1).astype(F32)
    g_down = ordered(*parts_d, core, 0).astype(F32)

    return (
        ungroup(output_own, after(output_there, g_tok)),
        distill_loss,
        ungroup(g_tok, g_tok_there),
        g_qkv,
        g_out,
        g_up,
        g_down,
        vec(7, 0),
        vec(8, 1),
        vec(5, 6, 2, 3),
        up_mine,
    )


def solution(mesh):
    seq, owners = mesh.shape["seq"], mesh.shape["shard"]
    fine = Mesh(mesh.devices.reshape(seq // 2, 2, owners // 2, 2), ALL)
    rows = ("z", "y")
    act = P(rows, ("x", "core"), None)
    mat, vec, col = P(rows, None), P(rows), P(None, rows)
    return jax.shard_map(
        shards,
        mesh=fine,
        in_specs=(act, act, act, vec, mat, mat, mat, mat, col, col, col, vec),
        out_specs=(act, P(), act, mat, mat, mat, mat, col, col, col, vec),
        check_vma=False,
    )
```

```python
import functools

import jax
import jax.numpy as jnp
from jax import lax
from jax.experimental import pallas as pl
from jax.experimental.pallas import tpu as pltpu
from jax.sharding import Mesh
from jax.sharding import PartitionSpec as P

HD = 64
EPSILON = 1e-06
NEG_FILL = -1e30
SCALE2 = HD**-0.5 * 1.4426950408889634
ALL = ("x", "core", "z", "y")
BF = jnp.bfloat16
F32 = jnp.float32
BRIEF = pl.CostEstimate(flops=10**8, bytes_accessed=10**5, transcendentals=0)


def dot_f32(a, b, dims):
    return lax.dot_general(a, b, (dims, ((), ())), preferred_element_type=F32)


def after(value, *done):
    return lax.optimization_barrier((value, *done))[0]


def folded_max(x):
    size = x.shape[0]
    while size > 8:
        size //= 2
        x = jnp.maximum(x[:size], x[size:])
    return jnp.max(x, axis=0, keepdims=True)


def side_rows(first, second):
    n = first.shape[1]

    def split(v):
        a = v.astype(BF).astype(F32)
        b = (v - a).astype(BF).astype(F32)
        return [a, b, (v - a - b).astype(BF).astype(F32)]

    zero = jnp.zeros((HD - 3, n), F32)
    return jnp.concatenate(split(second) + [zero] + split(first) + [zero], axis=0).T.astype(BF)


def by_lane(low, first, second):
    return jnp.where(low, first, second)


def attn_fwd_kernel(q_ref, k_ref, v_ref, side_ref, out_ref, aux_ref):
    rows = q_ref.shape[0]
    lane = lax.broadcasted_iota(jnp.int32, (rows, 2 * HD), 1)
    low = lane < HD
    q, k, side = q_ref[...], k_ref[...], side_ref[...]
    vt = v_ref[...].T
    ones = jnp.ones((16, rows), BF)
    mask_lane = jnp.where((lane == 3) | (lane == HD + 3), jnp.ones_like(q), jnp.zeros_like(q))
    parts, norms = [], []
    for head in range(2):
        sel = (lambda a, b: by_lane(low, a, b)) if head == 0 else (lambda a, b: by_lane(low, b, a))
        scores = dot_f32(sel(k, side), sel(q, mask_lane), ((1,), (1,)))
        top = folded_max(scores)
        expo = jnp.exp2((scores - top) * SCALE2).astype(BF)
        left = jnp.concatenate([vt[head * HD : (head + 1) * HD], ones], axis=0)
        mixed_t = dot_f32(left, expo, ((1,), (0,)))
        total = mixed_t[HD : HD + 1]
        parts.append(mixed_t[:HD] / total)
        norms.append(-(top + jnp.log2(total) * (1.0 / SCALE2)))
    out_ref[...] = jnp.concatenate(parts, axis=0).T.astype(BF)
    aux_ref[...] = side_rows(norms[0], norms[1]) + mask_lane


def attn_bwd_kernel(q_ref, k_ref, v_ref, side_ref, aux_ref, mix_ref, dmix_ref, dqkv_ref, sum_ref):
    rows = q_ref.shape[0]
    factor = HD**-0.5
    low = lax.broadcasted_iota(jnp.int32, (rows, 2 * HD), 1) < HD
    q, k, v, side = q_ref[...], k_ref[...], v_ref[...], side_ref[...]
    d, aux = dmix_ref[...], aux_ref[...]
    kt = k.T
    prod = (d.astype(F32) * mix_ref[...].astype(F32)).T
    deltas = side_rows(
        -jnp.sum(prod[:HD], axis=0, keepdims=True), -jnp.sum(prod[HD:], axis=0, keepdims=True)
    )
    zero = jnp.zeros_like(q)
    parts, dv, dk = [], None, None
    for head in range(2):
        sel = (lambda a, b: by_lane(low, a, b)) if head == 0 else (lambda a, b: by_lane(low, b, a))
        probs = jnp.exp2(dot_f32(sel(k, side), sel(q, aux), ((1,), (1,))) * SCALE2)
        d_scores = (probs * dot_f32(sel(v, side), sel(d, deltas), ((1,), (1,)))).astype(BF)
        dv_one = dot_f32(probs.astype(BF), sel(d, zero), ((1,), (0,)))
        dk_one = dot_f32(d_scores, sel(q, zero), ((1,), (0,)))
        dv = dv_one if head == 0 else dv + dv_one
        dk = dk_one if head == 0 else dk + dk_one
        parts.append(dot_f32(kt[head * HD : (head + 1) * HD], d_scores, ((1,), (0,))))
    dq = (jnp.concatenate(parts, axis=0) * factor).T
    for at, grad in enumerate((dq, dk * factor, dv)):
        grad = grad.astype(BF)
        dqkv_ref[:, at * 2 * HD : (at + 1) * 2 * HD] = grad
        sums = jnp.sum(grad.astype(F32), axis=0, keepdims=True)
        sum_ref[:, at * 2 * HD : (at + 1) * 2 * HD] = jnp.broadcast_to(sums, (8, 2 * HD))


def attention_forward(qkv, side, pair):
    rows = qkv.shape[0]
    col = lambda base: pl.BlockSpec((rows, 2 * HD), lambda i: (0, base))
    piece = jax.ShapeDtypeStruct((rows, 2 * HD), BF)
    return pl.pallas_call(
        attn_fwd_kernel,
        grid=(1,),
        in_specs=[col(3 * pair), col(3 * pair + 1), col(3 * pair + 2), col(0)],
        out_specs=[col(0), col(0)],
        out_shape=[piece, piece],
        cost_estimate=BRIEF,
        name="attn_fwd",
    )(qkv, qkv, qkv, side)


def attention_backward(qkv, side, aux, mixed, d_mixed, pair):
    rows = qkv.shape[0]
    col = lambda base: pl.BlockSpec((rows, 2 * HD), lambda i: (0, base))
    return pl.pallas_call(
        attn_bwd_kernel,
        grid=(1,),
        in_specs=[col(3 * pair), col(3 * pair + 1), col(3 * pair + 2), col(0), col(0), col(0), col(pair)],
        out_specs=[
            pl.BlockSpec((rows, 6 * HD), lambda i: (0, 0)), pl.BlockSpec((8, 6 * HD), lambda i: (0, 0))
        ],
        out_shape=[
            jax.ShapeDtypeStruct((rows, 6 * HD), BF), jax.ShapeDtypeStruct((8, 6 * HD), F32)
        ],
        cost_estimate=BRIEF,
        name="attn_bwd",
    )(qkv, qkv, qkv, side, aux, mixed, d_mixed)


def swap(value, axis):
    return lax.ppermute(value, axis, [(0, 1), (1, 0)])


def trade_z(blocks):
    return lax.all_to_all(blocks, "z", 0, 0, tiled=True)


def cross_swap(value, first_axis):
    sizes = [lax.axis_size(a) for a in ALL]
    pairs = []
    for x in range(sizes[0]):
        for core in range(sizes[1]):
            for z in range(sizes[2]):
                for y in range(sizes[3]):
                    over_y = (core == 0) == (first_axis == "y")
                    tx, ty = (x, 1 - y) if over_y else (1 - x, y)
                    flat = lambda a, b: ((a * sizes[1] + core) * sizes[2] + z) * sizes[3] + b
                    pairs.append((flat(x, y), flat(tx, ty)))
    return lax.ppermute(value, ALL, pairs)


def spread_z(piece):
    return trade_z(jnp.broadcast_to(piece[None], (lax.axis_size("z"),) + piece.shape))


def place_kernel(moves, n_sources, slot_ref, *refs):
    sources, outs, sem = refs[:n_sources], refs[n_sources:-1], refs[-1]
    copies = []
    for source, step, slot_at, start, rows, offset, cols, out in moves:
        copies.append(
            pltpu.make_async_copy(
                sources[source].at[step, pl.ds(start, rows), pl.ds(offset, cols)],
                outs[out].at[step, slot_ref[slot_at]],
                sem.at[len(copies)],
            )
        )
    for copy in copies:
        copy.start()
    for copy in copies:
        copy.wait()


def place(slots, sources, moves, shapes):
    return pl.pallas_call(
        functools.partial(place_kernel, moves, len(sources)),
        grid_spec=pltpu.PrefetchScalarGridSpec(
            num_scalar_prefetch=1,
            grid=(1,),
            in_specs=[pl.BlockSpec(memory_space=pl.ANY)] * len(sources),
            out_specs=[pl.BlockSpec(shape, lambda i, s: (0, 0, 0, 0)) for shape in shapes],
            scratch_shapes=[pltpu.SemaphoreType.DMA((len(moves),))],
        ),
        out_shape=[jax.ShapeDtypeStruct(shape, BF) for shape in shapes],
        name="place",
    )(slots, *sources)


def take(value, index, axis):
    return lax.dynamic_index_in_dim(value, index, axis, keepdims=False)


def join(parts):
    return parts[0] if len(parts) == 1 else jnp.concatenate(parts, axis=-1)


def blocks_z(grads, got, row_y):
    here = join([take(g, row_y, 1) for g in grads])
    return (here.astype(F32) + got.astype(F32)).astype(BF)


def away_y(grads, row_y):
    return join([take(g, 1 - row_y, 1) for g in grads])


def summed(parts):
    return jnp.sum(parts.astype(F32), axis=0).astype(BF)


def pick(grads, slot):
    halves = [g.reshape(g.shape[0], 4, -1, g.shape[-1]) for g in grads]
    return join([take(g, slot, 1) for g in halves])


def slots_of(chip, core, row_y):
    keep = jnp.where(core == 0, chip, 2 * row_y)
    send = jnp.where(core == 0, 1 - chip, 2 * (1 - row_y))
    return keep, send, jnp.where(core == 0, 2, 1), jnp.where(core == 0, row_y, chip)


def first_send(grads, slots):
    return jnp.stack([pick(grads, slots[1] + i * slots[2]) for i in range(2)], axis=1)


def after_first(grads, got, slots, bit):
    return pick(grads, slots[0] + bit * slots[2]).astype(F32) + take(got, bit, 1).astype(F32)


def second_send(grads, got, slots):
    return after_first(grads, got, slots, 1 - slots[3]).astype(BF)


def after_second(grads, got, got_second, slots):
    return (after_first(grads, got, slots, slots[3]) + got_second.astype(F32)).astype(BF)


def reduce_core(own, got):
    both = (own.astype(F32) + got.astype(F32)).astype(BF)
    return both, swap(both, "core")


def ordered(mine, other, bit, axis):
    return jnp.where(
        bit == 0,
        jnp.concatenate([mine, other], axis),
        jnp.concatenate([other, mine], axis),
    )


def row_sum(v):
    return jnp.sum(v.astype(F32), axis=0, keepdims=True)


def table(rows, entries):
    index = lax.broadcasted_iota(jnp.int32, rows, 0)
    out = jnp.zeros(rows, F32)
    for at, entry in entries:
        out = jnp.where(index == at, entry, out)
    return out


def add_to(ref, value):
    @pl.when(pl.program_id(0) == 0)
    def _():
        ref[...] = value

    @pl.when(pl.program_id(0) > 0)
    def _():
        ref[...] += value


def loss_kernel(
    at_ref, resid_ref, down_ref, away_ref, here_ref, there_ref, par_ref,
    out_ref, grad_ref, branch_ref, sum_ref,
):
    i = pl.program_id(0)
    n = resid_ref.shape[0]
    live = (lax.broadcasted_iota(jnp.int32, (n, 1), 0) + at_ref[i] < at_ref[4]).astype(F32)
    mine = i // 2 == at_ref[5]
    teacher, cotangent = (
        jnp.where(mine, here_ref[k].astype(F32), there_ref[k].astype(F32)) for k in range(2)
    )
    result = resid_ref[...] + (down_ref[...].astype(F32) + away_ref[...].astype(F32)) + par_ref[0:1]
    error = result - teacher
    grad = live * (cotangent + par_ref[1:2] * error)
    branch = grad.astype(BF)
    out_ref[...] = result.astype(BF)
    grad_ref[...] = grad
    branch_ref[...] = branch
    add_to(sum_ref, table(sum_ref.shape, [(0, row_sum(branch)), (1, row_sum(live * error * error))]))


def mid_kernel(
    at_ref, part_ref, away_ref, resid_ref, grad_ref, par_ref, prev_ref, out_ref, attn_ref, sum_ref
):
    xhat, rstd = normed(resid_ref[...])
    grad = part_ref[...].astype(F32) + away_ref[...].astype(F32)
    back, d_gain, d_shift = norm_back(grad, xhat, rstd, par_ref[2:3])
    out = grad_ref[...] + back
    attn = out.astype(BF)
    out_ref[...] = out
    attn_ref[...] = attn
    new = table(sum_ref.shape, [(2, d_gain), (3, d_shift), (4, row_sum(attn))])
    add_to(sum_ref, jnp.where(pl.program_id(0) == 0, new + prev_ref[...], new))


def first_kernel(
    at_ref, part_ref, away_ref, in_ref, grad_ref, par_ref, prev_ref, up_ref, *refs
):
    sums, (own_ref, send_ref, sum_ref) = refs[:-3], refs[-3:]
    core = at_ref[5]
    xhat, rstd = normed(in_ref[...].astype(F32))
    grad = part_ref[...].astype(F32) + away_ref[...].astype(F32)
    back, d_gain, d_shift = norm_back(grad, xhat, rstd, par_ref[3:4])
    out = grad_ref[...] + back

    @pl.when(pl.program_id(0) == 0)
    def _():
        own_ref[...] = out
        spread = []
        for column in (0, 2):
            cols = slice(column * 2 * HD, (column + 1) * 2 * HD)
            half = jnp.concatenate([ref[0:1, cols] for ref in sums], axis=1)
            parts = [jnp.where(core == c, half, jnp.zeros_like(half)) for c in range(2)]
            spread.append(jnp.concatenate(parts, axis=1))
        entries = [(5, d_gain), (6, d_shift), (12, spread[0]), (13, spread[1])]
        for c in range(2):
            for k in range(2):
                up = up_ref[k : k + 1]
                entries.append((8 + 2 * c + k, jnp.where(core == c, up, jnp.zeros_like(up))))
        new = table(sum_ref.shape, entries)
        sum_ref[...] = new
        sum_ref[0:8] += prev_ref[...]

    @pl.when(pl.program_id(0) > 0)
    def _():
        send_ref[...] = out.astype(BF)
        sum_ref[...] += table(sum_ref.shape, [(5, d_gain), (6, d_shift)])


def row_call(kernel, steps, at, operands, outs, name):
    return pl.pallas_call(
        kernel,
        grid_spec=pltpu.PrefetchScalarGridSpec(
            num_scalar_prefetch=1,
            grid=(steps,),
            in_specs=[pl.BlockSpec(block, index) for _, block, index in operands],
            out_specs=[pl.BlockSpec(block, index) for _, _, block, index in outs],
        ),
        out_shape=[jax.ShapeDtypeStruct(shape, kind) for shape, kind, _, _ in outs],
        name=name,
    )(at, *[array for array, _, _ in operands])


def weave_kernel(width, core_ref, own_ref, got_ref, out_ref):
    first = core_ref[0] == 0
    own, got = own_ref[...].astype(F32), got_ref[...].astype(F32)
    halves = (jnp.where(first, own, got), jnp.where(first, got, own))
    owners = out_ref.shape[1] // (2 * width)
    for at in range(owners):
        part = [v[:, at * width : (at + 1) * width] for v in halves]
        out_ref[:, 2 * at * width : 2 * (at + 1) * width] = jnp.concatenate(part, axis=1)


def norm_stats(rows_in):
    centre = jnp.mean(rows_in, axis=-1, keepdims=True)
    centred = rows_in - centre
    second = jnp.mean(centred * centred, axis=-1, keepdims=True)
    return centre, lax.rsqrt(second + EPSILON)


def normed(rows_in):
    centre, rstd = norm_stats(rows_in)
    return (rows_in - centre) * rstd, rstd


def norm_back(grad, xhat, rstd, gain):
    scaled = grad * gain
    mean_a = jnp.mean(scaled, axis=-1, keepdims=True)
    mean_b = jnp.mean(scaled * xhat, axis=-1, keepdims=True)
    return (
        rstd * (scaled - mean_a - xhat * mean_b),
        jnp.sum(grad * xhat, axis=0, keepdims=True),
        jnp.sum(grad, axis=0, keepdims=True),
    )


def shards(
    tokens, teacher, cotangent, lengths, w_qkv, w_out, w_up, w_down,
    norm_gain, norm_bias, proj_bias, up_bias,
):
    groups, local_len, width = tokens.shape
    chip = lax.axis_index("x")
    core = lax.axis_index("core")
    row_y = lax.axis_index("y")
    row_z = lax.axis_index("z")
    depth = lax.axis_size("z")
    owners = depth * 2
    ff = w_down.shape[0] * owners
    span = width // owners
    fast = span % 32 == 0
    half = width // 2
    rows = 2 * groups * local_len
    mine = rows // 2
    pairs = half // (2 * HD)
    per_owner = ff // owners // 2

    def regroup(blocks):
        own = take(blocks, chip, 0)
        got = swap(take(blocks, 1 - chip, 0), "x")
        return jnp.concatenate([own, got], axis=0)

    def chip_rows(part):
        return ordered(part, swap(part, "core"), core, 0)

    def own_rows(value):
        return lax.dynamic_slice_in_dim(value, core * mine, mine, 0)

    def pair_major(v):
        part = take(v.reshape(-1, 3, 2, pairs, 2 * HD), core, 2)
        return part.transpose(0, 2, 1, 3).reshape(-1, 3 * half)

    wq_core = pair_major(w_qkv)
    wup_core = take(w_up.reshape(-1, owners, 2, per_owner), core, 2).reshape(-1, ff // 2)
    wdn_core = take(w_down.reshape(2, per_owner, width), core, 0)

    small = jnp.concatenate(
        [norm_gain.reshape(-1), norm_bias.reshape(-1), proj_bias.reshape(-1), up_bias]
    )
    len_parts = jnp.concatenate([lengths // 32, lengths % 32]).astype(BF)
    if fast:
        x_half = lambda w: take(w.reshape(2, -1, w.shape[1]), chip, 0)
        packed = jnp.zeros((8, 3 * half), BF)
        packed = packed.at[0, : small.size].set(small)
        packed = packed.at[1, : len_parts.size].set(len_parts)
        piece_a = jnp.concatenate([x_half(wq_core), packed], axis=0)
        own_a = spread_z(piece_a)
        tok_part = regroup(tokens)
        piece_b = jnp.concatenate([x_half(w_out), x_half(wup_core)], axis=1)
        rest_a = [cross_swap(own_a, "y"), cross_swap(own_a, "x")]
        rest_a.append(cross_swap(rest_a[0], "x"))
        own_b = spread_z(after(piece_b, own_a))
        tok_all = chip_rows(after(tok_part, own_a))
        rest_b = [cross_swap(after(own_b, rest_a[2]), axis) for axis in "yx"]

        slot_of = lambda y, x: y * 2 + x
        slot_first = jnp.where(core == 0, slot_of(1 - row_y, chip), slot_of(row_y, 1 - chip))
        slot_second = jnp.where(core == 0, slot_of(row_y, 1 - chip), slot_of(1 - row_y, chip))
        slots = jnp.stack(
            [slot_of(row_y, chip), slot_first, slot_second, slot_of(1 - row_y, 1 - chip)]
            + [row_y, 1 - row_y]
        ).astype(jnp.int32)
        rows_a = span // 2
        steps = range(depth)
        wq_all, small_all = place(
            slots, [own_a, *rest_a],
            [(i, s, i, 0, rows_a, 0, 3 * half, 0) for i in range(4) for s in steps]
            + [(i, s, i, rows_a, 8, 0, 3 * half, 1) for i in range(4) for s in steps],
            [(depth, 4, rows_a, 3 * half), (depth, 4, 8, 3 * half)],
        )
        wq_all = wq_all.reshape(width, -1)
        small_all = small_all[:, ::2].reshape(owners, 8, -1)
        lens_all = small_all[:, 1, : len_parts.size]
        small_all = small_all[:, 0, : small.size]
    else:
        tok_all = chip_rows(regroup(tokens))
        full = lambda w: lax.all_gather(w, ("z", "y"), axis=0, tiled=True)
        wq_all, wup_all, wdn_all, wo_all = map(full, (wq_core, wup_core, wdn_core, w_out))
        small_all = lax.all_gather(small, ("z", "y"), axis=0)
        lens_all = lax.all_gather(len_parts, ("z", "y"), axis=0)
    small_all = small_all.astype(F32)

    def vectors(start, count):
        part = small_all[:, start * span : (start + count) * span]
        return part.reshape(owners, count, span).transpose(1, 0, 2).reshape(count, width)

    gains, shifts, biases = vectors(0, 2), vectors(2, 2), vectors(4, 4)
    up_shift = take(small_all[:, 8 * span :].reshape(owners, 2, per_owner), core, 1).reshape(-1)
    qkv_bias = pair_major(
        jnp.concatenate([biases[0], jnp.zeros((width,), F32), biases[1]])[None]
    )
    lens_f = lens_all.astype(F32)
    count = jnp.sum(lens_f[:, :groups] * 32.0 + lens_f[:, groups:])

    length = take(lengths, chip, 0)
    steps_at = jnp.arange(local_len, dtype=jnp.int32)
    row_at = jnp.concatenate(
        [(x_at * 2 + c_at) * local_len + steps_at for c_at in range(2) for x_at in (chip, 1 - chip)]
    )
    live = (row_at < length).astype(F32)[:, None]
    lane = jnp.arange(2 * HD, dtype=jnp.int32)[None, :] % HD
    mask = jnp.where(row_at < length, 0.0, NEG_FILL)[:, None]
    side = jnp.where(lane < 3, 1.0, jnp.where(lane == 3, mask, 0.0)).astype(BF)

    inputs = tok_all.astype(F32)
    centre_in, rstd_in = norm_stats(inputs)
    normed_in = ((inputs - centre_in) * rstd_in * gains[0] + shifts[0]).astype(BF)
    if fast:
        own_c = spread_z(after(wdn_core, normed_in))
    qkv = (dot_f32(normed_in, wq_all, ((1,), (0,))) + qkv_bias).astype(BF)
    fwd = []
    mixed_away = []
    targets = [teacher, cotangent]
    for pair in range(pairs):
        if fast and pair == 1:
            qkv = after(qkv, fwd[0][0])
        if fast and pair == 2:
            qkv = after(qkv, own_c, fwd[1][0], rest_b[0], rest_b[1])
        fwd.append(attention_forward(qkv, side, pair))
        mixed_away.append(swap(fwd[pair][0], "core"))
        if fast and pair == 1:
            rest_b.append(cross_swap(after(rest_b[0], fwd[1][0]), "x"))
        if fast and pair == 1:
            biases, up_shift = (after(v, fwd[1][0]) for v in (biases, up_shift))
    if fast:
        away_c = swap(own_c, "y")
        targets = [after(v, rest_b[2]) for v in targets]
        moves = []
        for i in range(4):
            for s in steps:
                moves.append((i, s, i, 0, rows_a, width, ff // 2, 1))
                moves.append((i, s, i, 0, rows_a, 0, width, 0))
        wo_all, wup_all = place(
            slots, [own_b, *rest_b], moves,
            [(depth, 4, rows_a, width), (depth, 4, rows_a, ff // 2)],
        )
        wo_all, wup_all = wo_all.reshape(width, -1), wup_all.reshape(width, -1)
    mixed_parts = [part for part, _ in fwd]
    tied = [after(part, wo_all) for part in mixed_parts]
    mixed = ordered(
        jnp.concatenate(tied, axis=1), jnp.concatenate(mixed_away, axis=1), core, 1
    )
    resid_mid = inputs + dot_f32(mixed, wo_all, ((1,), (0,))) + biases[2]
    centre_mid, rstd_mid = norm_stats(resid_mid)
    xhat_mid = (resid_mid - centre_mid) * rstd_mid
    normed_mid = (xhat_mid * gains[1] + shifts[1]).astype(BF)
    preact = dot_f32(normed_mid, wup_all, ((1,), (0,))) + up_shift
    bell = 0.5 * (1.0 + lax.erf(preact * 0.7071067811865476))
    activ = (preact * bell).astype(BF)
    slope = (
        bell + preact * jnp.exp(-0.5 * preact * preact) * 0.3989422804014327
    ).astype(BF)
    if fast:
        (wdn_all,) = place(
            slots, [after(own_c, activ), away_c],
            [(i, s, 4 + i, 0, per_owner, 0, width, 0) for i in range(2) for s in steps],
            [(depth, 2, per_owner, width)],
        )
        wdn_all = wdn_all.reshape(-1, width)
    down = dot_f32(activ, wdn_all, ((1,), (0,))).astype(BF)
    both_at = lambda at: jnp.stack([take(v, at, 0) for v in targets])
    here, there = both_at(chip), after(swap(both_at(1 - chip), "x"), down)
    here = jnp.concatenate([here, there], axis=1)
    there = swap(here, "core")
    down_away = swap(down, "core")
    starts = [(x_at * 2 + c_at) * local_len for c_at in range(2) for x_at in (chip, 1 - chip)]
    at = jnp.stack(starts + [length, core, 2 * core]).astype(jnp.int32)
    unit = jnp.full((1, width), 2.0, F32) / (count * width)
    params = jnp.concatenate([biases[3:4], unit, gains[1:2], gains[0:1], jnp.zeros((4, width), F32)])
    blk, wide = (local_len, width), (8, width)
    step = lambda i, at: (i, 0)
    fixed = lambda i, at: (0, 0)
    own = lambda i, at: (at[6] + i, 0)
    pair_at = lambda i, at: (0, i % 2, 0)
    full = (rows, width)
    result, d_result, d_branch, loss_sums = row_call(
        loss_kernel, rows // local_len, at,
        [
            (resid_mid, blk, step), (down, blk, step), (down_away, blk, step),
            (here, (2,) + blk, pair_at), (there, (2,) + blk, pair_at), (params, wide, fixed),
        ],
        [
            (full, BF, blk, step), (full, F32, blk, step), (full, BF, blk, step),
            (wide, F32, wide, fixed),
        ],
        "loss",
    )

    def leave(value):
        return swap(value[local_len:].astype(BF), "x")

    def ungroup(value, there):
        return ordered(value[None, :local_len], there.astype(value.dtype)[None], chip, 0)

    def weight_grad(left, right):
        grad = dot_f32(left, right, ((0,), (0,))).astype(BF if fast else F32)
        return grad.reshape(depth, 2, -1, grad.shape[1])

    column_sum = lambda v: jnp.sum(v.astype(F32), axis=0, keepdims=True)
    output_own = own_rows(result)
    g_wdn = weight_grad(activ, d_branch)
    if fast:
        slot = slots_of(chip, core, row_y)
        send_c = first_send([g_wdn], slot)
        first_c = cross_swap(send_c, "x")
        d_branch_b = after(d_branch, send_c)
    else:
        d_branch_b = d_branch
    d_activ = dot_f32(d_branch_b, wdn_all, ((1,), (1,)))
    d_preact = (d_activ * slope.astype(F32)).astype(BF)
    if fast:
        send_c = second_send([g_wdn], first_c, slot)
        second_c = cross_swap(send_c, "y")
        d_preact = after(d_preact, send_c)
    d_norm_part = dot_f32(d_preact, wup_all, ((1,), (1,))).astype(BF)
    d_norm_away = swap(d_norm_part, "core")
    g_wup = weight_grad(normed_mid, d_preact)
    if fast:
        first_b = cross_swap(first_send([g_wup], slot), "x")
    d_resid_mid, d_attn, mid_sums = row_call(
        mid_kernel, rows // local_len, at,
        [
            (d_norm_part, blk, step), (d_norm_away, blk, step), (resid_mid, blk, step),
            (d_result, blk, step), (params, wide, fixed), (loss_sums, wide, fixed),
        ],
        [(full, F32, blk, step), (full, BF, blk, step), (wide, F32, wide, fixed)],
        "mid",
    )
    wo_rows = lax.dynamic_slice_in_dim(wo_all, core * half, half, 0)
    d_mixed = dot_f32(d_attn, wo_rows, ((1,), (1,))).astype(BF)
    g_wo = weight_grad(mixed, lax.dynamic_slice_in_dim(d_attn, core * half, half, 1))
    d_pairs, sums, g_pairs = [], [], []
    if fast:
        blocks_c = after_second([g_wdn], first_c, after(second_c, d_attn), slot)
        parts_c = trade_z(blocks_c)
        d_mixed = after(d_mixed, blocks_c)
    for pair in range(pairs):
        if fast and pair == 1:
            send_b = second_send([g_wup], after(first_b, d_pairs[0]), slot)
            second_b = cross_swap(send_b, "y")
            d_mixed = after(d_mixed, send_b, d_pairs[0])
            output_own = after(output_own, d_pairs[0])
        if fast and pair == pairs - 1:
            early = [g_wo] + g_pairs
            send_o = first_send(early, slot)
            first_o = cross_swap(send_o, "x")
            blocks_b = after_second([g_wup], first_b, after(second_b, d_pairs[1]), slot)
            parts_b = trade_z(after(blocks_b, parts_c))
            d_mixed = after(d_mixed, send_o, parts_c, blocks_b, d_pairs[1])
        d_pair, sum_pair = attention_backward(
            qkv, side, fwd[pair][1], mixed_parts[pair], d_mixed, pair
        )
        d_pairs.append(d_pair)
        sums.append(sum_pair)
        g_pairs.append(weight_grad(normed_in, d_pair))
    output_there = leave(output_own)
    if fast:
        late = g_pairs[pairs - 1 :]
        y_a = swap(away_y(late, row_y), "y")
    d_qkv = jnp.concatenate(d_pairs, axis=1)
    d_in_half = dot_f32(d_qkv, wq_all, ((1,), (1,))).astype(BF)
    if fast:
        send_o = second_send(early, after(first_o, d_in_half), slot)
        second_o = cross_swap(send_o, "y")
        blocks_o = after_second(early, first_o, second_o, slot)
        parts_o = trade_z(after(blocks_o, parts_b))
    d_in_away = swap(lax.dynamic_slice_in_dim(d_in_half, (1 - core) * mine, mine, 0), "core")
    if fast:
        d_in_away = after(d_in_away, blocks_o)
    if fast:
        parts_b, parts_c = after(parts_b, d_in_half), after(parts_c, d_pairs[-1])
    up_sums = after(column_sum(d_preact), d_in_half).reshape(2, width)
    g_tok, g_send, total = row_call(
        first_kernel, mine // local_len, at,
        [
            (d_in_half, blk, own), (d_in_away, blk, step), (tok_all, blk, own),
            (d_resid_mid, blk, own), (params, wide, fixed), (mid_sums, wide, fixed),
            (up_sums, (2, width), fixed),
        ]
        + [(v, (8, 6 * HD), fixed) for v in sums],
        [(blk, F32, blk, fixed), (blk, BF, blk, fixed), ((16, width), F32, (16, width), fixed)],
        "first",
    )
    if fast:
        parts_o = after(parts_o, total)
    if fast:
        for axis in ("core", "x", "y"):
            total = total + swap(after(total, parts_o) if axis == "y" else total, axis)
        parts_o, g_send = after(parts_o, total), after(g_send, total)
        high = total.astype(BF)
        low = (total - high.astype(F32)).astype(BF)
        extra = jnp.concatenate([v[:, at : at + half] for v in (high, low) for at in (0, half)])
        blocks_a = blocks_z(late, y_a, row_y)
        extra = jnp.broadcast_to(extra[None], (depth,) + extra.shape)
        blocks_a = after(jnp.concatenate([blocks_a, extra], axis=1), parts_o)
        parts_a = trade_z(blocks_a)
        n_rows = total.shape[0]
        extra = jnp.sum(parts_a[:, span:].astype(F32), axis=0).reshape(2, 2, n_rows, half)
        total = jnp.concatenate([extra[0, 0] + extra[1, 0], extra[0, 1] + extra[1, 1]], axis=1)
    else:
        total = lax.psum(total, ALL)
    g_tok_there = swap(g_send, "x")
    owner = row_z * 2 + row_y
    vec_mine = lax.dynamic_slice_in_dim(total, owner * span, span, 1)
    both_cores = jnp.arange(vec_mine.shape[0])[:, None] < 5
    vec_mine = jnp.where(both_cores, 0.5 * vec_mine, vec_mine)
    up_table = total[8:12].reshape(2, owners, per_owner)
    up_mine = take(up_table, owner, 1).reshape(-1)
    distill_loss = 0.5 * jnp.sum(total[1]) / (count * width)
    vec = lambda *at: jnp.concatenate([vec_mine[i : i + 1] for i in at], axis=0)

    if fast:

        def gathered(parts):
            part = summed(parts)
            part = ordered(part, swap(part, "x"), chip, 0)
            return part, swap(part, "core")

        part_c, part_b, part_o = gathered(parts_c), gathered(parts_b), gathered(parts_o)
        sum_a = summed(parts_a[:, :span])
        part_a = reduce_core(sum_a, swap(sum_a, "x"))
        cut = lambda part, at: [v[:, at * half : (at + 1) * half] for v in part]
        part_w = cut(part_o, 0)
        parts_q = [cut(part_o, 1 + at) for at in range(pairs - 1)] + [list(part_a)]
        parts_u, parts_d = part_b, part_c
    else:

        def generic(grad):
            grad = grad.reshape(-1, grad.shape[-1])
            part = lax.psum_scatter(
                grad, ("z", "y"), scatter_dimension=0, tiled=True
            ).astype(BF)
            part = lax.psum(part, "x")
            return part, swap(part, "core")

        part_w, parts_u, parts_d = generic(g_wo), generic(g_wup), generic(g_wdn)
        parts_q = [generic(g) for g in g_pairs]

    sorted_q = [ordered(own[None], got[None], core, 0) for own, got in parts_q]
    g_qkv = jnp.concatenate(
        [
            part[c, :, at * 2 * HD : (at + 1) * 2 * HD]
            for at in range(3) for c in range(2) for part in sorted_q
        ],
        axis=1,
    ).astype(F32)
    g_out = ordered(*part_w, core, 1).astype(F32)
    if fast:
        whole = lambda n: pl.BlockSpec((span, n), lambda i, c: (0, 0))
        g_up = pl.pallas_call(
            functools.partial(weave_kernel, per_owner),
            grid_spec=pltpu.PrefetchScalarGridSpec(
                num_scalar_prefetch=1,
                grid=(1,),
                in_specs=[whole(ff // 2), whole(ff // 2)],
                out_specs=whole(ff),
            ),
            out_shape=jax.ShapeDtypeStruct((span, ff), F32),
            name="weave",
        )(core[None].astype(jnp.int32), *parts_u)
    else:
        cols_u = lambda v: v.reshape(span, owners, 1, per_owner)
        g_up = ordered(*map(cols_u, parts_u), core, 2).reshape(span, -1).astype(F32)
    g_down = ordered(*parts_d, core, 0).astype(F32)

    return (
        ungroup(output_own, after(output_there, g_tok)),
        distill_loss,
        ungroup(g_tok, g_tok_there),
        g_qkv,
        g_out,
        g_up,
        g_down,
        vec(5, 2),
        vec(6, 3),
        vec(12, 13, 4, 0),
        up_mine,
    )


def solution(mesh):
    seq, owners = mesh.shape["seq"], mesh.shape["shard"]
    fine = Mesh(mesh.devices.reshape(seq // 2, 2, owners // 2, 2), ALL)
    rows = ("z", "y")
    act = P(rows, ("x", "core"), None)
    mat, vec, col = P(rows, None), P(rows), P(None, rows)
    return jax.shard_map(
        shards,
        mesh=fine,
        in_specs=(act, act, act, vec, mat, mat, mat, mat, col, col, col, vec),
        out_specs=(act, P(), act, mat, mat, mat, mat, col, col, col, vec),
        check_vma=False,
    )
```

```python
import functools

import jax
import jax.numpy as jnp
from jax import lax
from jax.experimental import pallas as pl
from jax.experimental.pallas import tpu as pltpu
from jax.sharding import Mesh
from jax.sharding import PartitionSpec as P

HD = 64
EPSILON = 1e-06
NEG_FILL = -1e30
SCALE2 = HD**-0.5 * 1.4426950408889634
ALL = ("x", "core", "z", "y")
BF = jnp.bfloat16
F32 = jnp.float32
BRIEF = pl.CostEstimate(flops=10**8, bytes_accessed=10**5, transcendentals=0)


def dot_f32(a, b, dims):
    return lax.dot_general(a, b, (dims, ((), ())), preferred_element_type=F32)


def after(value, *done):
    return lax.optimization_barrier((value, *done))[0]


def folded_max(x):
    size = x.shape[0]
    while size > 8:
        size //= 2
        x = jnp.maximum(x[:size], x[size:])
    return jnp.max(x, axis=0, keepdims=True)


def side_rows(first, second):
    n = first.shape[1]

    def split(v):
        a = v.astype(BF).astype(F32)
        b = (v - a).astype(BF).astype(F32)
        return [a, b, (v - a - b).astype(BF).astype(F32)]

    zero = jnp.zeros((HD - 3, n), F32)
    return jnp.concatenate(split(second) + [zero] + split(first) + [zero], axis=0).T.astype(BF)


def by_lane(low, first, second):
    return jnp.where(low, first, second)


def attn_fwd_kernel(q_ref, k_ref, v_ref, side_ref, out_ref, aux_ref):
    rows = q_ref.shape[0]
    lane = lax.broadcasted_iota(jnp.int32, (rows, 2 * HD), 1)
    low = lane < HD
    q, k, side = q_ref[...], k_ref[...], side_ref[...]
    vt = v_ref[...].T
    ones = jnp.ones((16, rows), BF)
    mask_lane = jnp.where((lane == 3) | (lane == HD + 3), jnp.ones_like(q), jnp.zeros_like(q))
    parts, norms = [], []
    for head in range(2):
        sel = (lambda a, b: by_lane(low, a, b)) if head == 0 else (lambda a, b: by_lane(low, b, a))
        scores = dot_f32(sel(k, side), sel(q, mask_lane), ((1,), (1,)))
        top = folded_max(scores)
        expo = jnp.exp2((scores - top) * SCALE2).astype(BF)
        left = jnp.concatenate([vt[head * HD : (head + 1) * HD], ones], axis=0)
        mixed_t = dot_f32(left, expo, ((1,), (0,)))
        total = mixed_t[HD : HD + 1]
        parts.append(mixed_t[:HD] / total)
        norms.append(-(top + jnp.log2(total) * (1.0 / SCALE2)))
    out_ref[...] = jnp.concatenate(parts, axis=0).T.astype(BF)
    aux_ref[...] = side_rows(norms[0], norms[1]) + mask_lane


def attn_bwd_kernel(q_ref, k_ref, v_ref, side_ref, aux_ref, mix_ref, dmix_ref, dqkv_ref, sum_ref):
    rows = q_ref.shape[0]
    factor = HD**-0.5
    low = lax.broadcasted_iota(jnp.int32, (rows, 2 * HD), 1) < HD
    q, k, v, side = q_ref[...], k_ref[...], v_ref[...], side_ref[...]
    d, aux = dmix_ref[...], aux_ref[...]
    kt = k.T
    prod = (d.astype(F32) * mix_ref[...].astype(F32)).T
    deltas = side_rows(
        -jnp.sum(prod[:HD], axis=0, keepdims=True), -jnp.sum(prod[HD:], axis=0, keepdims=True)
    )
    zero = jnp.zeros_like(q)
    parts, dv, dk = [], None, None
    for head in range(2):
        sel = (lambda a, b: by_lane(low, a, b)) if head == 0 else (lambda a, b: by_lane(low, b, a))
        probs = jnp.exp2(dot_f32(sel(k, side), sel(q, aux), ((1,), (1,))) * SCALE2)
        d_scores = (probs * dot_f32(sel(v, side), sel(d, deltas), ((1,), (1,)))).astype(BF)
        dv_one = dot_f32(probs.astype(BF), sel(d, zero), ((1,), (0,)))
        dk_one = dot_f32(d_scores, sel(q, zero), ((1,), (0,)))
        dv = dv_one if head == 0 else dv + dv_one
        dk = dk_one if head == 0 else dk + dk_one
        parts.append(dot_f32(kt[head * HD : (head + 1) * HD], d_scores, ((1,), (0,))))
    dq = (jnp.concatenate(parts, axis=0) * factor).T
    for at, grad in enumerate((dq, dk * factor, dv)):
        grad = grad.astype(BF)
        dqkv_ref[:, at * 2 * HD : (at + 1) * 2 * HD] = grad
        sums = jnp.sum(grad.astype(F32), axis=0, keepdims=True)
        sum_ref[:, at * 2 * HD : (at + 1) * 2 * HD] = jnp.broadcast_to(sums, (8, 2 * HD))


def attention_forward(qkv, side, pair):
    rows = qkv.shape[0]
    col = lambda base: pl.BlockSpec((rows, 2 * HD), lambda i: (0, base))
    piece = jax.ShapeDtypeStruct((rows, 2 * HD), BF)
    return pl.pallas_call(
        attn_fwd_kernel,
        grid=(1,),
        in_specs=[col(3 * pair), col(3 * pair + 1), col(3 * pair + 2), col(0)],
        out_specs=[col(0), col(0)],
        out_shape=[piece, piece],
        cost_estimate=BRIEF,
        name="attn_fwd",
    )(qkv, qkv, qkv, side)


def attention_backward(qkv, side, aux, mixed, d_mixed, pair):
    rows = qkv.shape[0]
    col = lambda base: pl.BlockSpec((rows, 2 * HD), lambda i: (0, base))
    return pl.pallas_call(
        attn_bwd_kernel,
        grid=(1,),
        in_specs=[col(3 * pair), col(3 * pair + 1), col(3 * pair + 2), col(0), col(0), col(0), col(pair)],
        out_specs=[
            pl.BlockSpec((rows, 6 * HD), lambda i: (0, 0)), pl.BlockSpec((8, 6 * HD), lambda i: (0, 0))
        ],
        out_shape=[
            jax.ShapeDtypeStruct((rows, 6 * HD), BF), jax.ShapeDtypeStruct((8, 6 * HD), F32)
        ],
        cost_estimate=BRIEF,
        name="attn_bwd",
    )(qkv, qkv, qkv, side, aux, mixed, d_mixed)


def swap(value, axis):
    return lax.ppermute(value, axis, [(0, 1), (1, 0)])


def trade_z(blocks):
    return lax.all_to_all(blocks, "z", 0, 0, tiled=True)


def cross_swap(value, first_axis):
    sizes = [lax.axis_size(a) for a in ALL]
    pairs = []
    for x in range(sizes[0]):
        for core in range(sizes[1]):
            for z in range(sizes[2]):
                for y in range(sizes[3]):
                    over_y = (core == 0) == (first_axis == "y")
                    tx, ty = (x, 1 - y) if over_y else (1 - x, y)
                    flat = lambda a, b: ((a * sizes[1] + core) * sizes[2] + z) * sizes[3] + b
                    pairs.append((flat(x, y), flat(tx, ty)))
    return lax.ppermute(value, ALL, pairs)


def spread_z(piece):
    return trade_z(jnp.broadcast_to(piece[None], (lax.axis_size("z"),) + piece.shape))


def place_kernel(moves, n_sources, slot_ref, *refs):
    sources, outs, sem = refs[:n_sources], refs[n_sources:-1], refs[-1]
    copies = []
    for source, step, slot_at, start, rows, offset, cols, out in moves:
        copies.append(
            pltpu.make_async_copy(
                sources[source].at[step, pl.ds(start, rows), pl.ds(offset, cols)],
                outs[out].at[step, slot_ref[slot_at]],
                sem.at[len(copies)],
            )
        )
    for copy in copies:
        copy.start()
    for copy in copies:
        copy.wait()


def place(slots, sources, moves, shapes):
    return pl.pallas_call(
        functools.partial(place_kernel, moves, len(sources)),
        grid_spec=pltpu.PrefetchScalarGridSpec(
            num_scalar_prefetch=1,
            grid=(1,),
            in_specs=[pl.BlockSpec(memory_space=pl.ANY)] * len(sources),
            out_specs=[pl.BlockSpec(shape, lambda i, s: (0, 0, 0, 0)) for shape in shapes],
            scratch_shapes=[pltpu.SemaphoreType.DMA((len(moves),))],
        ),
        out_shape=[jax.ShapeDtypeStruct(shape, BF) for shape in shapes],
        name="place",
    )(slots, *sources)


def take(value, index, axis):
    return lax.dynamic_index_in_dim(value, index, axis, keepdims=False)


def join(parts):
    return parts[0] if len(parts) == 1 else jnp.concatenate(parts, axis=-1)


def blocks_z(grads, got, row_y):
    here = join([take(g, row_y, 1) for g in grads])
    return (here.astype(F32) + got.astype(F32)).astype(BF)


def away_y(grads, row_y):
    return join([take(g, 1 - row_y, 1) for g in grads])


def summed(parts):
    return jnp.sum(parts.astype(F32), axis=0).astype(BF)


def pick(grads, slot):
    halves = [g.reshape(g.shape[0], 4, -1, g.shape[-1]) for g in grads]
    return join([take(g, slot, 1) for g in halves])


def slots_of(chip, core, row_y):
    keep = jnp.where(core == 0, chip, 2 * row_y)
    send = jnp.where(core == 0, 1 - chip, 2 * (1 - row_y))
    return keep, send, jnp.where(core == 0, 2, 1), jnp.where(core == 0, row_y, chip)


def first_send(grads, slots):
    return jnp.stack([pick(grads, slots[1] + i * slots[2]) for i in range(2)], axis=1)


def after_first(grads, got, slots, bit):
    return pick(grads, slots[0] + bit * slots[2]).astype(F32) + take(got, bit, 1).astype(F32)


def second_send(grads, got, slots):
    return after_first(grads, got, slots, 1 - slots[3]).astype(BF)


def after_second(grads, got, got_second, slots):
    return (after_first(grads, got, slots, slots[3]) + got_second.astype(F32)).astype(BF)


def reduce_core(own, got):
    both = (own.astype(F32) + got.astype(F32)).astype(BF)
    return both, swap(both, "core")


def ordered(mine, other, bit, axis):
    return jnp.where(
        bit == 0,
        jnp.concatenate([mine, other], axis),
        jnp.concatenate([other, mine], axis),
    )


def row_sum(v):
    return jnp.sum(v.astype(F32), axis=0, keepdims=True)


def table(rows, entries):
    index = lax.broadcasted_iota(jnp.int32, rows, 0)
    out = jnp.zeros(rows, F32)
    for at, entry in entries:
        out = jnp.where(index == at, entry, out)
    return out


def add_to(ref, value):
    @pl.when(pl.program_id(0) == 0)
    def _():
        ref[...] = value

    @pl.when(pl.program_id(0) > 0)
    def _():
        ref[...] += value


def is_mine(at_ref):
    return pl.program_id(0) // (pl.num_programs(0) // 2) == at_ref[5]


def loss_kernel(
    at_ref, resid_ref, down_ref, away_ref, here_ref, there_ref, par_ref, out_ref, branch_ref, sum_ref
):
    i = pl.program_id(0)
    n = resid_ref.shape[0]
    parts = pl.num_programs(0) // 4
    start = at_ref[i // parts] + i % parts * n
    live = (lax.broadcasted_iota(jnp.int32, (n, 1), 0) + start < at_ref[4]).astype(F32)
    mine = is_mine(at_ref)
    teacher, cotangent = (
        jnp.where(mine, here_ref[k].astype(F32), there_ref[k].astype(F32)) for k in range(2)
    )
    result = resid_ref[...] + (down_ref[...].astype(F32) + away_ref[...].astype(F32)) + par_ref[0:1]
    error = result - teacher
    branch = (live * (cotangent + par_ref[1:2] * error)).astype(BF)

    @pl.when(mine)
    def _():
        out_ref[...] = result.astype(BF)

    branch_ref[...] = branch
    add_to(sum_ref, table(sum_ref.shape, [(0, row_sum(branch)), (1, row_sum(live * error * error))]))


def mid_kernel(
    at_ref, part_ref, away_ref, resid_ref, branch_ref, par_ref, prev_ref, out_ref, attn_ref, sum_ref
):
    xhat, rstd = normed(resid_ref[...])
    grad = part_ref[...].astype(F32) + away_ref[...].astype(F32)
    back, d_gain, d_shift = norm_back(grad, xhat, rstd, par_ref[2:3])
    out = branch_ref[...].astype(F32) + back
    attn = out.astype(BF)

    @pl.when(is_mine(at_ref))
    def _():
        out_ref[...] = out

    attn_ref[...] = attn
    new = table(sum_ref.shape, [(2, d_gain), (3, d_shift), (4, row_sum(attn))])
    add_to(sum_ref, jnp.where(pl.program_id(0) == 0, new + prev_ref[...], new))


def first_kernel(
    at_ref, part_ref, away_ref, in_ref, grad_ref, par_ref, prev_ref, up_ref, *refs
):
    sums, (own_ref, send_ref, sum_ref) = refs[:-3], refs[-3:]
    core = at_ref[5]
    xhat, rstd = normed(in_ref[...].astype(F32))
    grad = part_ref[...].astype(F32) + away_ref[...].astype(F32)
    back, d_gain, d_shift = norm_back(grad, xhat, rstd, par_ref[3:4])
    out = grad_ref[...] + back

    @pl.when(pl.program_id(0) == 0)
    def _():
        own_ref[...] = out
        spread = []
        for column in (0, 2):
            cols = slice(column * 2 * HD, (column + 1) * 2 * HD)
            half = jnp.concatenate([ref[0:1, cols] for ref in sums], axis=1)
            parts = [jnp.where(core == c, half, jnp.zeros_like(half)) for c in range(2)]
            spread.append(jnp.concatenate(parts, axis=1))
        entries = [(5, d_gain), (6, d_shift), (12, spread[0]), (13, spread[1])]
        for c in range(2):
            for k in range(2):
                up = up_ref[k : k + 1]
                entries.append((8 + 2 * c + k, jnp.where(core == c, up, jnp.zeros_like(up))))
        new = table(sum_ref.shape, entries)
        sum_ref[...] = new
        sum_ref[0:8] += prev_ref[...]

    @pl.when(pl.program_id(0) > 0)
    def _():
        send_ref[...] = out.astype(BF)
        sum_ref[...] += table(sum_ref.shape, [(5, d_gain), (6, d_shift)])


def row_call(kernel, steps, at, operands, outs, name):
    return pl.pallas_call(
        kernel,
        grid_spec=pltpu.PrefetchScalarGridSpec(
            num_scalar_prefetch=1,
            grid=(steps,),
            in_specs=[pl.BlockSpec(block, index) for _, block, index in operands],
            out_specs=[pl.BlockSpec(block, index) for _, _, block, index in outs],
        ),
        out_shape=[jax.ShapeDtypeStruct(shape, kind) for shape, kind, _, _ in outs],
        name=name,
    )(at, *[array for array, _, _ in operands])


def weave_kernel(width, core_ref, own_ref, got_ref, out_ref):
    first = core_ref[0] == 0
    own, got = own_ref[...].astype(F32), got_ref[...].astype(F32)
    halves = (jnp.where(first, own, got), jnp.where(first, got, own))
    owners = out_ref.shape[1] // (2 * width)
    for at in range(owners):
        part = [v[:, at * width : (at + 1) * width] for v in halves]
        out_ref[:, 2 * at * width : 2 * (at + 1) * width] = jnp.concatenate(part, axis=1)


def norm_stats(rows_in):
    centre = jnp.mean(rows_in, axis=-1, keepdims=True)
    centred = rows_in - centre
    second = jnp.mean(centred * centred, axis=-1, keepdims=True)
    return centre, lax.rsqrt(second + EPSILON)


def normed(rows_in):
    centre, rstd = norm_stats(rows_in)
    return (rows_in - centre) * rstd, rstd


def norm_back(grad, xhat, rstd, gain):
    scaled = grad * gain
    mean_a = jnp.mean(scaled, axis=-1, keepdims=True)
    mean_b = jnp.mean(scaled * xhat, axis=-1, keepdims=True)
    return (
        rstd * (scaled - mean_a - xhat * mean_b),
        jnp.sum(grad * xhat, axis=0, keepdims=True),
        jnp.sum(grad, axis=0, keepdims=True),
    )


def shards(
    tokens, teacher, cotangent, lengths, w_qkv, w_out, w_up, w_down,
    norm_gain, norm_bias, proj_bias, up_bias,
):
    groups, local_len, width = tokens.shape
    chip = lax.axis_index("x")
    core = lax.axis_index("core")
    row_y = lax.axis_index("y")
    row_z = lax.axis_index("z")
    depth = lax.axis_size("z")
    owners = depth * 2
    ff = w_down.shape[0] * owners
    span = width // owners
    fast = span % 32 == 0
    half = width // 2
    rows = 2 * groups * local_len
    mine = rows // 2
    pairs = half // (2 * HD)
    per_owner = ff // owners // 2

    def regroup(blocks):
        own = take(blocks, chip, 0)
        got = swap(take(blocks, 1 - chip, 0), "x")
        return jnp.concatenate([own, got], axis=0)

    def chip_rows(part):
        return ordered(part, swap(part, "core"), core, 0)

    def own_rows(value):
        return lax.dynamic_slice_in_dim(value, core * mine, mine, 0)

    def pair_major(v):
        part = take(v.reshape(-1, 3, 2, pairs, 2 * HD), core, 2)
        return part.transpose(0, 2, 1, 3).reshape(-1, 3 * half)

    wq_core = pair_major(w_qkv)
    wup_core = take(w_up.reshape(-1, owners, 2, per_owner), core, 2).reshape(-1, ff // 2)
    wdn_core = take(w_down.reshape(2, per_owner, width), core, 0)

    small = jnp.concatenate(
        [norm_gain.reshape(-1), norm_bias.reshape(-1), proj_bias.reshape(-1), up_bias]
    )
    len_parts = jnp.concatenate([lengths // 32, lengths % 32]).astype(BF)
    if fast:
        x_half = lambda w: take(w.reshape(2, -1, w.shape[1]), chip, 0)
        packed = jnp.zeros((8, 3 * half), BF)
        packed = packed.at[0, : small.size].set(small)
        packed = packed.at[1, : len_parts.size].set(len_parts)
        piece_a = jnp.concatenate([x_half(wq_core), packed], axis=0)
        own_a = spread_z(piece_a)
        tok_part = regroup(tokens)
        piece_b = jnp.concatenate([x_half(w_out), x_half(wup_core)], axis=1)
        rest_a = [cross_swap(own_a, "y"), cross_swap(own_a, "x")]
        rest_a.append(cross_swap(rest_a[0], "x"))
        own_b = spread_z(after(piece_b, own_a))
        tok_all = chip_rows(after(tok_part, own_a))
        rest_b = [cross_swap(after(own_b, rest_a[2]), axis) for axis in "yx"]

        slot_of = lambda y, x: y * 2 + x
        slot_first = jnp.where(core == 0, slot_of(1 - row_y, chip), slot_of(row_y, 1 - chip))
        slot_second = jnp.where(core == 0, slot_of(row_y, 1 - chip), slot_of(1 - row_y, chip))
        slots = jnp.stack(
            [slot_of(row_y, chip), slot_first, slot_second, slot_of(1 - row_y, 1 - chip)]
            + [row_y, 1 - row_y]
        ).astype(jnp.int32)
        rows_a = span // 2
        steps = range(depth)
        wq_all, small_all = place(
            slots, [own_a, *rest_a],
            [(i, s, i, 0, rows_a, 0, 3 * half, 0) for i in range(4) for s in steps]
            + [(i, s, i, rows_a, 8, 0, 3 * half, 1) for i in range(4) for s in steps],
            [(depth, 4, rows_a, 3 * half), (depth, 4, 8, 3 * half)],
        )
        wq_all = wq_all.reshape(width, -1)
        small_all = small_all[:, ::2].reshape(owners, 8, -1)
        lens_all = small_all[:, 1, : len_parts.size]
        small_all = small_all[:, 0, : small.size]
    else:
        tok_all = chip_rows(regroup(tokens))
        full = lambda w: lax.all_gather(w, ("z", "y"), axis=0, tiled=True)
        wq_all, wup_all, wdn_all, wo_all = map(full, (wq_core, wup_core, wdn_core, w_out))
        small_all = lax.all_gather(small, ("z", "y"), axis=0)
        lens_all = lax.all_gather(len_parts, ("z", "y"), axis=0)
    small_all = small_all.astype(F32)

    def vectors(start, count):
        part = small_all[:, start * span : (start + count) * span]
        return part.reshape(owners, count, span).transpose(1, 0, 2).reshape(count, width)

    gains, shifts, biases = vectors(0, 2), vectors(2, 2), vectors(4, 4)
    up_shift = take(small_all[:, 8 * span :].reshape(owners, 2, per_owner), core, 1).reshape(-1)
    qkv_bias = pair_major(
        jnp.concatenate([biases[0], jnp.zeros((width,), F32), biases[1]])[None]
    )
    lens_f = lens_all.astype(F32)
    count = jnp.sum(lens_f[:, :groups] * 32.0 + lens_f[:, groups:])

    length = take(lengths, chip, 0)
    steps_at = jnp.arange(local_len, dtype=jnp.int32)
    row_at = jnp.concatenate(
        [(x_at * 2 + c_at) * local_len + steps_at for c_at in range(2) for x_at in (chip, 1 - chip)]
    )
    live = (row_at < length).astype(F32)[:, None]
    lane = jnp.arange(2 * HD, dtype=jnp.int32)[None, :] % HD
    mask = jnp.where(row_at < length, 0.0, NEG_FILL)[:, None]
    side = jnp.where(lane < 3, 1.0, jnp.where(lane == 3, mask, 0.0)).astype(BF)

    inputs = tok_all.astype(F32)
    centre_in, rstd_in = norm_stats(inputs)
    normed_in = ((inputs - centre_in) * rstd_in * gains[0] + shifts[0]).astype(BF)
    if fast:
        own_c = spread_z(after(wdn_core, normed_in))
    qkv = (dot_f32(normed_in, wq_all, ((1,), (0,))) + qkv_bias).astype(BF)
    fwd = []
    mixed_away = []
    targets = [teacher, cotangent]
    for pair in range(pairs):
        if fast and pair == 1:
            qkv = after(qkv, fwd[0][0])
        if fast and pair == 2:
            qkv = after(qkv, own_c, fwd[1][0], rest_b[0], rest_b[1])
        fwd.append(attention_forward(qkv, side, pair))
        mixed_away.append(swap(fwd[pair][0], "core"))
        if fast and pair == 1:
            rest_b.append(cross_swap(after(rest_b[0], fwd[1][0]), "x"))
        if fast and pair == 1:
            biases, up_shift = (after(v, fwd[1][0]) for v in (biases, up_shift))
    if fast:
        away_c = swap(own_c, "y")
        targets = [after(v, rest_b[2]) for v in targets]
        moves = []
        for i in range(4):
            for s in steps:
                moves.append((i, s, i, 0, rows_a, width, ff // 2, 1))
                moves.append((i, s, i, 0, rows_a, 0, width, 0))
        wo_all, wup_all = place(
            slots, [own_b, *rest_b], moves,
            [(depth, 4, rows_a, width), (depth, 4, rows_a, ff // 2)],
        )
        wo_all, wup_all = wo_all.reshape(width, -1), wup_all.reshape(width, -1)
    mixed_parts = [part for part, _ in fwd]
    tied = [after(part, wo_all) for part in mixed_parts]
    mixed = ordered(
        jnp.concatenate(tied, axis=1), jnp.concatenate(mixed_away, axis=1), core, 1
    )
    resid_mid = inputs + dot_f32(mixed, wo_all, ((1,), (0,))) + biases[2]
    centre_mid, rstd_mid = norm_stats(resid_mid)
    xhat_mid = (resid_mid - centre_mid) * rstd_mid
    normed_mid = (xhat_mid * gains[1] + shifts[1]).astype(BF)
    preact = dot_f32(normed_mid, wup_all, ((1,), (0,))) + up_shift
    bell = 0.5 * (1.0 + lax.erf(preact * 0.7071067811865476))
    activ = (preact * bell).astype(BF)
    slope = (
        bell + preact * jnp.exp(-0.5 * preact * preact) * 0.3989422804014327
    ).astype(BF)
    if fast:
        (wdn_all,) = place(
            slots, [after(own_c, activ), away_c],
            [(i, s, 4 + i, 0, per_owner, 0, width, 0) for i in range(2) for s in steps],
            [(depth, 2, per_owner, width)],
        )
        wdn_all = wdn_all.reshape(-1, width)
    down = dot_f32(activ, wdn_all, ((1,), (0,))).astype(BF)
    both_at = lambda at: jnp.stack([take(v, at, 0) for v in targets])
    here, there = both_at(chip), after(swap(both_at(1 - chip), "x"), down)
    here = jnp.concatenate([here, there], axis=1)
    there = swap(here, "core")
    down_away = swap(down, "core")
    starts = [(x_at * 2 + c_at) * local_len for c_at in range(2) for x_at in (chip, 1 - chip)]
    at = jnp.stack(starts + [length, core, 2 * core]).astype(jnp.int32)
    unit = jnp.full((1, width), 2.0, F32) / (count * width)
    params = jnp.concatenate([biases[3:4], unit, gains[1:2], gains[0:1], jnp.zeros((4, width), F32)])
    blk, wide = (local_len, width), (8, width)
    step = lambda i, at: (i, 0)
    fixed = lambda i, at: (0, 0)
    own = lambda i, at: (at[6] + i, 0)
    full, half_full, part_blk = (rows, width), (mine, width), (local_len, width)
    n_half = mine // part_blk[0]

    def own_at(i, at):
        return jnp.clip(i - at[5] * n_half, 0, n_half - 1)

    other_at = lambda i, at: jnp.clip(i - (1 - at[5]) * n_half, 0, n_half - 1)
    result, d_branch, loss_sums = row_call(
        loss_kernel, 2 * n_half, at,
        [
            (resid_mid, part_blk, step), (down, part_blk, step), (down_away, part_blk, step),
            (here, (2,) + part_blk, lambda i, at: (0, own_at(i, at), 0)),
            (there, (2,) + part_blk, lambda i, at: (0, other_at(i, at), 0)), (params, wide, fixed),
        ],
        [
            (half_full, BF, part_blk, lambda i, at: (own_at(i, at), 0)), (full, BF, part_blk, step),
            (wide, F32, wide, fixed),
        ],
        "loss",
    )

    def leave(value):
        return swap(value[local_len:].astype(BF), "x")

    def ungroup(value, there):
        return ordered(value[None, :local_len], there.astype(value.dtype)[None], chip, 0)

    def weight_grad(left, right):
        grad = dot_f32(left, right, ((0,), (0,))).astype(BF if fast else F32)
        return grad.reshape(depth, 2, -1, grad.shape[1])

    column_sum = lambda v: jnp.sum(v.astype(F32), axis=0, keepdims=True)
    output_own = result
    g_wdn = weight_grad(activ, d_branch)
    if fast:
        slot = slots_of(chip, core, row_y)
        send_c = first_send([g_wdn], slot)
        first_c = cross_swap(send_c, "x")
        d_branch_b = after(d_branch, send_c)
    else:
        d_branch_b = d_branch
    d_activ = dot_f32(d_branch_b, wdn_all, ((1,), (1,)))
    d_preact = (d_activ * slope.astype(F32)).astype(BF)
    if fast:
        send_c = second_send([g_wdn], first_c, slot)
        second_c = cross_swap(send_c, "y")
        d_preact_b = after(d_preact, send_c)
    else:
        d_preact_b = d_preact
    d_norm_part = dot_f32(d_preact_b, wup_all, ((1,), (1,))).astype(BF)
    d_norm_away = swap(d_norm_part, "core")
    g_wup = weight_grad(normed_mid, d_preact)
    if fast:
        first_b = cross_swap(first_send([g_wup], slot), "x")
    d_resid_mid, d_attn, mid_sums = row_call(
        mid_kernel, 2 * n_half, at,
        [
            (d_norm_part, part_blk, step), (d_norm_away, part_blk, step), (resid_mid, part_blk, step),
            (d_branch, part_blk, step), (params, wide, fixed), (loss_sums, wide, fixed),
        ],
        [
            (half_full, F32, part_blk, lambda i, at: (own_at(i, at), 0)), (full, BF, part_blk, step),
            (wide, F32, wide, fixed),
        ],
        "mid",
    )
    wo_rows = lax.dynamic_slice_in_dim(wo_all, core * half, half, 0)
    d_mixed = dot_f32(d_attn, wo_rows, ((1,), (1,))).astype(BF)
    g_wo = weight_grad(mixed, lax.dynamic_slice_in_dim(d_attn, core * half, half, 1))
    d_pairs, sums, g_pairs = [], [], []
    for pair in range(pairs):
        if fast and pair == 1:
            blocks_c = after_second([g_wdn], first_c, after(second_c, d_pairs[0]), slot)
            parts_c = trade_z(blocks_c)
            send_b = second_send([g_wup], after(first_b, d_pairs[0]), slot)
            second_b = cross_swap(send_b, "y")
            d_mixed = after(d_mixed, blocks_c, send_b, d_pairs[0])
            output_own = after(output_own, d_pairs[0])
        if fast and pair == pairs - 1:
            early = [g_wo] + g_pairs
            send_o = first_send(early, slot)
            first_o = cross_swap(send_o, "x")
            blocks_b = after_second([g_wup], first_b, after(second_b, d_pairs[1]), slot)
            parts_b = trade_z(after(blocks_b, parts_c))
            d_mixed = after(d_mixed, send_o, parts_c, blocks_b, d_pairs[1])
        d_pair, sum_pair = attention_backward(
            qkv, side, fwd[pair][1], mixed_parts[pair], d_mixed, pair
        )
        d_pairs.append(d_pair)
        sums.append(sum_pair)
        g_pairs.append(weight_grad(normed_in, d_pair))
    output_there = leave(output_own)
    if fast:
        late = g_pairs[pairs - 1 :]
        y_a = swap(away_y(late, row_y), "y")
    d_qkv = jnp.concatenate(d_pairs, axis=1)
    d_in_half = dot_f32(d_qkv, wq_all, ((1,), (1,))).astype(BF)
    if fast:
        send_o = second_send(early, after(first_o, d_in_half), slot)
        second_o = cross_swap(send_o, "y")
        blocks_o = after_second(early, first_o, second_o, slot)
        parts_o = trade_z(after(blocks_o, parts_b))
    d_in_away = swap(lax.dynamic_slice_in_dim(d_in_half, (1 - core) * mine, mine, 0), "core")
    if fast:
        parts_b, parts_c = after(parts_b, d_in_half), after(parts_c, d_pairs[-1])
    up_sums = after(column_sum(d_preact), d_in_half).reshape(2, width)
    g_tok, g_send, total = row_call(
        first_kernel, mine // local_len, at,
        [
            (d_in_half, blk, own), (d_in_away, blk, step), (tok_all, blk, own),
            (d_resid_mid, blk, step), (params, wide, fixed), (mid_sums, wide, fixed),
            (up_sums, (2, width), fixed),
        ]
        + [(v, (8, 6 * HD), fixed) for v in sums],
        [(blk, F32, blk, fixed), (blk, BF, blk, fixed), ((16, width), F32, (16, width), fixed)],
        "first",
    )
    if fast:
        parts_o = after(parts_o, total)
    if fast:
        for axis in ("core", "x", "y"):
            total = total + swap(after(total, parts_o) if axis == "y" else total, axis)
        parts_o, g_send = after(parts_o, total), after(g_send, total)
        extra = total.astype(BF)
        extra = jnp.concatenate([extra[:, :half], extra[:, half:]])
        blocks_a = blocks_z(late, y_a, row_y)
        extra = jnp.broadcast_to(extra[None], (depth,) + extra.shape)
        blocks_a = after(jnp.concatenate([blocks_a, extra], axis=1), parts_o)
        parts_a = trade_z(blocks_a)
        extra = jnp.sum(parts_a[:, span:].astype(F32), axis=0)
        n_rows = total.shape[0]
        total = jnp.concatenate([extra[:n_rows], extra[n_rows:]], axis=1)
    else:
        total = lax.psum(total, ALL)
    g_tok_there = swap(g_send, "x")
    owner = row_z * 2 + row_y
    vec_mine = lax.dynamic_slice_in_dim(total, owner * span, span, 1)
    both_cores = jnp.arange(vec_mine.shape[0])[:, None] < 5
    vec_mine = jnp.where(both_cores, 0.5 * vec_mine, vec_mine)
    up_table = total[8:12].reshape(2, owners, per_owner)
    up_mine = take(up_table, owner, 1).reshape(-1)
    distill_loss = 0.5 * jnp.sum(total[1]) / (count * width)
    vec = lambda *at: jnp.concatenate([vec_mine[i : i + 1] for i in at], axis=0)

    if fast:

        def gathered(parts):
            part = summed(parts)
            part = ordered(part, swap(part, "x"), chip, 0)
            return part, swap(part, "core")

        part_c, part_b, part_o = gathered(parts_c), gathered(parts_b), gathered(parts_o)
        sum_a = summed(parts_a[:, :span])
        part_a = reduce_core(sum_a, swap(sum_a, "x"))
        cut = lambda part, at: [v[:, at * half : (at + 1) * half] for v in part]
        part_w = cut(part_o, 0)
        parts_q = [cut(part_o, 1 + at) for at in range(pairs - 1)] + [list(part_a)]
        parts_u, parts_d = part_b, part_c
    else:

        def generic(grad):
            grad = grad.reshape(-1, grad.shape[-1])
            part = lax.psum_scatter(
                grad, ("z", "y"), scatter_dimension=0, tiled=True
            ).astype(BF)
            part = lax.psum(part, "x")
            return part, swap(part, "core")

        part_w, parts_u, parts_d = generic(g_wo), generic(g_wup), generic(g_wdn)
        parts_q = [generic(g) for g in g_pairs]

    sorted_q = [ordered(own[None], got[None], core, 0) for own, got in parts_q]
    g_qkv = jnp.concatenate(
        [
            part[c, :, at * 2 * HD : (at + 1) * 2 * HD]
            for at in range(3) for c in range(2) for part in sorted_q
        ],
        axis=1,
    ).astype(F32)
    g_out = ordered(*part_w, core, 1).astype(F32)
    if fast:
        whole = lambda n: pl.BlockSpec((span, n), lambda i, c: (0, 0))
        g_up = pl.pallas_call(
            functools.partial(weave_kernel, per_owner),
            grid_spec=pltpu.PrefetchScalarGridSpec(
                num_scalar_prefetch=1,
                grid=(1,),
                in_specs=[whole(ff // 2), whole(ff // 2)],
                out_specs=whole(ff),
            ),
            out_shape=jax.ShapeDtypeStruct((span, ff), F32),
            name="weave",
        )(core[None].astype(jnp.int32), *parts_u)
    else:
        cols_u = lambda v: v.reshape(span, owners, 1, per_owner)
        g_up = ordered(*map(cols_u, parts_u), core, 2).reshape(span, -1).astype(F32)
    g_down = ordered(*parts_d, core, 0).astype(F32)

    return (
        ungroup(output_own, after(output_there, g_tok)),
        distill_loss,
        ungroup(g_tok, g_tok_there),
        g_qkv,
        g_out,
        g_up,
        g_down,
        vec(5, 2),
        vec(6, 3),
        vec(12, 13, 4, 0),
        up_mine,
    )


def solution(mesh):
    seq, owners = mesh.shape["seq"], mesh.shape["shard"]
    fine = Mesh(mesh.devices.reshape(seq // 2, 2, owners // 2, 2), ALL)
    rows = ("z", "y")
    act = P(rows, ("x", "core"), None)
    mat, vec, col = P(rows, None), P(rows), P(None, rows)
    return jax.shard_map(
        shards,
        mesh=fine,
        in_specs=(act, act, act, vec, mat, mat, mat, mat, col, col, col, vec),
        out_specs=(act, P(), act, mat, mat, mat, mat, col, col, col, vec),
        check_vma=False,
    )
```

```python
import functools

import jax
import jax.numpy as jnp
from jax import lax
from jax.experimental import pallas as pl
from jax.experimental.pallas import tpu as pltpu
from jax.sharding import Mesh
from jax.sharding import PartitionSpec as P

HD = 64
EPSILON = 1e-06
NEG_FILL = -1e30
SCALE2 = HD**-0.5 * 1.4426950408889634
ALL = ("x", "core", "z", "y")
BF = jnp.bfloat16
F32 = jnp.float32
BRIEF = pl.CostEstimate(flops=10**8, bytes_accessed=10**5, transcendentals=0)


def dot_f32(a, b, dims):
    return lax.dot_general(a, b, (dims, ((), ())), preferred_element_type=F32)


def after(value, *done):
    return lax.optimization_barrier((value, *done))[0]


def folded_max(x):
    size = x.shape[0]
    while size > 8:
        size //= 2
        x = jnp.maximum(x[:size], x[size:])
    return jnp.max(x, axis=0, keepdims=True)


def side_rows(first, second):
    n = first.shape[1]

    def split(v):
        a = v.astype(BF).astype(F32)
        b = (v - a).astype(BF).astype(F32)
        return [a, b, (v - a - b).astype(BF).astype(F32)]

    zero = jnp.zeros((HD - 3, n), F32)
    return jnp.concatenate(split(second) + [zero] + split(first) + [zero], axis=0).T.astype(BF)


def by_lane(low, first, second):
    return jnp.where(low, first, second)


def attn_fwd_kernel(q_ref, k_ref, v_ref, side_ref, out_ref, aux_ref):
    rows = q_ref.shape[0]
    lane = lax.broadcasted_iota(jnp.int32, (rows, 2 * HD), 1)
    low = lane < HD
    q, k, side = q_ref[...], k_ref[...], side_ref[...]
    vt = v_ref[...].T
    ones = jnp.ones((16, rows), BF)
    mask_lane = jnp.where((lane == 3) | (lane == HD + 3), jnp.ones_like(q), jnp.zeros_like(q))
    parts, norms = [], []
    for head in range(2):
        sel = (lambda a, b: by_lane(low, a, b)) if head == 0 else (lambda a, b: by_lane(low, b, a))
        scores = dot_f32(sel(k, side), sel(q, mask_lane), ((1,), (1,)))
        top = folded_max(scores)
        expo = jnp.exp2((scores - top) * SCALE2).astype(BF)
        left = jnp.concatenate([vt[head * HD : (head + 1) * HD], ones], axis=0)
        mixed_t = dot_f32(left, expo, ((1,), (0,)))
        total = mixed_t[HD : HD + 1]
        parts.append(mixed_t[:HD] / total)
        norms.append(-(top + jnp.log2(total) * (1.0 / SCALE2)))
    out_ref[...] = jnp.concatenate(parts, axis=0).T.astype(BF)
    aux_ref[...] = side_rows(norms[0], norms[1]) + mask_lane


def attn_bwd_kernel(q_ref, k_ref, v_ref, side_ref, aux_ref, mix_ref, dmix_ref, dqkv_ref, sum_ref):
    rows = q_ref.shape[0]
    factor = HD**-0.5
    low = lax.broadcasted_iota(jnp.int32, (rows, 2 * HD), 1) < HD
    q, k, v, side = q_ref[...], k_ref[...], v_ref[...], side_ref[...]
    d, aux = dmix_ref[...], aux_ref[...]
    kt = k.T
    prod = (d.astype(F32) * mix_ref[...].astype(F32)).T
    deltas = side_rows(
        -jnp.sum(prod[:HD], axis=0, keepdims=True), -jnp.sum(prod[HD:], axis=0, keepdims=True)
    )
    zero = jnp.zeros_like(q)
    parts, dv, dk = [], None, None
    for head in range(2):
        sel = (lambda a, b: by_lane(low, a, b)) if head == 0 else (lambda a, b: by_lane(low, b, a))
        probs = jnp.exp2(dot_f32(sel(k, side), sel(q, aux), ((1,), (1,))) * SCALE2)
        d_scores = (probs * dot_f32(sel(v, side), sel(d, deltas), ((1,), (1,)))).astype(BF)
        dv_one = dot_f32(probs.astype(BF), sel(d, zero), ((1,), (0,)))
        dk_one = dot_f32(d_scores, sel(q, zero), ((1,), (0,)))
        dv = dv_one if head == 0 else dv + dv_one
        dk = dk_one if head == 0 else dk + dk_one
        parts.append(dot_f32(kt[head * HD : (head + 1) * HD], d_scores, ((1,), (0,))))
    dq = (jnp.concatenate(parts, axis=0) * factor).T
    for at, grad in enumerate((dq, dk * factor, dv)):
        grad = grad.astype(BF)
        dqkv_ref[:, at * 2 * HD : (at + 1) * 2 * HD] = grad
        sums = jnp.sum(grad.astype(F32), axis=0, keepdims=True)
        sum_ref[:, at * 2 * HD : (at + 1) * 2 * HD] = jnp.broadcast_to(sums, (8, 2 * HD))


def attention_forward(qkv, side, pair):
    rows = qkv.shape[0]
    col = lambda base: pl.BlockSpec((rows, 2 * HD), lambda i: (0, base))
    piece = jax.ShapeDtypeStruct((rows, 2 * HD), BF)
    return pl.pallas_call(
        attn_fwd_kernel,
        grid=(1,),
        in_specs=[col(3 * pair), col(3 * pair + 1), col(3 * pair + 2), col(0)],
        out_specs=[col(0), col(0)],
        out_shape=[piece, piece],
        cost_estimate=BRIEF,
        name="attn_fwd",
    )(qkv, qkv, qkv, side)


def attention_backward(qkv, side, aux, mixed, d_mixed, pair):
    rows = qkv.shape[0]
    col = lambda base: pl.BlockSpec((rows, 2 * HD), lambda i: (0, base))
    return pl.pallas_call(
        attn_bwd_kernel,
        grid=(1,),
        in_specs=[col(3 * pair), col(3 * pair + 1), col(3 * pair + 2), col(0), col(0), col(0), col(pair)],
        out_specs=[
            pl.BlockSpec((rows, 6 * HD), lambda i: (0, 0)), pl.BlockSpec((8, 6 * HD), lambda i: (0, 0))
        ],
        out_shape=[
            jax.ShapeDtypeStruct((rows, 6 * HD), BF), jax.ShapeDtypeStruct((8, 6 * HD), F32)
        ],
        cost_estimate=BRIEF,
        name="attn_bwd",
    )(qkv, qkv, qkv, side, aux, mixed, d_mixed)


def swap(value, axis):
    return lax.ppermute(value, axis, [(0, 1), (1, 0)])


def trade_z(blocks):
    return lax.all_to_all(blocks, "z", 0, 0, tiled=True)


def cross_swap(value, first_axis):
    sizes = [lax.axis_size(a) for a in ALL]
    pairs = []
    for x in range(sizes[0]):
        for core in range(sizes[1]):
            for z in range(sizes[2]):
                for y in range(sizes[3]):
                    over_y = (core == 0) == (first_axis == "y")
                    tx, ty = (x, 1 - y) if over_y else (1 - x, y)
                    flat = lambda a, b: ((a * sizes[1] + core) * sizes[2] + z) * sizes[3] + b
                    pairs.append((flat(x, y), flat(tx, ty)))
    return lax.ppermute(value, ALL, pairs)


def spread_z(piece):
    return trade_z(jnp.broadcast_to(piece[None], (lax.axis_size("z"),) + piece.shape))


def place_kernel(moves, n_sources, slot_ref, *refs):
    sources, outs, sem = refs[:n_sources], refs[n_sources:-1], refs[-1]
    copies = []
    for source, step, slot_at, start, rows, offset, cols, out in moves:
        copies.append(
            pltpu.make_async_copy(
                sources[source].at[step, pl.ds(start, rows), pl.ds(offset, cols)],
                outs[out].at[step, slot_ref[slot_at]],
                sem.at[len(copies)],
            )
        )
    for copy in copies:
        copy.start()
    for copy in copies:
        copy.wait()


def place(slots, sources, moves, shapes):
    return pl.pallas_call(
        functools.partial(place_kernel, moves, len(sources)),
        grid_spec=pltpu.PrefetchScalarGridSpec(
            num_scalar_prefetch=1,
            grid=(1,),
            in_specs=[pl.BlockSpec(memory_space=pl.ANY)] * len(sources),
            out_specs=[pl.BlockSpec(shape, lambda i, s: (0, 0, 0, 0)) for shape in shapes],
            scratch_shapes=[pltpu.SemaphoreType.DMA((len(moves),))],
        ),
        out_shape=[jax.ShapeDtypeStruct(shape, BF) for shape in shapes],
        name="place",
    )(slots, *sources)


def take(value, index, axis):
    return lax.dynamic_index_in_dim(value, index, axis, keepdims=False)


def join(parts):
    return parts[0] if len(parts) == 1 else jnp.concatenate(parts, axis=-1)


def blocks_z(grads, got, row_y):
    here = join([take(g, row_y, 1) for g in grads])
    return (here.astype(F32) + got.astype(F32)).astype(BF)


def away_y(grads, row_y):
    return join([take(g, 1 - row_y, 1) for g in grads])


def summed(parts):
    return jnp.sum(parts.astype(F32), axis=0).astype(BF)


def pick(grads, slot):
    halves = [g.reshape(g.shape[0], 4, -1, g.shape[-1]) for g in grads]
    return join([take(g, slot, 1) for g in halves])


def slots_of(chip, core, row_y):
    keep = jnp.where(core == 0, chip, 2 * row_y)
    send = jnp.where(core == 0, 1 - chip, 2 * (1 - row_y))
    return keep, send, jnp.where(core == 0, 2, 1), jnp.where(core == 0, row_y, chip)


def first_send(grads, slots):
    return jnp.stack([pick(grads, slots[1] + i * slots[2]) for i in range(2)], axis=1)


def after_first(grads, got, slots, bit):
    return pick(grads, slots[0] + bit * slots[2]).astype(F32) + take(got, bit, 1).astype(F32)


def second_send(grads, got, slots):
    return after_first(grads, got, slots, 1 - slots[3]).astype(BF)


def after_second(grads, got, got_second, slots):
    return (after_first(grads, got, slots, slots[3]) + got_second.astype(F32)).astype(BF)


def reduce_core(own, got):
    both = (own.astype(F32) + got.astype(F32)).astype(BF)
    return both, swap(both, "core")


def ordered(mine, other, bit, axis):
    return jnp.where(
        bit == 0,
        jnp.concatenate([mine, other], axis),
        jnp.concatenate([other, mine], axis),
    )


def row_sum(v):
    return jnp.sum(v.astype(F32), axis=0, keepdims=True)


def table(rows, entries):
    index = lax.broadcasted_iota(jnp.int32, rows, 0)
    out = jnp.zeros(rows, F32)
    for at, entry in entries:
        out = jnp.where(index == at, entry, out)
    return out


def add_to(ref, value):
    @pl.when(pl.program_id(0) == 0)
    def _():
        ref[...] = value

    @pl.when(pl.program_id(0) > 0)
    def _():
        ref[...] += value


def is_mine(at_ref):
    return pl.program_id(0) // (pl.num_programs(0) // 2) == at_ref[5]


def loss_kernel(
    at_ref, resid_ref, down_ref, away_ref, here_ref, there_ref, par_ref, out_ref, branch_ref, sum_ref
):
    i = pl.program_id(0)
    n = resid_ref.shape[0]
    parts = pl.num_programs(0) // 4
    start = at_ref[i // parts] + i % parts * n
    live = (lax.broadcasted_iota(jnp.int32, (n, 1), 0) + start < at_ref[4]).astype(F32)
    mine = is_mine(at_ref)
    teacher, cotangent = (
        jnp.where(mine, here_ref[k].astype(F32), there_ref[k].astype(F32)) for k in range(2)
    )
    result = resid_ref[...] + (down_ref[...].astype(F32) + away_ref[...].astype(F32)) + par_ref[0:1]
    error = result - teacher
    branch = (live * (cotangent + par_ref[1:2] * error)).astype(BF)

    @pl.when(mine)
    def _():
        out_ref[...] = result.astype(BF)

    branch_ref[...] = branch
    add_to(sum_ref, table(sum_ref.shape, [(0, row_sum(branch)), (1, row_sum(live * error * error))]))


def mid_kernel(
    at_ref, part_ref, away_ref, resid_ref, branch_ref, par_ref, prev_ref, out_ref, attn_ref, sum_ref
):
    xhat, rstd = normed(resid_ref[...])
    grad = part_ref[...].astype(F32) + away_ref[...].astype(F32)
    back, d_gain, d_shift = norm_back(grad, xhat, rstd, par_ref[2:3])
    out = branch_ref[...].astype(F32) + back
    attn = out.astype(BF)

    @pl.when(is_mine(at_ref))
    def _():
        out_ref[...] = out

    attn_ref[...] = attn
    new = table(sum_ref.shape, [(2, d_gain), (3, d_shift), (4, row_sum(attn))])
    add_to(sum_ref, jnp.where(pl.program_id(0) == 0, new + prev_ref[...], new))


def first_kernel(
    at_ref, part_ref, away_ref, in_ref, grad_ref, par_ref, prev_ref, up_ref, *refs
):
    sums, (own_ref, send_ref, sum_ref) = refs[:-3], refs[-3:]
    core = at_ref[5]
    xhat, rstd = normed(in_ref[...].astype(F32))
    grad = part_ref[...].astype(F32) + away_ref[...].astype(F32)
    back, d_gain, d_shift = norm_back(grad, xhat, rstd, par_ref[3:4])
    out = grad_ref[...] + back

    @pl.when(pl.program_id(0) == 0)
    def _():
        own_ref[...] = out
        spread = []
        for column in (0, 2):
            cols = slice(column * 2 * HD, (column + 1) * 2 * HD)
            half = jnp.concatenate([ref[0:1, cols] for ref in sums], axis=1)
            parts = [jnp.where(core == c, half, jnp.zeros_like(half)) for c in range(2)]
            spread.append(jnp.concatenate(parts, axis=1))
        entries = [(5, d_gain), (6, d_shift), (12, spread[0]), (13, spread[1])]
        for c in range(2):
            for k in range(2):
                up = up_ref[k : k + 1]
                entries.append((8 + 2 * c + k, jnp.where(core == c, up, jnp.zeros_like(up))))
        new = table(sum_ref.shape, entries)
        sum_ref[...] = new
        sum_ref[0:8] += prev_ref[...]

    @pl.when(pl.program_id(0) > 0)
    def _():
        send_ref[...] = out.astype(BF)
        sum_ref[...] += table(sum_ref.shape, [(5, d_gain), (6, d_shift)])


def row_call(kernel, steps, at, operands, outs, name):
    return pl.pallas_call(
        kernel,
        grid_spec=pltpu.PrefetchScalarGridSpec(
            num_scalar_prefetch=1,
            grid=(steps,),
            in_specs=[pl.BlockSpec(block, index) for _, block, index in operands],
            out_specs=[pl.BlockSpec(block, index) for _, _, block, index in outs],
        ),
        out_shape=[jax.ShapeDtypeStruct(shape, kind) for shape, kind, _, _ in outs],
        name=name,
    )(at, *[array for array, _, _ in operands])


def weave_kernel(width, core_ref, own_ref, got_ref, out_ref):
    first = core_ref[0] == 0
    own, got = own_ref[...].astype(F32), got_ref[...].astype(F32)
    halves = (jnp.where(first, own, got), jnp.where(first, got, own))
    owners = out_ref.shape[1] // (2 * width)
    for at in range(owners):
        part = [v[:, at * width : (at + 1) * width] for v in halves]
        out_ref[:, 2 * at * width : 2 * (at + 1) * width] = jnp.concatenate(part, axis=1)


def norm_stats(rows_in):
    centre = jnp.mean(rows_in, axis=-1, keepdims=True)
    centred = rows_in - centre
    second = jnp.mean(centred * centred, axis=-1, keepdims=True)
    return centre, lax.rsqrt(second + EPSILON)


def normed(rows_in):
    centre, rstd = norm_stats(rows_in)
    return (rows_in - centre) * rstd, rstd


def norm_back(grad, xhat, rstd, gain):
    scaled = grad * gain
    mean_a = jnp.mean(scaled, axis=-1, keepdims=True)
    mean_b = jnp.mean(scaled * xhat, axis=-1, keepdims=True)
    return (
        rstd * (scaled - mean_a - xhat * mean_b),
        jnp.sum(grad * xhat, axis=0, keepdims=True),
        jnp.sum(grad, axis=0, keepdims=True),
    )


def shards(
    tokens, teacher, cotangent, lengths, w_qkv, w_out, w_up, w_down,
    norm_gain, norm_bias, proj_bias, up_bias,
):
    groups, local_len, width = tokens.shape
    chip = lax.axis_index("x")
    core = lax.axis_index("core")
    row_y = lax.axis_index("y")
    row_z = lax.axis_index("z")
    depth = lax.axis_size("z")
    owners = depth * 2
    ff = w_down.shape[0] * owners
    span = width // owners
    fast = span % 32 == 0
    half = width // 2
    rows = 2 * groups * local_len
    mine = rows // 2
    pairs = half // (2 * HD)
    per_owner = ff // owners // 2

    def regroup(blocks):
        own = take(blocks, chip, 0)
        got = swap(take(blocks, 1 - chip, 0), "x")
        return jnp.concatenate([own, got], axis=0)

    def chip_rows(part):
        return ordered(part, swap(part, "core"), core, 0)

    def own_rows(value):
        return lax.dynamic_slice_in_dim(value, core * mine, mine, 0)

    def pair_major(v):
        part = take(v.reshape(-1, 3, 2, pairs, 2 * HD), core, 2)
        return part.transpose(0, 2, 1, 3).reshape(-1, 3 * half)

    wq_core = pair_major(w_qkv)
    wup_core = take(w_up.reshape(-1, owners, 2, per_owner), core, 2).reshape(-1, ff // 2)
    wdn_core = take(w_down.reshape(2, per_owner, width), core, 0)

    small = jnp.concatenate(
        [norm_gain.reshape(-1), norm_bias.reshape(-1), proj_bias.reshape(-1), up_bias]
    )
    len_parts = jnp.concatenate([lengths // 32, lengths % 32]).astype(BF)
    if fast:
        x_half = lambda w: take(w.reshape(2, -1, w.shape[1]), chip, 0)
        packed = jnp.zeros((8, 3 * half), BF)
        packed = packed.at[0, : small.size].set(small)
        packed = packed.at[1, : len_parts.size].set(len_parts)
        piece_a = jnp.concatenate([x_half(wq_core), packed], axis=0)
        own_a = spread_z(piece_a)
        tok_part = regroup(tokens)
        piece_b = jnp.concatenate([x_half(w_out), x_half(wup_core)], axis=1)
        rest_a = [cross_swap(own_a, "y"), cross_swap(own_a, "x")]
        rest_a.append(cross_swap(rest_a[0], "x"))
        own_b = spread_z(after(piece_b, own_a))
        tok_all = chip_rows(after(tok_part, own_a))
        rest_b = [cross_swap(after(own_b, rest_a[2]), axis) for axis in "yx"]

        slot_of = lambda y, x: y * 2 + x
        slot_first = jnp.where(core == 0, slot_of(1 - row_y, chip), slot_of(row_y, 1 - chip))
        slot_second = jnp.where(core == 0, slot_of(row_y, 1 - chip), slot_of(1 - row_y, chip))
        slots = jnp.stack(
            [slot_of(row_y, chip), slot_first, slot_second, slot_of(1 - row_y, 1 - chip)]
            + [row_y, 1 - row_y]
        ).astype(jnp.int32)
        rows_a = span // 2
        steps = range(depth)
        wq_all, small_all = place(
            slots, [own_a, *rest_a],
            [(i, s, i, 0, rows_a, 0, 3 * half, 0) for i in range(4) for s in steps]
            + [(i, s, i, rows_a, 8, 0, 3 * half, 1) for i in range(4) for s in steps],
            [(depth, 4, rows_a, 3 * half), (depth, 4, 8, 3 * half)],
        )
        wq_all = wq_all.reshape(width, -1)
        small_all = small_all[:, ::2].reshape(owners, 8, -1)
        lens_all = small_all[:, 1, : len_parts.size]
        small_all = small_all[:, 0, : small.size]
    else:
        tok_all = chip_rows(regroup(tokens))
        full = lambda w: lax.all_gather(w, ("z", "y"), axis=0, tiled=True)
        wq_all, wup_all, wdn_all, wo_all = map(full, (wq_core, wup_core, wdn_core, w_out))
        small_all = lax.all_gather(small, ("z", "y"), axis=0)
        lens_all = lax.all_gather(len_parts, ("z", "y"), axis=0)
    small_all = small_all.astype(F32)

    def vectors(start, count):
        part = small_all[:, start * span : (start + count) * span]
        return part.reshape(owners, count, span).transpose(1, 0, 2).reshape(count, width)

    gains, shifts, biases = vectors(0, 2), vectors(2, 2), vectors(4, 4)
    up_shift = take(small_all[:, 8 * span :].reshape(owners, 2, per_owner), core, 1).reshape(-1)
    qkv_bias = pair_major(
        jnp.concatenate([biases[0], jnp.zeros((width,), F32), biases[1]])[None]
    )
    lens_f = lens_all.astype(F32)
    count = jnp.sum(lens_f[:, :groups] * 32.0 + lens_f[:, groups:])

    length = take(lengths, chip, 0)
    steps_at = jnp.arange(local_len, dtype=jnp.int32)
    row_at = jnp.concatenate(
        [(x_at * 2 + c_at) * local_len + steps_at for c_at in range(2) for x_at in (chip, 1 - chip)]
    )
    live = (row_at < length).astype(F32)[:, None]
    lane = jnp.arange(2 * HD, dtype=jnp.int32)[None, :] % HD
    mask = jnp.where(row_at < length, 0.0, NEG_FILL)[:, None]
    side = jnp.where(lane < 3, 1.0, jnp.where(lane == 3, mask, 0.0)).astype(BF)

    inputs = tok_all.astype(F32)
    centre_in, rstd_in = norm_stats(inputs)
    normed_in = ((inputs - centre_in) * rstd_in * gains[0] + shifts[0]).astype(BF)
    if fast:
        own_c = spread_z(after(wdn_core, normed_in))
    qkv = (dot_f32(normed_in, wq_all, ((1,), (0,))) + qkv_bias).astype(BF)
    fwd = []
    mixed_away = []
    targets = [teacher, cotangent]
    for pair in range(pairs):
        if fast and pair == 1:
            qkv = after(qkv, fwd[0][0])
        if fast and pair == 2:
            qkv = after(qkv, own_c, fwd[1][0], rest_b[0], rest_b[1])
        fwd.append(attention_forward(qkv, side, pair))
        mixed_away.append(swap(fwd[pair][0], "core"))
        if fast and pair == 1:
            rest_b.append(cross_swap(after(rest_b[0], fwd[1][0]), "x"))
        if fast and pair == 1:
            biases, up_shift = (after(v, fwd[1][0]) for v in (biases, up_shift))
    if fast:
        away_c = swap(own_c, "y")
        targets = [after(v, rest_b[2]) for v in targets]
        moves = []
        for i in range(4):
            for s in steps:
                moves.append((i, s, i, 0, rows_a, width, ff // 2, 1))
                moves.append((i, s, i, 0, rows_a, 0, width, 0))
        wo_all, wup_all = place(
            slots, [own_b, *rest_b], moves,
            [(depth, 4, rows_a, width), (depth, 4, rows_a, ff // 2)],
        )
        wo_all, wup_all = wo_all.reshape(width, -1), wup_all.reshape(width, -1)
    mixed_parts = [part for part, _ in fwd]
    tied = [after(part, wo_all) for part in mixed_parts]
    mixed = ordered(
        jnp.concatenate(tied, axis=1), jnp.concatenate(mixed_away, axis=1), core, 1
    )
    resid_mid = inputs + dot_f32(mixed, wo_all, ((1,), (0,))) + biases[2]
    centre_mid, rstd_mid = norm_stats(resid_mid)
    xhat_mid = (resid_mid - centre_mid) * rstd_mid
    normed_mid = (xhat_mid * gains[1] + shifts[1]).astype(BF)
    preact = dot_f32(normed_mid, wup_all, ((1,), (0,))) + up_shift
    bell = 0.5 * (1.0 + lax.erf(preact * 0.7071067811865476))
    activ = (preact * bell).astype(BF)
    slope = (
        bell + preact * jnp.exp(-0.5 * preact * preact) * 0.3989422804014327
    ).astype(BF)
    if fast:
        (wdn_all,) = place(
            slots, [after(own_c, activ), away_c],
            [(i, s, 4 + i, 0, per_owner, 0, width, 0) for i in range(2) for s in steps],
            [(depth, 2, per_owner, width)],
        )
        wdn_all = wdn_all.reshape(-1, width)
    down = dot_f32(activ, wdn_all, ((1,), (0,))).astype(BF)
    both_at = lambda at: jnp.stack([take(v, at, 0) for v in targets])
    here, there = both_at(chip), after(swap(both_at(1 - chip), "x"), down)
    here = jnp.concatenate([here, there], axis=1)
    there = swap(here, "core")
    down_away = swap(down, "core")
    starts = [(x_at * 2 + c_at) * local_len for c_at in range(2) for x_at in (chip, 1 - chip)]
    at = jnp.stack(starts + [length, core, 2 * core]).astype(jnp.int32)
    unit = jnp.full((1, width), 2.0, F32) / (count * width)
    params = jnp.concatenate([biases[3:4], unit, gains[1:2], gains[0:1], jnp.zeros((4, width), F32)])
    blk, wide = (local_len, width), (8, width)
    step = lambda i, at: (i, 0)
    fixed = lambda i, at: (0, 0)
    own = lambda i, at: (at[6] + i, 0)
    full, half_full, part_blk = (rows, width), (mine, width), (local_len, width)
    n_half = mine // part_blk[0]

    def own_at(i, at):
        return jnp.clip(i - at[5] * n_half, 0, n_half - 1)

    other_at = lambda i, at: jnp.clip(i - (1 - at[5]) * n_half, 0, n_half - 1)
    result, d_branch, loss_sums = row_call(
        loss_kernel, 2 * n_half, at,
        [
            (resid_mid, part_blk, step), (down, part_blk, step), (down_away, part_blk, step),
            (here, (2,) + part_blk, lambda i, at: (0, own_at(i, at), 0)),
            (there, (2,) + part_blk, lambda i, at: (0, other_at(i, at), 0)), (params, wide, fixed),
        ],
        [
            (half_full, BF, part_blk, lambda i, at: (own_at(i, at), 0)), (full, BF, part_blk, step),
            (wide, F32, wide, fixed),
        ],
        "loss",
    )

    def leave(value):
        return swap(value[local_len:].astype(BF), "x")

    def ungroup(value, there):
        return ordered(value[None, :local_len], there.astype(value.dtype)[None], chip, 0)

    def weight_grad(left, right):
        grad = dot_f32(left, right, ((0,), (0,))).astype(BF if fast else F32)
        return grad.reshape(depth, 2, -1, grad.shape[1])

    column_sum = lambda v: jnp.sum(v.astype(F32), axis=0, keepdims=True)
    output_own = result
    g_wdn = weight_grad(activ, d_branch)
    if fast:
        slot = slots_of(chip, core, row_y)
        send_c = first_send([g_wdn], slot)
        first_c = cross_swap(send_c, "x")
        d_branch_b = after(d_branch, send_c)
    else:
        d_branch_b = d_branch
    d_activ = dot_f32(d_branch_b, wdn_all, ((1,), (1,)))
    d_preact = (d_activ * slope.astype(F32)).astype(BF)
    if fast:
        send_c = second_send([g_wdn], first_c, slot)
        second_c = cross_swap(send_c, "y")
        d_preact_b = after(d_preact, send_c)
    else:
        d_preact_b = d_preact
    d_norm_part = dot_f32(d_preact_b, wup_all, ((1,), (1,))).astype(BF)
    d_norm_away = swap(d_norm_part, "core")
    g_wup = weight_grad(normed_mid, d_preact)
    if fast:
        first_b = cross_swap(first_send([g_wup], slot), "x")
    d_resid_mid, d_attn, mid_sums = row_call(
        mid_kernel, 2 * n_half, at,
        [
            (d_norm_part, part_blk, step), (d_norm_away, part_blk, step), (resid_mid, part_blk, step),
            (d_branch, part_blk, step), (params, wide, fixed), (loss_sums, wide, fixed),
        ],
        [
            (half_full, F32, part_blk, lambda i, at: (own_at(i, at), 0)), (full, BF, part_blk, step),
            (wide, F32, wide, fixed),
        ],
        "mid",
    )
    wo_rows = lax.dynamic_slice_in_dim(wo_all, core * half, half, 0)
    d_mixed = dot_f32(d_attn, wo_rows, ((1,), (1,))).astype(BF)
    g_wo = weight_grad(mixed, lax.dynamic_slice_in_dim(d_attn, core * half, half, 1))
    d_pairs, sums, g_pairs = [], [], []
    for pair in range(pairs):
        if fast and pair == 1:
            blocks_c = after_second([g_wdn], first_c, after(second_c, d_pairs[0]), slot)
            parts_c = trade_z(blocks_c)
            send_b = second_send([g_wup], after(first_b, d_pairs[0]), slot)
            second_b = cross_swap(send_b, "y")
            d_mixed = after(d_mixed, blocks_c, send_b, d_pairs[0])
            output_own = after(output_own, d_pairs[0])
        if fast and pair == pairs - 1:
            early = [g_wo] + g_pairs
            send_o = first_send(early, slot)
            first_o = cross_swap(send_o, "x")
            blocks_b = after_second([g_wup], first_b, after(second_b, d_pairs[1]), slot)
            parts_b = trade_z(after(blocks_b, parts_c))
            d_mixed = after(d_mixed, send_o, parts_c, blocks_b, d_pairs[1])
        d_pair, sum_pair = attention_backward(
            qkv, side, fwd[pair][1], mixed_parts[pair], d_mixed, pair
        )
        d_pairs.append(d_pair)
        sums.append(sum_pair)
        g_pairs.append(weight_grad(normed_in, d_pair))
    output_there = leave(output_own)
    if fast:
        late = g_pairs[pairs - 1 :]
        y_a = swap(away_y(late, row_y), "y")
    d_qkv = jnp.concatenate(d_pairs, axis=1)
    d_in_half = dot_f32(d_qkv, wq_all, ((1,), (1,))).astype(BF)
    if fast:
        send_o = second_send(early, after(first_o, d_in_half, parts_b), slot)
        second_o = cross_swap(send_o, "y")
    d_in_away = swap(lax.dynamic_slice_in_dim(d_in_half, (1 - core) * mine, mine, 0), "core")
    if fast:
        parts_b, parts_c = after(parts_b, d_in_half), after(parts_c, d_pairs[-1])
    up_sums = after(column_sum(d_preact), d_in_half).reshape(2, width)
    g_tok, g_send, total = row_call(
        first_kernel, mine // local_len, at,
        [
            (d_in_half, blk, own), (d_in_away, blk, step), (tok_all, blk, own),
            (d_resid_mid, blk, step), (params, wide, fixed), (mid_sums, wide, fixed),
            (up_sums, (2, width), fixed),
        ]
        + [(v, (8, 6 * HD), fixed) for v in sums],
        [(blk, F32, blk, fixed), (blk, BF, blk, fixed), ((16, width), F32, (16, width), fixed)],
        "first",
    )
    if fast:
        blocks_o = after_second(early, first_o, after(second_o, total), slot)
        parts_o = trade_z(after(blocks_o, parts_b))
    if fast:
        for axis in ("core", "x", "y"):
            total = total + swap(after(total, parts_o) if axis == "y" else total, axis)
        parts_o, g_send = after(parts_o, total), after(g_send, total)
        extra = total.astype(BF)
        extra = jnp.concatenate([extra[:, :half], extra[:, half:]])
        blocks_a = blocks_z(late, y_a, row_y)
        extra = jnp.broadcast_to(extra[None], (depth,) + extra.shape)
        blocks_a = after(jnp.concatenate([blocks_a, extra], axis=1), parts_o)
        parts_a = trade_z(blocks_a)
        extra = jnp.sum(parts_a[:, span:].astype(F32), axis=0)
        n_rows = total.shape[0]
        total = jnp.concatenate([extra[:n_rows], extra[n_rows:]], axis=1)
    else:
        total = lax.psum(total, ALL)
    g_tok_there = swap(g_send, "x")
    owner = row_z * 2 + row_y
    vec_mine = lax.dynamic_slice_in_dim(total, owner * span, span, 1)
    both_cores = jnp.arange(vec_mine.shape[0])[:, None] < 5
    vec_mine = jnp.where(both_cores, 0.5 * vec_mine, vec_mine)
    up_table = total[8:12].reshape(2, owners, per_owner)
    up_mine = take(up_table, owner, 1).reshape(-1)
    distill_loss = 0.5 * jnp.sum(total[1]) / (count * width)
    vec = lambda *at: jnp.concatenate([vec_mine[i : i + 1] for i in at], axis=0)

    if fast:

        def gathered(parts):
            part = summed(parts)
            part = ordered(part, swap(part, "x"), chip, 0)
            return part, swap(part, "core")

        part_c, part_b, part_o = gathered(parts_c), gathered(parts_b), gathered(parts_o)
        sum_a = summed(parts_a[:, :span])
        part_a = reduce_core(sum_a, swap(sum_a, "x"))
        cut = lambda part, at: [v[:, at * half : (at + 1) * half] for v in part]
        part_w = cut(part_o, 0)
        parts_q = [cut(part_o, 1 + at) for at in range(pairs - 1)] + [list(part_a)]
        parts_u, parts_d = [after(v, blocks_a) for v in part_b], part_c
    else:

        def generic(grad):
            grad = grad.reshape(-1, grad.shape[-1])
            part = lax.psum_scatter(
                grad, ("z", "y"), scatter_dimension=0, tiled=True
            ).astype(BF)
            part = lax.psum(part, "x")
            return part, swap(part, "core")

        part_w, parts_u, parts_d = generic(g_wo), generic(g_wup), generic(g_wdn)
        parts_q = [generic(g) for g in g_pairs]

    sorted_q = [ordered(own[None], got[None], core, 0) for own, got in parts_q]
    g_qkv = jnp.concatenate(
        [
            part[c, :, at * 2 * HD : (at + 1) * 2 * HD]
            for at in range(3) for c in range(2) for part in sorted_q
        ],
        axis=1,
    ).astype(F32)
    g_out = ordered(*part_w, core, 1).astype(F32)
    if fast:
        whole = lambda n: pl.BlockSpec((span, n), lambda i, c: (0, 0))
        g_up = pl.pallas_call(
            functools.partial(weave_kernel, per_owner),
            grid_spec=pltpu.PrefetchScalarGridSpec(
                num_scalar_prefetch=1,
                grid=(1,),
                in_specs=[whole(ff // 2), whole(ff // 2)],
                out_specs=whole(ff),
            ),
            out_shape=jax.ShapeDtypeStruct((span, ff), F32),
            name="weave",
        )(core[None].astype(jnp.int32), *parts_u)
    else:
        cols_u = lambda v: v.reshape(span, owners, 1, per_owner)
        g_up = ordered(*map(cols_u, parts_u), core, 2).reshape(span, -1).astype(F32)
    g_down = ordered(*parts_d, core, 0).astype(F32)

    return (
        ungroup(output_own, after(output_there, g_tok)),
        distill_loss,
        ungroup(g_tok, g_tok_there),
        g_qkv,
        g_out,
        g_up,
        g_down,
        vec(5, 2),
        vec(6, 3),
        vec(12, 13, 4, 0),
        up_mine,
    )


def solution(mesh):
    seq, owners = mesh.shape["seq"], mesh.shape["shard"]
    fine = Mesh(mesh.devices.reshape(seq // 2, 2, owners // 2, 2), ALL)
    rows = ("z", "y")
    act = P(rows, ("x", "core"), None)
    mat, vec, col = P(rows, None), P(rows), P(None, rows)
    return jax.shard_map(
        shards,
        mesh=fine,
        in_specs=(act, act, act, vec, mat, mat, mat, mat, col, col, col, vec),
        out_specs=(act, P(), act, mat, mat, mat, mat, col, col, col, vec),
        check_vma=False,
    )
```
